512 devices in a mesh: seq: 64 (over y, x, z_hi), tp: 8 (over z_lo, core).
Axes of the slice: x: 4, y: 8, z: 8 (z_hi: 2, z_lo: 4; z = z_hi * 4 + z_lo), core: 2. Of those that a mesh axis runs over, the one named last changes fastest.
Arguments:
- queries: bfloat16 [16384, 4096], P('seq', 'tp'), may hold values from -90 to 90
- key_rows: bfloat16 [16384, 4096], P('seq', 'tp'), may hold values from -4 to 4
- value_rows: bfloat16 [16384, 4096], P('seq', 'tp'), may hold values from -5 to 5
- residual: bfloat16 [16384, 4096], P('seq', 'tp'), may hold values from -1.5 to 1.5
- out_weight: bfloat16 [4096, 4096], P('tp', 'seq'), may hold values from -0.09375 to 0.09375
- norm_gain: float32 [4096], P('tp'), may hold values from 0.5 to 1.5
- norm_bias: float32 [4096], P('tp'), may hold values from -1 to 1
- global_list: int32 [2], replicated, may hold values from 0 to 1023
- random_device: int32 [1024, 3], P('seq'), may hold values from 0 to 63, all different within a row; in each aligned block of 16 rows (0 to 15, 16 to 31, ...) at most 2 rows name the same one
- random_offset: int32 [1024, 3], P('seq'), may hold values from 0 to 15
- drop_seed: int32 [1], replicated, may hold values from 0 to 65535
- drop_offsets: int32 [1024], P('seq'), may hold values from 0 to 8388607
Outputs:
- encoded: bfloat16 [16384, 4096], P('seq', 'tp')
The draws below stay inside these ranges and needn't reach their ends.
Inputs may be any that keep to these rules, and one draw needn't show every extreme that they name: `random_device`: each row names 3 different indices; among the 16 rows of one index of seq no index is named more than 2 times.
All inputs are finite; a program needn't handle non-finite values.
Results may differ from the reference program's by a relative error of at most 0.013.
Values may be sent and summed in bfloat16 or wider, within the bound.
No kernel may reach another device: no remote copies, remote signals or barrier semaphores. Data moves between devices by JAX's collectives and lax.ppermute only.
A program may use at most 64 MiB of HBM per device.

```python
import math
import jax
import jax.numpy as jnp
import numpy as np
from jax import lax

D = 4096
HEADS = 32
DH = 128
BLOCK = 16
GLOB = 2
RAND = 3
BLK_DEV = 16
BLOCKS = 1024
TOKENS = 16384
CAP = 2
N_SEQ = 64
N_TP = 8


def base_keys(key):
    raw = jax.random.normal(jax.random.fold_in(key, 101), (BLOCKS, BLOCK, HEADS * DH), jnp.float32)
    raw = jnp.clip(raw, -4.0, 4.0)
    return raw


def draw_key_rows(key, part):
    return base_keys(key).reshape(TOKENS, HEADS * DH).astype(jnp.bfloat16)


def draw_queries(key, part):
    drawn = jax.random.normal(jax.random.fold_in(key, 404), (BLOCKS, BLOCK, HEADS * DH), jnp.float32)
    drawn = jnp.clip(drawn, -5.0, 5.0)
    return drawn.reshape(TOKENS, HEADS * DH).astype(jnp.bfloat16)


def with_ends(entries, key, smallest, high):
    longest = entries.shape.index(max(entries.shape))
    spots = []
    for shift in (0, 1):
        where = [jax.random.randint(jax.random.fold_in(key, axis), (), 0, length) for axis, length in enumerate(entries.shape)]
        where[longest] = (where[longest] + shift) % entries.shape[longest]
        spots.append(tuple(where))
    return entries.at[spots[0]].set(smallest).at[spots[1]].set(high)


def steps_of(rng, shape, pieces, least, high):
    def one(position, shards_of):
        heights = jax.random.uniform(jax.random.fold_in(jax.random.fold_in(rng, 6), position), (shards_of,), jnp.float32, least / len(pieces), high / len(pieces))
        return jnp.repeat(jnp.exp(heights), shape[position] // shards_of).reshape((-1,) + (1,) * (len(shape) - position - 1))

    gain = one(*pieces[0])
    for cut in pieces[1:]:
        gain = gain * one(*cut)
    return gain


def assign_block(key, own, number, rows, amount, top, reach, lean):
    ranking = jax.random.permutation(key, amount)
    crowded, common = portions_of(amount, rows * top, reach, lean, True), portions_of(amount, rows * top, reach, lean, False)
    places = jnp.arange(amount)

    def named(sizes, rotation):
        used = int((sizes > 0).sum())
        fixed = max(1, used // 4)
        shifted = fixed + (places - fixed + rotation * (used - fixed)) % max(1, amount - fixed)
        return jnp.zeros((amount,), jnp.int32).at[ranking[jnp.where(places < fixed, places, shifted)]].set(jnp.asarray(sizes, jnp.int32))

    sizes = jnp.where(number % 4 == 0, named(crowded, number // 4), named(common, number - number // 4 - 1))
    mixed = jax.random.permutation(jax.random.fold_in(own, 3), amount)
    source_of, sink = mixed[0:amount // 2 * 2:2], mixed[1:amount // 2 * 2:2]
    room = jnp.minimum(sizes[source_of] - 1, reach - sizes[sink]) // 2
    room = jnp.where((source_of == ranking[0]) | (sink == ranking[0]) | (sizes[sink] == 0), 0, jnp.maximum(room, 0))
    shifted = jax.random.randint(jax.random.fold_in(own, 4), (amount // 2,), 0, 1 << 20) % (room + 1)
    sizes = sizes.at[source_of].add(-shifted).at[sink].add(shifted)
    labels = jnp.searchsorted(jnp.cumsum(sizes), jnp.arange(rows * top), side="right").astype(jnp.int32)
    grid = labels.reshape(top, rows).T
    grid = grid[jax.random.permutation(jax.random.fold_in(own, 1), rows)]
    rotation = jax.random.randint(jax.random.fold_in(own, 2), (rows, 1), 0, top)
    return jnp.take_along_axis(grid, (jnp.arange(top)[None, :] + rotation) % top, axis=1)


def portions_of(count, total, reach, skew, full):
    weights = [(1 << 20) // math.isqrt(grade ** skew) + 1 for grade in range(1, count + 1)]
    largest = reach if full else min(reach, max(-(-total // count), total * weights[0] // sum(weights)))
    least = 1 if total - largest >= count - 1 else 0
    counts, rest = [largest] + [least] * (count - 1), total - largest - least * (count - 1)
    while rest > 0:
        candidates = [i for i in range(1, count) if counts[i] < largest] or [i for i in range(1, count) if counts[i] < reach]
        pool, left = sum([weights[i] for i in candidates]), rest
        for i in candidates:
            more = min(reach - counts[i], max(1, left * weights[i] // pool), rest)
            counts[i] = counts[i] + more
            rest = rest - more
    return np.array(counts)


def centred(own_key, dims, deviation, limit, cuts=(), held_as=jnp.bfloat16):
    factor_of = steps_of(own_key, dims, cuts, -0.22, 0.18) if cuts else 1.0
    result = jax.random.normal(own_key, dims, jnp.float32) * deviation * factor_of
    return jnp.minimum(jnp.maximum(result, -limit), limit).astype(held_as)


def setup_inputs(seed: int = 0) -> dict:
    key_of = jax.random.split(jax.random.key(seed), 13)
    queries = draw_queries(jax.random.fold_in(key_of[12], 71), 0)
    key_rows = draw_key_rows(jax.random.fold_in(key_of[12], 71), 0)
    value_rows = centred(key_of[2], (TOKENS, HEADS * DH), 1.0, 5.0, ((0, 64), (1, 8)))
    residual = centred(key_of[3], (TOKENS, D), 0.25, 1.5, ((0, 64), (1, 8)))
    out_weight = centred(key_of[4], (HEADS * DH, D), (HEADS * DH) ** -0.5, 0.09375, ((0, 8), (1, 64)))
    norm_gain = jnp.clip(1.0 + 0.1 * jax.random.normal(key_of[5], (D,), jnp.float32), 0.5, 1.5)
    norm_bias = centred(key_of[6], (D,), 0.2, 1.0, ((0, 8),), jnp.float32)
    global_list = jax.random.randint(key_of[7], (GLOB,), 0, BLOCKS).astype(jnp.int32)
    random_device_keys = jax.random.split(jax.random.fold_in(key_of[8], 1), BLOCKS // BLK_DEV)
    random_device_turns = jax.random.permutation(jax.random.fold_in(key_of[8], 3), BLOCKS // BLK_DEV)
    random_device = jax.vmap(lambda own, number: assign_block(jax.random.fold_in(key_of[8], 2), own, number, BLK_DEV, N_SEQ, RAND, CAP, 2))(random_device_keys, random_device_turns).reshape((BLOCKS, RAND))
    random_offset = with_ends(jax.random.randint(key_of[9], (BLOCKS, RAND), 0, BLK_DEV), jax.random.fold_in(key_of[9], 1), 0, BLK_DEV - 1).astype(jnp.int32)
    drop_seed = jax.random.randint(key_of[10], (1,), 0, 65536).astype(jnp.int32)
    drop_offsets = with_ends(jax.random.randint(key_of[11], (BLOCKS,), 0, 8388608), jax.random.fold_in(key_of[11], 1), 0, 8388607).astype(jnp.int32)
    return {"queries": queries, "key_rows": key_rows, "value_rows": value_rows, "residual": residual, "out_weight": out_weight, "norm_gain": norm_gain, "norm_bias": norm_bias, "global_list": global_list, "random_device": random_device, "random_offset": random_offset, "drop_seed": drop_seed, "drop_offsets": drop_offsets}


def mix_bits(counter, seed_value):
    hashed = counter + seed_value * 1000003
    for rounds in range(2):
        hashed = jnp.bitwise_xor(hashed, lax.shift_right_logical(hashed, jnp.int32(16)))
        hashed = hashed * 73244475
    hashed = jnp.bitwise_xor(hashed, lax.shift_right_logical(hashed, jnp.int32(16)))
    return hashed

def keep_table(counter, seed_value):
    hashed = mix_bits(counter, seed_value)
    kept = jnp.bitwise_and(hashed, 1023) >= 102
    return jnp.where(kept, jnp.float32(1024.0 / 922.0), jnp.float32(0.0))

def reference(queries, key_rows, value_rows, residual, out_weight, norm_gain, norm_bias, global_list, random_device, random_offset, drop_seed, drop_offsets):
    width_all = HEADS * DH
    paired = jnp.concatenate([key_rows, value_rows], axis=1).reshape(BLOCKS, BLOCK, 2 * width_all)
    block_ids = jnp.arange(BLOCKS, dtype=jnp.int32)
    window = jnp.stack([(block_ids - 1) % BLOCKS, block_ids, (block_ids + 1) % BLOCKS], axis=1).astype(jnp.int32)
    glob_cols = jnp.broadcast_to(global_list[None, :], (BLOCKS, GLOB)).astype(jnp.int32)
    random_ids = (random_device * BLK_DEV + random_offset).astype(jnp.int32)
    key_lists = jnp.concatenate([window, glob_cols, random_ids], axis=1)
    list_len = key_lists.shape[1]
    group_count = BLOCKS // BLK_DEV
    query_groups = queries.reshape(group_count, BLK_DEV, BLOCK, HEADS, DH)
    list_groups = key_lists.reshape(group_count, BLK_DEV, list_len)
    score_scale = jnp.float32(1.0 / DH ** 0.5)

    def one_group(packed):
        query_part, list_part = packed
        listed = jnp.take(paired, list_part.reshape(-1), axis=0)
        listed = listed.reshape(BLK_DEV, list_len * BLOCK, 2 * width_all)
        key_heads = listed[:, :, :width_all].reshape(BLK_DEV, list_len * BLOCK, HEADS, DH).astype(jnp.float32)
        value_heads = listed[:, :, width_all:].reshape(BLK_DEV, list_len * BLOCK, HEADS, DH).astype(jnp.float32)
        scores = jnp.einsum('bqhd,bkhd->bhqk', query_part.astype(jnp.float32), key_heads) * score_scale
        top_score = lax.optimization_barrier(jnp.max(scores, axis=-1, keepdims=True))
        expo = jnp.exp(scores - top_score)
        attn_probs = (expo / lax.optimization_barrier(jnp.sum(expo, axis=-1, keepdims=True))).astype(jnp.bfloat16)
        context = jnp.einsum('bhqk,bkhd->bqhd', attn_probs.astype(jnp.float32), value_heads)
        return context.astype(jnp.bfloat16)
    context = lax.map(one_group, (query_groups, list_groups)).reshape(TOKENS, width_all)
    group_width = width_all // N_TP
    attended = jnp.zeros((TOKENS, D), jnp.float32)
    for group in range(N_TP):
        part = jnp.dot(context[:, group * group_width:(group + 1) * group_width], out_weight[group * group_width:(group + 1) * group_width], preferred_element_type=jnp.float32)
        part = lax.optimization_barrier(part.astype(jnp.bfloat16))
        attended = attended + part.astype(jnp.float32)
    inner = jnp.arange(BLOCK, dtype=jnp.int32)
    columns = jnp.arange(D, dtype=jnp.int32)
    counter = drop_offsets[:, None, None] + inner[None, :, None] * D + columns[None, None, :]
    keep_factor = keep_table(counter.astype(jnp.int32), drop_seed[0]).reshape(TOKENS, D)
    summed_rows = residual.astype(jnp.float32) + keep_factor * attended
    row_mean = lax.optimization_barrier(jnp.mean(summed_rows, axis=1, keepdims=True))
    centered = summed_rows - row_mean
    row_var = lax.optimization_barrier(jnp.mean(centered * centered, axis=1, keepdims=True))
    encoded = centered * lax.rsqrt(row_var + 1e-05) * norm_gain[None, :] + norm_bias[None, :]
    return encoded.astype(jnp.bfloat16)
```

```python
import functools

import jax
import jax.numpy as jnp
from jax import lax
from jax.experimental import pallas as pl
from jax.experimental.pallas import tpu as pltpu
from jax.sharding import PartitionSpec as P

D = 4096
DH = 128
BLOCK = 16
GLOB = 2
RAND = 3
CAP = 2
BF = jnp.bfloat16
F32 = jnp.float32
VMEM_LIMIT = 48 * 1024 * 1024


def whole(shape):
    return pl.BlockSpec(shape, lambda *a: (0,) * len(shape))


def params():
    return pltpu.CompilerParams(vmem_limit_bytes=VMEM_LIMIT)


def pack_kernel(want_ref, k_ref, v_ref, out_ref):
    width = k_ref.shape[1]

    def step(i, carry):
        rows = pl.ds(pl.multiple_of(want_ref[i] * BLOCK, BLOCK), BLOCK)
        out_ref[i, :, :width] = k_ref[rows, :]
        out_ref[i, :, width:] = v_ref[rows, :]
        return carry

    lax.fori_loop(0, out_ref.shape[0], step, 0, unroll=8)


def pack(want, k, v):
    slots = want.shape[0]
    width = k.shape[1]
    out = (slots, BLOCK, 2 * width)
    return pl.pallas_call(
        pack_kernel,
        grid_spec=pltpu.PrefetchScalarGridSpec(
            num_scalar_prefetch=1,
            grid=(1,),
            in_specs=[whole(k.shape), whole(v.shape)],
            out_specs=whole(out),
        ),
        out_shape=jax.ShapeDtypeStruct(out, BF),
        compiler_params=params(),
        cost_estimate=pl.CostEstimate(flops=0, transcendentals=0, bytes_accessed=5 << 20),
        name="pack",
    )(want, k, v)


def attend_kernel(
    pick_ref, q_ref, k_ref, v_ref, prev_ref, next_ref, glob_ref, rep_ref, out_ref
):
    width = q_ref.shape[1]
    blocks = q_ref.shape[0] // BLOCK
    scale = jnp.float32(1.0 / DH**0.5)

    def pieces(local_ref, offset, b, h):
        lo, hi = h * DH, (h + 1) * DH
        olo, ohi = offset + lo, offset + hi
        parts = []
        if b == 0:
            parts.append(prev_ref[:, olo:ohi])
            parts.append(local_ref[0 : 2 * BLOCK, lo:hi])
        elif b == blocks - 1:
            parts.append(local_ref[(b - 1) * BLOCK : (b + 1) * BLOCK, lo:hi])
            parts.append(next_ref[:, olo:ohi])
        else:
            parts.append(local_ref[(b - 1) * BLOCK : (b + 2) * BLOCK, lo:hi])
        tile = olo // DH
        chunk, inner = tile // 2, tile % 2
        for g in range(GLOB):
            at = (2 * g + inner) * DH
            parts.append(glob_ref[chunk * BLOCK : (chunk + 1) * BLOCK, at : at + DH])
        for r in range(RAND):
            parts.append(rep_ref[pick_ref[b * RAND + r], :, olo:ohi])
        return jnp.concatenate(parts, axis=0)

    for b in range(blocks):
        rows = slice(b * BLOCK, (b + 1) * BLOCK)
        for h in range(width // DH):
            keys = pieces(k_ref, 0, b, h)
            vals = pieces(v_ref, width, b, h)
            query = q_ref[rows, h * DH : (h + 1) * DH]
            scores = (
                lax.dot_general(
                    query, keys, (((1,), (1,)), ((), ())), preferred_element_type=F32
                )
                * scale
            )
            expo = jnp.exp(scores - jnp.max(scores, axis=-1, keepdims=True))
            probs = (expo / jnp.sum(expo, axis=-1, keepdims=True)).astype(BF)
            got = jnp.dot(probs, vals, preferred_element_type=F32)
            out_ref[rows, h * DH : (h + 1) * DH] = got.astype(BF)


def attend(pick, q, k, v, prev, after, glob, rep):
    args = (q, k, v, prev, after, glob, rep)
    return pl.pallas_call(
        attend_kernel,
        grid_spec=pltpu.PrefetchScalarGridSpec(
            num_scalar_prefetch=1,
            grid=(1,),
            in_specs=[whole(a.shape) for a in args],
            out_specs=whole(q.shape),
        ),
        out_shape=jax.ShapeDtypeStruct(q.shape, BF),
        compiler_params=params(),
        cost_estimate=pl.CostEstimate(
            flops=4 * 256 * 128 * 512, transcendentals=256 * 128 * 4, bytes_accessed=6 << 20
        ),
        name="attend",
    )(pick, *args)


def project_kernel(
    where_ref, drop_ref, mine_ref, other_ref, w_ref, res_ref, sum_ref, stat_ref, acc_ref
):
    step = pl.program_id(0)
    half = mine_ref.shape[0]
    lhs = jnp.where(step < half, 0, 1)

    @pl.when(step == 0)
    def _():
        acc_ref[...] = jnp.zeros_like(acc_ref)

    def add(ref, at):
        acc_ref[...] += lax.dot_general(
            ref[at], w_ref[0], (((1,), (1,)), ((), ())), preferred_element_type=F32
        )

    @pl.when(lhs == 0)
    def _():
        add(mine_ref, step)

    @pl.when(lhs == 1)
    def _():
        add(other_ref, step - half)

    @pl.when(step == pl.num_programs(0) - 1)
    def _():
        cols = acc_ref.shape[1]
        blocks = acc_ref.shape[0] // BLOCK
        seed = where_ref[1] * 1000003 + where_ref[2] * cols
        inner = lax.broadcasted_iota(jnp.int32, (BLOCK, cols), 0) * D
        inner = inner + lax.broadcasted_iota(jnp.int32, (BLOCK, cols), 1) + seed
        lane = lax.broadcasted_iota(jnp.int32, (BLOCK, DH), 1)
        for b in range(blocks):
            rows = slice(b * BLOCK, (b + 1) * BLOCK)
            hashed = inner + drop_ref[b]
            for _ in range(2):
                hashed = hashed ^ lax.shift_right_logical(hashed, jnp.int32(16))
                hashed = hashed * 73244475
            hashed = hashed ^ lax.shift_right_logical(hashed, jnp.int32(16))
            kept = (hashed & 1023) >= 102
            keep = jnp.where(kept, jnp.float32(1024.0 / 922.0), jnp.float32(0.0))
            total = res_ref[rows, :].astype(F32) + keep * acc_ref[rows, :]
            sum_ref[rows, :] = total
            mean = jnp.sum(total, axis=1, keepdims=True) * jnp.float32(1.0 / cols)
            dev = total - mean
            spread = jnp.sum(dev * dev, axis=1, keepdims=True)
            stat_ref[rows, :] = jnp.where(lane == 0, mean, spread)


def project(where, drops, mine, other, weight, residual):
    rows, cols = residual.shape
    half = mine.shape[0]
    steps = 2 * half

    def w_map(i, where_ref, drop_ref):
        core = where_ref[0]
        own = 2 * i + core
        far = 2 * (i - half) + (1 - core)
        return (jnp.where(i < half, own, far), 0, 0)

    return pl.pallas_call(
        project_kernel,
        grid_spec=pltpu.PrefetchScalarGridSpec(
            num_scalar_prefetch=2,
            grid=(steps,),
            in_specs=[
                whole(mine.shape),
                whole(other.shape),
                pl.BlockSpec((1,) + weight.shape[1:], w_map),
                whole(residual.shape),
            ],
            out_specs=[whole((rows, cols)), whole((rows, DH))],
            scratch_shapes=[pltpu.VMEM((rows, cols), F32)],
        ),
        out_shape=[
            jax.ShapeDtypeStruct((rows, cols), F32),
            jax.ShapeDtypeStruct((rows, DH), F32),
        ],
        compiler_params=params(),
        cost_estimate=pl.CostEstimate(
            flops=2 * rows * D * cols, transcendentals=0, bytes_accessed=8 << 20
        ),
        name="project",
    )(where, drops, mine, other, weight, residual)


def on_device(
    queries,
    key_rows,
    value_rows,
    residual,
    out_weight,
    norm_gain,
    norm_bias,
    global_list,
    random_device,
    random_offset,
    drop_seed,
    drop_offsets,
):
    row_count, width_here = queries.shape
    block_count = row_count // BLOCK
    seq_count = lax.axis_size("seq")
    tp_count = lax.axis_size("tp")
    tp_at = lax.axis_index("tp")
    cols_here = out_weight.shape[1]

    per = seq_count // tp_count
    moves = [
        (s * tp_count + t, (t * per + s % per) * tp_count + s // per)
        for s in range(seq_count)
        for t in range(tp_count)
    ]
    moved = lax.ppermute(out_weight.T, ("seq", "tp"), moves)
    weight = lax.all_gather(moved, "seq", axis=0, tiled=True)
    weight = weight.reshape(tp_count, per * cols_here, width_here)

    request_count = block_count * RAND
    target = random_device.reshape(request_count)
    wanted = random_offset.reshape(request_count)
    rank = jnp.arange(request_count, dtype=jnp.int32)
    same = target[:, None] == target[None, :]
    earlier = rank[None, :] < rank[:, None]
    slot = jnp.sum(jnp.logical_and(same, earlier), axis=1).astype(jnp.int32)
    dest_ids = jnp.arange(seq_count, dtype=jnp.int32)
    matched = jnp.logical_and(
        target[None, None, :] == dest_ids[:, None, None],
        slot[None, None, :] == jnp.arange(CAP, dtype=jnp.int32)[None, :, None],
    )
    table = jnp.sum(jnp.where(matched, wanted[None, None, :], 0), axis=2)
    chunks = seq_count // BLOCK
    share = 2 * width_here // chunks
    sent = []
    for which in range(GLOB):
        first = (global_list[which] % block_count) * BLOCK
        block = jnp.concatenate(
            [
                lax.dynamic_slice_in_dim(key_rows, first, BLOCK, axis=0),
                lax.dynamic_slice_in_dim(value_rows, first, BLOCK, axis=0),
            ],
            axis=1,
        )
        block = block.reshape(BLOCK, chunks, share).transpose(1, 0, 2)
        sent.append(block.reshape(seq_count, share))
    sent.append(jnp.pad(table.astype(BF), ((0, 0), (0, 2 * share - CAP))))
    first_payload = jnp.concatenate(sent, axis=1).reshape(seq_count, 8, DH)
    first_got = lax.all_to_all(first_payload, "seq", split_axis=0, concat_axis=0, tiled=True)
    want = first_got[:, 4, :CAP].astype(jnp.int32).reshape(seq_count * CAP)

    replies = pack(want, key_rows, value_rows)
    replies = lax.all_to_all(
        replies.reshape(seq_count, CAP, BLOCK, 2 * width_here),
        "seq",
        split_axis=0,
        concat_axis=0,
        tiled=True,
    ).reshape(seq_count * CAP, BLOCK, 2 * width_here)

    held = jnp.concatenate(
        [
            lax.dynamic_index_in_dim(first_got, global_list[g] // block_count, 0)[
                :, 2 * g : 2 * g + 2
            ]
            for g in range(GLOB)
        ]
        + [jnp.zeros((1, 4, DH), BF)],
        axis=1,
    )
    held = jnp.broadcast_to(held, (seq_count, 8, DH))
    glob = lax.all_to_all(held, "seq", split_axis=0, concat_axis=0, tiled=True)
    glob = glob.reshape(seq_count, 8 * DH)

    up = [(i, (i + 1) % seq_count) for i in range(seq_count)]
    down = [(j, i) for i, j in up]
    tail = row_count - BLOCK
    last = jnp.concatenate([key_rows[tail:], value_rows[tail:]], axis=1)
    head = jnp.concatenate([key_rows[:BLOCK], value_rows[:BLOCK]], axis=1)
    prev = lax.ppermute(last, "seq", up)
    after = lax.ppermute(head, "seq", down)

    context = attend(
        target * CAP + slot, queries, key_rows, value_rows, prev, after, glob, replies
    )

    pairs = tp_count // 2
    groups = [[2 * z + c for z in range(pairs)] for c in range(2)]
    mine = lax.all_to_all(
        jnp.broadcast_to(context[None], (pairs,) + context.shape),
        "tp",
        split_axis=0,
        concat_axis=0,
        tiled=True,
        axis_index_groups=groups,
    )
    other = lax.ppermute(mine, "tp", [(i, i ^ 1) for i in range(tp_count)])

    where = jnp.stack([tp_at % 2, drop_seed[0], tp_at]).astype(jnp.int32)
    summed, stats = project(where, drop_offsets, mine, other, weight, residual)

    stats = jnp.broadcast_to(stats[:, :2].T[None], (tp_count, 2, row_count))
    stats = lax.all_to_all(stats, "tp", split_axis=0, concat_axis=0, tiled=True)
    means, spreads = stats[:, 0], stats[:, 1]
    mean = jnp.sum(means, axis=0) / tp_count
    away = means - mean[None]
    cols = summed.shape[1]
    spread = jnp.sum(spreads, axis=0) + cols * jnp.sum(away * away, axis=0)
    factor = lax.rsqrt(spread / D + 1e-05)
    encoded = (summed - mean[:, None]) * factor[:, None] * norm_gain[None] + norm_bias[None]
    return encoded.astype(BF)


def solution(mesh):
    placed = (
        P("seq", "tp"),
        P("seq", "tp"),
        P("seq", "tp"),
        P("seq", "tp"),
        P("tp", "seq"),
        P("tp"),
        P("tp"),
        P(),
        P("seq", None),
        P("seq", None),
        P(),
        P("seq"),
    )
    return jax.shard_map(
        on_device, mesh=mesh, in_specs=placed, out_specs=P("seq", "tp"), check_vma=False
    )
```

```python
import jax
import jax.numpy as jnp
from jax import lax
from jax.experimental import pallas as pl
from jax.experimental.pallas import tpu as pltpu
from jax.sharding import Mesh
from jax.sharding import PartitionSpec as P

D = 4096
DH = 128
BLOCK = 16
GLOB = 2
RAND = 3
CAP = 2
BF = jnp.bfloat16
F32 = jnp.float32
SEQ = ("y", "x", "zh")
TP = ("zl", "core")
PLANE = ("x", "zh")
VMEM_LIMIT = 48 * 1024 * 1024


def whole(shape):
    return pl.BlockSpec(shape, lambda *a: (0,) * len(shape))


def params():
    return pltpu.CompilerParams(vmem_limit_bytes=VMEM_LIMIT)


def pack_kernel(want_ref, pool_ref, out_ref):
    def step(i, carry):
        rows = pl.ds(pl.multiple_of(want_ref[i] * BLOCK, BLOCK), BLOCK)
        out_ref[i] = pool_ref[rows, :]
        return carry

    lax.fori_loop(0, out_ref.shape[0], step, 0, unroll=8)


def pack(want, pool):
    out = (want.shape[0], BLOCK, pool.shape[1])
    return pl.pallas_call(
        pack_kernel,
        grid_spec=pltpu.PrefetchScalarGridSpec(
            num_scalar_prefetch=1,
            grid=(1,),
            in_specs=[whole(pool.shape)],
            out_specs=whole(out),
        ),
        out_shape=jax.ShapeDtypeStruct(out, BF),
        compiler_params=params(),
        cost_estimate=pl.CostEstimate(flops=0, transcendentals=0, bytes_accessed=9 << 20),
        name="pack",
    )(want, pool)


def attend_kernel(pick_ref, q_ref, k_ref, v_ref, prev_ref, next_ref, rep_ref, out_ref):
    width = q_ref.shape[1]
    blocks = q_ref.shape[0] // BLOCK
    heads = width // DH
    scale = jnp.float32(1.0 / DH**0.5)

    def listed(local_ref, offset, b, h):
        lo, hi = h * DH, (h + 1) * DH
        olo, ohi = offset + lo, offset + hi
        parts = []
        if b == 0:
            parts.append(prev_ref[:, olo:ohi])
            parts.append(local_ref[0 : 2 * BLOCK, lo:hi])
        elif b == blocks - 1:
            parts.append(local_ref[(b - 1) * BLOCK : (b + 1) * BLOCK, lo:hi])
            parts.append(next_ref[:, olo:ohi])
        else:
            parts.append(local_ref[(b - 1) * BLOCK : (b + 2) * BLOCK, lo:hi])
        for g in range(GLOB):
            parts.append(rep_ref[pick_ref[blocks * RAND + g], :, olo:ohi])
        for r in range(RAND):
            parts.append(rep_ref[pick_ref[b * RAND + r], :, olo:ohi])
        return jnp.concatenate(parts, axis=0)

    for first in range(0, blocks, 4):
        pairs = [(b, h) for b in range(first, first + 4) for h in range(heads)]
        scores = []
        for b, h in pairs:
            query = q_ref[b * BLOCK : (b + 1) * BLOCK, h * DH : (h + 1) * DH]
            scores.append(
                lax.dot_general(
                    query,
                    listed(k_ref, 0, b, h),
                    (((1,), (1,)), ((), ())),
                    preferred_element_type=F32,
                )
            )
        scores = jnp.concatenate(scores, axis=0) * scale
        expo = jnp.exp(scores - jnp.max(scores, axis=-1, keepdims=True))
        probs = (expo / jnp.sum(expo, axis=-1, keepdims=True)).astype(BF)
        for i, (b, h) in enumerate(pairs):
            got = jnp.dot(
                probs[i * BLOCK : (i + 1) * BLOCK],
                listed(v_ref, width, b, h),
                preferred_element_type=F32,
            )
            out_ref[b * BLOCK : (b + 1) * BLOCK, h * DH : (h + 1) * DH] = got.astype(BF)


def attend(pick, q, k, v, prev, after, rep):
    args = (q, k, v, prev, after, rep)
    return pl.pallas_call(
        attend_kernel,
        grid_spec=pltpu.PrefetchScalarGridSpec(
            num_scalar_prefetch=1,
            grid=(1,),
            in_specs=[whole(a.shape) for a in args],
            out_specs=whole(q.shape),
        ),
        out_shape=jax.ShapeDtypeStruct(q.shape, BF),
        compiler_params=params(),
        cost_estimate=pl.CostEstimate(
            flops=4 * 256 * 128 * 512, transcendentals=256 * 128 * 4, bytes_accessed=6 << 20
        ),
        name="attend",
    )(pick, *args)


def project_kernel(
    where_ref, drop_ref, mine_ref, other_ref, w_ref, res_ref, sum_ref, stat_ref, acc_ref
):
    step = pl.program_id(0)
    half = mine_ref.shape[0]
    lhs = jnp.where(step < half, 0, 1)

    @pl.when(step == 0)
    def _():
        acc_ref[...] = jnp.zeros_like(acc_ref)

    def add(ref, at):
        acc_ref[...] += lax.dot_general(
            ref[at], w_ref[0], (((1,), (1,)), ((), ())), preferred_element_type=F32
        )

    @pl.when(lhs == 0)
    def _():
        add(mine_ref, step)

    @pl.when(lhs == 1)
    def _():
        add(other_ref, step - half)

    @pl.when(step == pl.num_programs(0) - 1)
    def _():
        cols = acc_ref.shape[1]
        blocks = acc_ref.shape[0] // BLOCK
        seed = where_ref[1] * 1000003 + where_ref[2] * cols
        inner = lax.broadcasted_iota(jnp.int32, (BLOCK, cols), 0) * D
        inner = inner + lax.broadcasted_iota(jnp.int32, (BLOCK, cols), 1) + seed
        lane = lax.broadcasted_iota(jnp.int32, (BLOCK, DH), 1)
        for b in range(blocks):
            rows = slice(b * BLOCK, (b + 1) * BLOCK)
            hashed = inner + drop_ref[b]
            for _ in range(2):
                hashed = hashed ^ lax.shift_right_logical(hashed, jnp.int32(16))
                hashed = hashed * 73244475
            hashed = hashed ^ lax.shift_right_logical(hashed, jnp.int32(16))
            kept = (hashed & 1023) >= 102
            keep = jnp.where(kept, jnp.float32(1024.0 / 922.0), jnp.float32(0.0))
            total = res_ref[rows, :].astype(F32) + keep * acc_ref[rows, :]
            sum_ref[rows, :] = total
            mean = jnp.sum(total, axis=1, keepdims=True) * jnp.float32(1.0 / cols)
            dev = total - mean
            spread = jnp.sum(dev * dev, axis=1, keepdims=True)
            stat_ref[rows, :] = jnp.where(lane == 0, mean, spread)


def project(where, drops, mine, other, weight, residual):
    rows, cols = residual.shape
    half = mine.shape[0]
    steps = 2 * half

    def w_map(i, where_ref, drop_ref):
        core = where_ref[0]
        own = 2 * i + core
        far = 2 * (i - half) + (1 - core)
        return (jnp.where(i < half, own, far), 0, 0)

    return pl.pallas_call(
        project_kernel,
        grid_spec=pltpu.PrefetchScalarGridSpec(
            num_scalar_prefetch=2,
            grid=(steps,),
            in_specs=[
                whole(mine.shape),
                whole(other.shape),
                pl.BlockSpec((1,) + weight.shape[1:], w_map),
                whole(residual.shape),
            ],
            out_specs=[whole((rows, cols)), whole((rows, DH))],
            scratch_shapes=[pltpu.VMEM((rows, cols), F32)],
        ),
        out_shape=[
            jax.ShapeDtypeStruct((rows, cols), F32),
            jax.ShapeDtypeStruct((rows, DH), F32),
        ],
        compiler_params=params(),
        cost_estimate=pl.CostEstimate(
            flops=2 * rows * D * cols, transcendentals=0, bytes_accessed=8 << 20
        ),
        name="project",
    )(where, drops, mine, other, weight, residual)


def on_device(
    queries,
    key_rows,
    value_rows,
    residual,
    out_weight,
    norm_gain,
    norm_bias,
    global_list,
    random_device,
    random_offset,
    drop_seed,
    drop_offsets,
):
    row_count, width_here = queries.shape
    block_count = row_count // BLOCK
    n_y, n_x, n_zh = (lax.axis_size(a) for a in SEQ)
    plane = n_x * n_zh
    seq_count = n_y * plane
    n_zl = lax.axis_size("zl")
    tp_count = n_zl * lax.axis_size("core")
    tp_at = lax.axis_index(TP)
    cols_here = out_weight.shape[1]

    paired = jnp.concatenate([key_rows, value_rows], axis=1)
    pool = lax.all_gather(paired, "y", axis=0, tiled=True)

    moves = [
        ((y * plane + p) * tp_count + t, (t * plane + p) * tp_count + y)
        for y in range(n_y)
        for p in range(plane)
        for t in range(tp_count)
    ]
    moved = lax.ppermute(out_weight.T, SEQ + TP, moves)

    request_count = block_count * RAND
    target = random_device.reshape(request_count)
    wanted = random_offset.reshape(request_count)
    rank = jnp.arange(request_count, dtype=jnp.int32)
    same = target[:, None] == target[None, :]
    earlier = rank[None, :] < rank[:, None]
    slot = jnp.sum(jnp.logical_and(same, earlier), axis=1).astype(jnp.int32)
    place = (target // plane) * CAP + slot
    column = target % plane
    slots = n_y * CAP
    matched = jnp.logical_and(
        column[None, None, :] == jnp.arange(plane, dtype=jnp.int32)[:, None, None],
        place[None, None, :] == jnp.arange(slots, dtype=jnp.int32)[None, :, None],
    )
    table = jnp.sum(jnp.where(matched, wanted[None, None, :], 0), axis=2)
    asked = jnp.pad(table.astype(BF)[:, None, :], ((0, 0), (0, 7), (0, width_here - slots)))
    spread_w = jnp.broadcast_to(moved[None], (plane,) + moved.shape)
    got = lax.all_to_all(
        jnp.concatenate([spread_w, asked], axis=1),
        PLANE,
        split_axis=0,
        concat_axis=0,
        tiled=True,
    )
    want = got[:, cols_here, :slots].astype(jnp.int32)
    weight = lax.all_gather(
        got[:, :cols_here].reshape(plane * cols_here, width_here), "y", axis=0, tiled=True
    )
    weight = weight.reshape(tp_count, plane * cols_here, width_here)

    base = (jnp.arange(slots, dtype=jnp.int32) // CAP) * block_count
    owner = global_list // block_count
    glob_row = (owner // plane) * block_count + global_list % block_count
    want = jnp.concatenate(
        [want + base[None], jnp.broadcast_to(glob_row[None], (plane, GLOB))], axis=1
    )
    sent = slots + GLOB
    replies = pack(want.reshape(plane * sent), pool)
    replies = lax.all_to_all(
        replies.reshape(plane, sent, BLOCK, 2 * width_here),
        PLANE,
        split_axis=0,
        concat_axis=0,
        tiled=True,
    ).reshape(plane * sent, BLOCK, 2 * width_here)

    up = [(i, (i + 1) % seq_count) for i in range(seq_count)]
    down = [(j, i) for i, j in up]
    tail = row_count - BLOCK
    prev = lax.ppermute(paired[tail:], SEQ, up)
    after = lax.ppermute(paired[:BLOCK], SEQ, down)

    pick = jnp.concatenate(
        [
            column * sent + place,
            (owner % plane) * sent + slots + jnp.arange(GLOB, dtype=jnp.int32),
        ]
    )
    context = attend(pick, queries, key_rows, value_rows, prev, after, replies)

    mine = lax.all_to_all(
        jnp.broadcast_to(context[None], (n_zl,) + context.shape),
        "zl",
        split_axis=0,
        concat_axis=0,
        tiled=True,
    )
    other = lax.ppermute(mine, "core", [(0, 1), (1, 0)])

    where = jnp.stack([tp_at % 2, drop_seed[0], tp_at]).astype(jnp.int32)
    summed, stats = project(where, drop_offsets, mine, other, weight, residual)

    stats = jnp.broadcast_to(stats[:, :2].T[None], (tp_count, 2, row_count))
    stats = lax.all_to_all(stats, TP, split_axis=0, concat_axis=0, tiled=True)
    means, spreads = stats[:, 0], stats[:, 1]
    mean = jnp.sum(means, axis=0) / tp_count
    away = means - mean[None]
    cols = summed.shape[1]
    spread = jnp.sum(spreads, axis=0) + cols * jnp.sum(away * away, axis=0)
    factor = lax.rsqrt(spread / D + 1e-05)
    encoded = (summed - mean[:, None]) * factor[:, None] * norm_gain[None] + norm_bias[None]
    return encoded.astype(BF)


def solution(mesh):
    fine = Mesh(mesh.devices.reshape(8, 4, 2, 4, 2), SEQ + TP)
    placed = (
        P(SEQ, TP),
        P(SEQ, TP),
        P(SEQ, TP),
        P(SEQ, TP),
        P(TP, SEQ),
        P(TP),
        P(TP),
        P(),
        P(SEQ, None),
        P(SEQ, None),
        P(),
        P(SEQ),
    )
    return jax.shard_map(
        on_device, mesh=fine, in_specs=placed, out_specs=P(SEQ, TP), check_vma=False
    )
```

```python
import functools

import jax
import jax.numpy as jnp
from jax import lax
from jax.experimental import pallas as pl
from jax.experimental.pallas import tpu as pltpu
from jax.sharding import Mesh
from jax.sharding import PartitionSpec as P

D = 4096
DH = 128
BLOCK = 16
GLOB = 2
RAND = 3
CAP = 2
BF = jnp.bfloat16
F32 = jnp.float32
SEQ = ("y", "x", "zh")
TP = ("zl", "core")
PLANE = ("x", "zh")
PARTS = 2
STAT_ROWS = 16
NEG = -1e30
VMEM_LIMIT = 48 * 1024 * 1024


def whole(shape):
    return pl.BlockSpec(shape, lambda *a: (0,) * len(shape))


def params():
    return pltpu.CompilerParams(vmem_limit_bytes=VMEM_LIMIT)


def partial(scores, listed, values):
    scores = jnp.where(listed, scores, NEG)
    top = jnp.max(scores, axis=0, keepdims=True)
    expo = jnp.where(listed, jnp.exp(scores - top), 0.0)
    total = jnp.sum(expo, axis=0, keepdims=True)
    got = lax.dot_general(
        expo.astype(BF), values, (((0,), (0,)), ((), ())), preferred_element_type=F32
    )
    return top, total, got


def dot_t(a, b):
    return lax.dot_general(a, b, (((1,), (1,)), ((), ())), preferred_element_type=F32)


def split(x, parts):
    out = []
    for _ in range(parts):
        out.append(x.astype(BF))
        x = x - out[-1].astype(F32)
    return out


def serve_kernel(row_ref, mark_ref, zh_ref, q_ref, pool_ref, out_ref):
    peer = pl.program_id(0)
    rows = q_ref.shape[2]
    wide = q_ref.shape[3]
    listings = row_ref.shape[0] // pl.num_programs(0)
    scale = jnp.float32(1.0 / DH**0.5)
    block_of = lax.broadcasted_iota(jnp.int32, (BLOCK, rows), 1) // BLOCK
    places, listed = [], []
    for i in range(listings):
        at = peer * listings + i
        places.append(pl.ds(pl.multiple_of(row_ref[at] * BLOCK, BLOCK), BLOCK))
        mark = mark_ref[at]
        listed.append(jnp.logical_or(block_of == mark, jnp.full(block_of.shape, mark) < 0))
    listed = jnp.concatenate(listed, axis=0)
    stats = []
    for h in range(wide // DH):
        lanes = slice(h * DH, (h + 1) * DH)
        keys = jnp.concatenate([pool_ref[p, lanes] for p in places], axis=0)
        after = slice(wide + h * DH, wide + (h + 1) * DH)
        values = jnp.concatenate([pool_ref[p, after] for p in places], axis=0)
        top, total, got = partial(
            dot_t(keys, q_ref[0, 0, :, lanes]) * scale, listed, values
        )
        out_ref[0, :rows, lanes] = got.astype(BF)
        stats += split(top, 3) + split(total, 2)
    stats.append(jnp.zeros((STAT_ROWS - len(stats), rows), BF))
    out_ref[0, rows:, :] = jnp.concatenate([x.astype(F32) for x in stats], axis=0).astype(BF)


def serve(row, mark, zh, q, pool, out_rows):
    n_x, _, _, wide = q.shape
    rows = out_rows
    peers = 2 * n_x
    out = (peers, rows + STAT_ROWS, wide)
    return pl.pallas_call(
        serve_kernel,
        grid_spec=pltpu.PrefetchScalarGridSpec(
            num_scalar_prefetch=3,
            grid=(peers,),
            in_specs=[
                pl.BlockSpec((1, 1, rows, wide), lambda i, a, b, c: (i // 2, i % 2, 0, 0)),
                whole(pool.shape),
            ],
            out_specs=pl.BlockSpec(
                (1,) + out[1:], lambda i, a, b, zh_ref: (2 * (i // 2) + (i % 2 + zh_ref[0]) % 2, 0, 0)
            ),
        ),
        out_shape=jax.ShapeDtypeStruct(out, BF),
        compiler_params=params(),
        cost_estimate=pl.CostEstimate(
            flops=4 * peers * rows * 320 * wide,
            transcendentals=peers * rows * 320 * wide // DH,
            bytes_accessed=4 << 20,
        ),
        name="serve",
    )(row, mark, zh, q, pool)


def local_kernel(q_ref, k_ref, v_ref, out_ref, stat_ref):
    rows = q_ref.shape[0]
    heads = q_ref.shape[1] // DH
    scale = jnp.float32(1.0 / DH**0.5)
    key_block = lax.broadcasted_iota(jnp.int32, (rows, rows), 0) // BLOCK
    query_block = lax.broadcasted_iota(jnp.int32, (rows, rows), 1) // BLOCK
    listed = jnp.abs(key_block - query_block) <= 1
    tops, totals = [], []
    for h in range(heads):
        lanes = slice(h * DH, (h + 1) * DH)
        top, total, got = partial(
            dot_t(k_ref[:, lanes], q_ref[:, lanes]) * scale, listed, v_ref[:, lanes]
        )
        out_ref[:, lanes] = got
        tops.append(top)
        totals.append(total)
    stat_ref[...] = jnp.concatenate(tops + totals, axis=0)


def local(q, k, v):
    rows, width = q.shape
    stat = (2 * (width // DH), rows)
    return pl.pallas_call(
        local_kernel,
        grid=(1,),
        in_specs=[whole(q.shape)] * 3,
        out_specs=[whole(q.shape), whole(stat)],
        out_shape=[jax.ShapeDtypeStruct(q.shape, F32), jax.ShapeDtypeStruct(stat, F32)],
        compiler_params=params(),
        cost_estimate=pl.CostEstimate(
            flops=4 * rows * rows * width,
            transcendentals=rows * rows * width // DH,
            bytes_accessed=2 << 20,
        ),
        name="local",
    )(q, k, v)


def merge_kernel(first, got_ref, near_ref, stat_ref, out_ref):
    peers, rows, wide = got_ref.shape
    rows = rows - STAT_ROWS
    heads = wide // DH
    all_heads = stat_ref.shape[0] // 2
    weights = []
    for h in range(heads):
        tops, totals = [], []
        for s in range(peers):
            stats = got_ref[s, rows:, :].astype(F32)
            at = 5 * h
            tops.append(stats[at : at + 1] + stats[at + 1 : at + 2] + stats[at + 2 : at + 3])
            totals.append(stats[at + 3 : at + 4] + stats[at + 4 : at + 5])
        tops.append(stat_ref[first + h : first + h + 1, :])
        totals.append(stat_ref[all_heads + first + h : all_heads + first + h + 1, :])
        top = functools.reduce(jnp.maximum, tops)
        factors = [jnp.exp(t - top) for t in tops]
        total = sum(f * t for f, t in zip(factors, totals))
        weights += [f / total for f in factors]
    weights.append(jnp.zeros((DH - len(weights), rows), F32))
    weights = jnp.concatenate(weights, axis=0).T
    for h in range(heads):
        lanes = slice(h * DH, (h + 1) * DH)
        at = h * (peers + 1)
        total = weights[:, at + peers : at + peers + 1] * near_ref[:, lanes]
        for s in range(peers):
            total += weights[:, at + s : at + s + 1] * got_ref[s, :rows, lanes].astype(F32)
        out_ref[:, lanes] = total.astype(BF)


def merge(part, got, near, stat):
    peers, rows, wide = got.shape
    rows = rows - STAT_ROWS
    return pl.pallas_call(
        functools.partial(merge_kernel, part * (wide // DH)),
        grid=(1,),
        in_specs=[
            whole(got.shape),
            pl.BlockSpec((rows, wide), lambda i: (0, part)),
            whole(stat.shape),
        ],
        out_specs=whole((rows, wide)),
        out_shape=jax.ShapeDtypeStruct((rows, wide), BF),
        compiler_params=params(),
        cost_estimate=pl.CostEstimate(
            flops=2 * peers * rows * wide, transcendentals=0, bytes_accessed=2 << 20
        ),
        name="merge",
    )(got, near, stat)


def project_kernel(
    where_ref, drop_ref, mine_ref, other_ref, w_ref, res_ref, sum_ref, stat_ref, acc_ref
):
    step = pl.program_id(0)
    half = mine_ref.shape[0]
    lhs = jnp.where(step < half, 0, 1)

    @pl.when(step == 0)
    def _():
        acc_ref[...] = jnp.zeros_like(acc_ref)

    def add(ref, at):
        acc_ref[...] += lax.dot_general(
            ref[at], w_ref[0], (((1,), (1,)), ((), ())), preferred_element_type=F32
        )

    @pl.when(lhs == 0)
    def _():
        add(mine_ref, step)

    @pl.when(lhs == 1)
    def _():
        add(other_ref, step - half)

    @pl.when(step == pl.num_programs(0) - 1)
    def _():
        cols = acc_ref.shape[1]
        blocks = acc_ref.shape[0] // BLOCK
        seed = where_ref[1] * 1000003 + where_ref[2] * cols
        inner = lax.broadcasted_iota(jnp.int32, (BLOCK, cols), 0) * D
        inner = inner + lax.broadcasted_iota(jnp.int32, (BLOCK, cols), 1) + seed
        lane = lax.broadcasted_iota(jnp.int32, (BLOCK, DH), 1)
        for b in range(blocks):
            rows = slice(b * BLOCK, (b + 1) * BLOCK)
            hashed = inner + drop_ref[b]
            for _ in range(2):
                hashed = hashed ^ lax.shift_right_logical(hashed, jnp.int32(16))
                hashed = hashed * 73244475
            hashed = hashed ^ lax.shift_right_logical(hashed, jnp.int32(16))
            kept = (hashed & 1023) >= 102
            keep = jnp.where(kept, jnp.float32(1024.0 / 922.0), jnp.float32(0.0))
            total = res_ref[rows, :].astype(F32) + keep * acc_ref[rows, :]
            sum_ref[rows, :] = total
            mean = jnp.sum(total, axis=1, keepdims=True) * jnp.float32(1.0 / cols)
            dev = total - mean
            spread = jnp.sum(dev * dev, axis=1, keepdims=True)
            stat_ref[rows, :] = jnp.where(lane == 0, mean, spread)


def project(where, drops, mine, other, weight, residual):
    rows, cols = residual.shape
    half = mine.shape[0]
    steps = 2 * half

    def w_map(i, where_ref, drop_ref):
        core = where_ref[0]
        own = 2 * i + core
        far = 2 * (i - half) + (1 - core)
        return (jnp.where(i < half, own, far), 0, 0)

    return pl.pallas_call(
        project_kernel,
        grid_spec=pltpu.PrefetchScalarGridSpec(
            num_scalar_prefetch=2,
            grid=(steps,),
            in_specs=[
                whole(mine.shape),
                whole(other.shape),
                pl.BlockSpec((1,) + weight.shape[1:], w_map),
                whole(residual.shape),
            ],
            out_specs=[whole((rows, cols)), whole((rows, DH))],
            scratch_shapes=[pltpu.VMEM((rows, cols), F32)],
        ),
        out_shape=[
            jax.ShapeDtypeStruct((rows, cols), F32),
            jax.ShapeDtypeStruct((rows, DH), F32),
        ],
        compiler_params=params(),
        cost_estimate=pl.CostEstimate(
            flops=2 * rows * D * cols, transcendentals=0, bytes_accessed=8 << 20
        ),
        name="project",
    )(where, drops, mine, other, weight, residual)


def on_device(
    queries,
    key_rows,
    value_rows,
    residual,
    out_weight,
    norm_gain,
    norm_bias,
    global_list,
    random_device,
    random_offset,
    drop_seed,
    drop_offsets,
):
    row_count, width_here = queries.shape
    block_count = row_count // BLOCK
    n_y, n_x, n_zh = (lax.axis_size(a) for a in SEQ)
    plane = n_x * n_zh
    seq_count = n_y * plane
    n_zl = lax.axis_size("zl")
    tp_count = n_zl * lax.axis_size("core")
    tp_at = lax.axis_index(TP)
    cols_here = out_weight.shape[1]

    plane_at = lax.axis_index(PLANE)
    y_at = lax.axis_index("y")
    zh_at = lax.axis_index("zh")
    wide = width_here // PARTS

    def cut(x, part):
        return x[:, part * wide : (part + 1) * wide]

    pools = []
    for part in range(PARTS):
        paired = jnp.concatenate([cut(key_rows, part), cut(value_rows, part)], axis=1)
        pools.append(lax.all_gather(paired, "y", axis=0, tiled=True))

    def moves(flip):
        return [
            ((y * plane + p) * tp_count + t, (t * plane + (p ^ flip)) * tp_count + y)
            for y in range(n_y)
            for p in range(plane)
            for t in range(tp_count)
        ]

    same_zh = lax.ppermute(out_weight.T, SEQ + TP, moves(0))
    other_zh = lax.ppermute(out_weight.T, SEQ + TP, moves(1))
    shards = jnp.concatenate(
        [
            jnp.where(zh_at == 0, same_zh, other_zh),
            jnp.where(zh_at == 0, other_zh, same_zh),
        ],
        axis=0,
    )
    shards = jnp.concatenate([shards[:, :wide], shards[:, wide:]], axis=0)

    request_count = block_count * RAND
    target = random_device.reshape(request_count)
    wanted = random_offset.reshape(request_count)
    rank = jnp.arange(request_count, dtype=jnp.int32)
    same = target[:, None] == target[None, :]
    earlier = rank[None, :] < rank[:, None]
    slot = jnp.sum(jnp.logical_and(same, earlier), axis=1).astype(jnp.int32)
    slots = n_y * CAP
    place = (target // plane) * CAP + slot
    column = target % plane
    entry = column * (2 * slots) + place
    cells = jnp.arange(plane * 2 * slots, dtype=jnp.int32)
    is_offset = entry[:, None] == cells[None, :]
    is_asker = entry[:, None] + slots == cells[None, :]
    asker = rank // RAND + 1
    table = jnp.sum(
        jnp.where(is_offset, wanted[:, None], jnp.where(is_asker, asker[:, None], 0)), axis=0
    )
    table = jnp.pad(table.astype(BF)[None], ((0, 7), (0, 0)))

    flip = [(0, 1), (1, 0)]
    asked = []
    for part in range(PARTS):
        mine = cut(queries, part)
        if part == 0:
            mine = jnp.concatenate([mine, table], axis=0)
        both = jnp.stack([mine, lax.ppermute(mine, "zh", flip)])
        if part == PARTS - 1:
            both = jnp.concatenate([both, shards[None]], axis=0)
        both = jnp.broadcast_to(both[None], (n_x,) + both.shape)
        asked.append(lax.all_to_all(both, "x", split_axis=0, concat_axis=0, tiled=True))
    shards = asked[-1][:, 2]
    shards = jnp.concatenate(
        [shards[:, : shards.shape[1] // 2], shards[:, shards.shape[1] // 2 :]], axis=2
    )
    weight = lax.all_gather(
        shards.reshape(plane * cols_here, width_here), "y", axis=0, tiled=True
    )
    weight = weight.reshape(tp_count, plane * cols_here, width_here)

    lists = asked[0][:, :, row_count].reshape(plane, plane, 2 * slots)
    lists = lax.dynamic_index_in_dim(lists, plane_at, 1, keepdims=False).astype(jnp.int32)
    base = (jnp.arange(slots, dtype=jnp.int32) // CAP) * block_count
    order = jnp.arange(plane, dtype=jnp.int32)
    peer = jnp.bitwise_xor(order, zh_at)
    nothing = jnp.int32(block_count)
    owner = global_list // block_count
    glob_row = (owner // plane) * block_count + global_list % block_count
    glob_mark = jnp.where(owner % plane == plane_at, -1, nothing)
    here = y_at * plane + peer
    low = (here + seq_count - 1) % seq_count
    high = (here + 1) % seq_count
    low_row = (low // plane) * block_count + block_count - 1
    high_row = (high // plane) * block_count
    low_mark = jnp.where(low % plane == plane_at, 0, nothing)
    high_mark = jnp.where(high % plane == plane_at, block_count - 1, nothing)
    marks = lists[:, slots:] - 1
    row = jnp.concatenate(
        [
            lists[:, :slots] + base[None],
            jnp.broadcast_to(glob_row[None], (plane, GLOB)),
            low_row[:, None],
            high_row[:, None],
        ],
        axis=1,
    ).reshape(-1)
    mark = jnp.concatenate(
        [
            jnp.where(marks < 0, nothing, marks),
            jnp.broadcast_to(glob_mark[None], (plane, GLOB)),
            low_mark[:, None],
            high_mark[:, None],
        ],
        axis=1,
    ).reshape(-1)
    zh = zh_at[None].astype(jnp.int32)

    near, stat = local(queries, key_rows, value_rows)
    context = []
    for part in range(PARTS):
        partials = serve(row, mark, zh, asked[part], pools[part], row_count)
        got = lax.all_to_all(partials, PLANE, split_axis=0, concat_axis=0, tiled=True)
        context.append(merge(part, got, near, stat))
    context = jnp.concatenate(context, axis=1)

    mine = lax.all_to_all(
        jnp.broadcast_to(context[None], (n_zl,) + context.shape),
        "zl",
        split_axis=0,
        concat_axis=0,
        tiled=True,
    )
    other = lax.ppermute(mine, "core", [(0, 1), (1, 0)])

    where = jnp.stack([tp_at % 2, drop_seed[0], tp_at]).astype(jnp.int32)
    summed, stats = project(where, drop_offsets, mine, other, weight, residual)

    stats = jnp.broadcast_to(stats[:, :2].T[None], (tp_count, 2, row_count))
    stats = lax.all_to_all(stats, TP, split_axis=0, concat_axis=0, tiled=True)
    means, spreads = stats[:, 0], stats[:, 1]
    mean = jnp.sum(means, axis=0) / tp_count
    away = means - mean[None]
    cols = summed.shape[1]
    spread = jnp.sum(spreads, axis=0) + cols * jnp.sum(away * away, axis=0)
    factor = lax.rsqrt(spread / D + 1e-05)
    encoded = (summed - mean[:, None]) * factor[:, None] * norm_gain[None] + norm_bias[None]
    return encoded.astype(BF)


def solution(mesh):
    fine = Mesh(mesh.devices.reshape(8, 4, 2, 4, 2), SEQ + TP)
    placed = (
        P(SEQ, TP),
        P(SEQ, TP),
        P(SEQ, TP),
        P(SEQ, TP),
        P(TP, SEQ),
        P(TP),
        P(TP),
        P(),
        P(SEQ, None),
        P(SEQ, None),
        P(),
        P(SEQ),
    )
    return jax.shard_map(
        on_device, mesh=fine, in_specs=placed, out_specs=P(SEQ, TP), check_vma=False
    )
```

```python
import functools

import jax
import jax.numpy as jnp
from jax import lax
from jax.experimental import pallas as pl
from jax.experimental.pallas import tpu as pltpu
from jax.sharding import Mesh
from jax.sharding import PartitionSpec as P

D = 4096
DH = 128
BLOCK = 16
GLOB = 2
RAND = 3
CAP = 2
BF = jnp.bfloat16
F32 = jnp.float32
SEQ = ("y", "x", "zh")
TP = ("zl", "core")
PLANE = ("x", "zh")
PARTS = 2
STAT_ROWS = 16
NEG = -1e30
VMEM_LIMIT = 48 * 1024 * 1024


def whole(shape):
    return pl.BlockSpec(shape, lambda *a: (0,) * len(shape))


def params():
    return pltpu.CompilerParams(vmem_limit_bytes=VMEM_LIMIT)


def partial(scores, listed, values):
    scores = jnp.where(listed, scores, NEG)
    top = jnp.max(scores, axis=0, keepdims=True)
    expo = jnp.where(listed, jnp.exp(scores - top), 0.0)
    total = jnp.sum(expo, axis=0, keepdims=True)
    got = lax.dot_general(
        expo.astype(BF), values, (((0,), (0,)), ((), ())), preferred_element_type=F32
    )
    return top, total, got


def dot_t(a, b):
    return lax.dot_general(a, b, (((1,), (1,)), ((), ())), preferred_element_type=F32)


def split(x, parts):
    out = []
    for _ in range(parts):
        out.append(x.astype(BF))
        x = x - out[-1].astype(F32)
    return out


def serve_kernel(row_ref, mark_ref, zh_ref, q_ref, key_ref, value_ref, out_ref):
    peer = pl.program_id(0)
    rows = q_ref.shape[2]
    wide = q_ref.shape[3]
    listings = row_ref.shape[0] // pl.num_programs(0)
    scale = jnp.float32(1.0 / DH**0.5)
    block_of = lax.broadcasted_iota(jnp.int32, (BLOCK, rows), 1) // BLOCK
    places, listed = [], []
    for i in range(listings):
        at = peer * listings + i
        places.append(pl.ds(pl.multiple_of(row_ref[at] * BLOCK, BLOCK), BLOCK))
        mark = mark_ref[at]
        listed.append(jnp.logical_or(block_of == mark, jnp.full(block_of.shape, mark) < 0))
    listed = jnp.concatenate(listed, axis=0)
    stats = []
    for h in range(wide // DH):
        lanes = slice(h * DH, (h + 1) * DH)
        keys = jnp.concatenate([key_ref[p, lanes] for p in places], axis=0)
        values = jnp.concatenate([value_ref[p, lanes] for p in places], axis=0)
        top, total, got = partial(
            dot_t(keys, q_ref[0, 0, :, lanes]) * scale, listed, values
        )
        out_ref[0, :rows, lanes] = got.astype(BF)
        stats += split(top, 3) + split(total, 2)
    stats.append(jnp.zeros((STAT_ROWS - len(stats), rows), BF))
    out_ref[0, rows:, :] = jnp.concatenate([x.astype(F32) for x in stats], axis=0).astype(BF)


def serve(part, row, mark, zh, q, pool, out_rows):
    n_x = q.shape[0]
    wide = q.shape[3] // PARTS
    rows = out_rows
    peers = 2 * n_x
    out = (peers, rows + STAT_ROWS, wide)
    return pl.pallas_call(
        serve_kernel,
        grid_spec=pltpu.PrefetchScalarGridSpec(
            num_scalar_prefetch=3,
            grid=(peers,),
            in_specs=[
                pl.BlockSpec((1, 1, rows, wide), lambda i, a, b, c: (i // 2, i % 2, 0, part)),
                pl.BlockSpec((pool.shape[0], wide), lambda i, a, b, c: (0, part)),
                pl.BlockSpec((pool.shape[0], wide), lambda i, a, b, c: (0, PARTS + part)),
            ],
            out_specs=pl.BlockSpec(
                (1,) + out[1:], lambda i, a, b, zh_ref: (2 * (i // 2) + (i % 2 + zh_ref[0]) % 2, 0, 0)
            ),
        ),
        out_shape=jax.ShapeDtypeStruct(out, BF),
        compiler_params=params(),
        cost_estimate=pl.CostEstimate(
            flops=4 * peers * rows * 320 * wide,
            transcendentals=peers * rows * 320 * wide // DH,
            bytes_accessed=4 << 20,
        ),
        name="serve",
    )(row, mark, zh, q, pool, pool)


def local_kernel(q_ref, k_ref, v_ref, out_ref, stat_ref):
    rows = q_ref.shape[0]
    heads = q_ref.shape[1] // DH
    scale = jnp.float32(1.0 / DH**0.5)
    key_block = lax.broadcasted_iota(jnp.int32, (rows, rows), 0) // BLOCK
    query_block = lax.broadcasted_iota(jnp.int32, (rows, rows), 1) // BLOCK
    listed = jnp.abs(key_block - query_block) <= 1
    tops, totals = [], []
    for h in range(heads):
        lanes = slice(h * DH, (h + 1) * DH)
        top, total, got = partial(
            dot_t(k_ref[:, lanes], q_ref[:, lanes]) * scale, listed, v_ref[:, lanes]
        )
        out_ref[:, lanes] = got
        tops.append(top)
        totals.append(total)
    stat_ref[...] = jnp.concatenate(tops + totals, axis=0)


def local(q, k, v):
    rows, width = q.shape
    stat = (2 * (width // DH), rows)
    return pl.pallas_call(
        local_kernel,
        grid=(1,),
        in_specs=[whole(q.shape)] * 3,
        out_specs=[whole(q.shape), whole(stat)],
        out_shape=[jax.ShapeDtypeStruct(q.shape, F32), jax.ShapeDtypeStruct(stat, F32)],
        compiler_params=params(),
        cost_estimate=pl.CostEstimate(
            flops=4 * rows * rows * width,
            transcendentals=rows * rows * width // DH,
            bytes_accessed=2 << 20,
        ),
        name="local",
    )(q, k, v)


def stats_of(block, rows, h):
    stats = block[rows:, :].astype(F32)
    at = 5 * h
    top = stats[at : at + 1] + stats[at + 1 : at + 2] + stats[at + 2 : at + 3]
    return top, stats[at + 3 : at + 4] + stats[at + 4 : at + 5]


def columns(lines):
    rows = lines[0].shape[1]
    lines = lines + [jnp.zeros((DH - len(lines), rows), F32)]
    return jnp.concatenate(lines, axis=0).T


def fold_kernel(zh_ref, got_ref, out_ref):
    peers, _, rows, wide = got_ref.shape
    rows = rows - STAT_ROWS
    heads = wide // DH
    factors, stats = [], []
    for h in range(heads):
        pairs = [stats_of(got_ref[s, 0], rows, h) for s in range(peers)]
        top = functools.reduce(jnp.maximum, [t for t, _ in pairs])
        factor = [jnp.exp(t - top) for t, _ in pairs]
        total = sum(f * l for f, (_, l) in zip(factor, pairs))
        factors += factor
        stats += split(top, 3) + split(total, 2)
    stats.append(jnp.zeros((STAT_ROWS - len(stats), rows), BF))
    out_ref[rows:, :] = jnp.concatenate([x.astype(F32) for x in stats], axis=0).astype(BF)
    factors = columns(factors)
    for h in range(heads):
        lanes = slice(h * DH, (h + 1) * DH)
        out_ref[:rows, lanes] = sum(
            factors[:, h * peers + s : h * peers + s + 1] * got_ref[s, 0, :rows, lanes].astype(F32)
            for s in range(peers)
        ).astype(BF)


def fold(zh, got):
    peers, _, rows, wide = got.shape
    return pl.pallas_call(
        fold_kernel,
        grid_spec=pltpu.PrefetchScalarGridSpec(
            num_scalar_prefetch=1,
            grid=(1,),
            in_specs=[
                pl.BlockSpec((peers, 1, rows, wide), lambda i, zh_ref: (0, 1 - zh_ref[0], 0, 0))
            ],
            out_specs=whole((rows, wide)),
        ),
        out_shape=jax.ShapeDtypeStruct((rows, wide), BF),
        compiler_params=params(),
        cost_estimate=pl.CostEstimate(
            flops=2 * peers * rows * wide, transcendentals=0, bytes_accessed=1 << 20
        ),
        name="fold",
    )(zh, got)


def merge_kernel(first, zh_ref, got_ref, far_ref, near_ref, stat_ref, out_ref):
    peers, _, rows, wide = got_ref.shape
    rows = rows - STAT_ROWS
    heads = wide // DH
    all_heads = stat_ref.shape[0] // 2
    weights = []
    for h in range(heads):
        pairs = [stats_of(got_ref[s, 0], rows, h) for s in range(peers)]
        pairs.append(stats_of(far_ref[...], rows, h))
        at = first + h
        pairs.append((stat_ref[at : at + 1, :], stat_ref[all_heads + at : all_heads + at + 1, :]))
        top = functools.reduce(jnp.maximum, [t for t, _ in pairs])
        factors = [jnp.exp(t - top) for t, _ in pairs]
        total = sum(f * l for f, (_, l) in zip(factors, pairs))
        weights += [f / total for f in factors]
    weights = columns(weights)
    for h in range(heads):
        lanes = slice(h * DH, (h + 1) * DH)
        at = h * (peers + 2)
        total = weights[:, at + peers + 1 : at + peers + 2] * near_ref[:, lanes]
        total += weights[:, at + peers : at + peers + 1] * far_ref[:rows, lanes].astype(F32)
        for s in range(peers):
            total += weights[:, at + s : at + s + 1] * got_ref[s, 0, :rows, lanes].astype(F32)
        out_ref[:, lanes] = total.astype(BF)


def merge(part, zh, got, far, near, stat):
    peers, _, rows, wide = got.shape
    out = (rows - STAT_ROWS, wide)
    return pl.pallas_call(
        functools.partial(merge_kernel, part * (wide // DH)),
        grid_spec=pltpu.PrefetchScalarGridSpec(
            num_scalar_prefetch=1,
            grid=(1,),
            in_specs=[
                pl.BlockSpec((peers, 1, rows, wide), lambda i, zh_ref: (0, zh_ref[0], 0, 0)),
                whole(far.shape),
                pl.BlockSpec(out, lambda i, zh_ref: (0, part)),
                whole(stat.shape),
            ],
            out_specs=whole(out),
        ),
        out_shape=jax.ShapeDtypeStruct(out, BF),
        compiler_params=params(),
        cost_estimate=pl.CostEstimate(
            flops=2 * peers * rows * wide, transcendentals=0, bytes_accessed=1 << 20
        ),
        name="merge",
    )(zh, got, far, near, stat)


def keep_kernel(where_ref, drop_ref, out_ref):
    rows, cols = out_ref.shape
    seed = where_ref[1] * 1000003 + where_ref[2] * cols
    inner = lax.broadcasted_iota(jnp.int32, (BLOCK, cols), 0) * D
    inner = inner + lax.broadcasted_iota(jnp.int32, (BLOCK, cols), 1) + seed
    for b in range(rows // BLOCK):
        hashed = inner + drop_ref[b]
        for _ in range(2):
            hashed = hashed ^ lax.shift_right_logical(hashed, jnp.int32(16))
            hashed = hashed * 73244475
        hashed = hashed ^ lax.shift_right_logical(hashed, jnp.int32(16))
        kept = (hashed & 1023) >= 102
        out_ref[b * BLOCK : (b + 1) * BLOCK, :] = jnp.where(
            kept, jnp.float32(1024.0 / 922.0), jnp.float32(0.0)
        )


def keep(where, drops, shape):
    return pl.pallas_call(
        keep_kernel,
        grid_spec=pltpu.PrefetchScalarGridSpec(
            num_scalar_prefetch=2, grid=(1,), in_specs=[], out_specs=whole(shape)
        ),
        out_shape=jax.ShapeDtypeStruct(shape, F32),
        compiler_params=params(),
        cost_estimate=pl.CostEstimate(
            flops=20 * shape[0] * shape[1], transcendentals=0, bytes_accessed=1 << 19
        ),
        name="keep",
    )(where, drops)


def project_kernel(shifts, last, where_ref, *refs):
    count = len(shifts)
    contexts, w_ref = refs[:count], refs[count]
    rest = refs[count + 1 :]
    acc_ref = rest[-1]
    step = pl.program_id(0)
    half = contexts[0].shape[0]

    @pl.when(step == 0)
    def _():
        acc_ref[...] = jnp.zeros_like(acc_ref) if rest[0] is acc_ref else rest[0][...]

    for i, ref in enumerate(contexts):

        @pl.when(step // half == i)
        def _():
            acc_ref[...] += dot_t(ref[step % half], w_ref[0])

    if last:
        _, keep_ref, res_ref, sum_ref, stat_ref, _ = rest

        @pl.when(step == pl.num_programs(0) - 1)
        def _():
            cols = acc_ref.shape[1]
            total = res_ref[...].astype(F32) + keep_ref[...] * acc_ref[...]
            sum_ref[...] = total
            mean = jnp.sum(total, axis=1, keepdims=True) * jnp.float32(1.0 / cols)
            dev = total - mean
            spread = jnp.sum(dev * dev, axis=1, keepdims=True)
            lane = lax.broadcasted_iota(jnp.int32, stat_ref.shape, 1)
            stat_ref[...] = jnp.where(lane == 0, mean, spread)


def project(part, shifts, where, contexts, weight, before=None, finish=None):
    half, rows, wide = contexts[0].shape
    cols = weight.shape[1]
    out = (rows, cols)

    def w_map(i, where_ref):
        core = where_ref[0]
        parity = jnp.int32(0)
        for at, shift in enumerate(shifts):
            parity = jnp.where(i // half == at, (core + shift) % 2, parity)
        return (2 * (i % half) + parity, 0, part)

    args = list(contexts) + [weight]
    specs = [whole(c.shape) for c in contexts] + [pl.BlockSpec((1, cols, wide), w_map)]
    scratch, out_specs, out_shape = [], [whole(out)], [jax.ShapeDtypeStruct(out, F32)]
    if before is not None:
        args.append(before)
        specs.append(whole(out))
    if finish is not None:
        args += list(finish)
        specs += [whole(x.shape) for x in finish]
        out_specs.append(whole((rows, DH)))
        out_shape.append(jax.ShapeDtypeStruct((rows, DH), F32))
        scratch.append(pltpu.VMEM(out, F32))
    steps = half * len(contexts)
    return pl.pallas_call(
        functools.partial(project_kernel, shifts, finish is not None),
        grid_spec=pltpu.PrefetchScalarGridSpec(
            num_scalar_prefetch=1,
            grid=(steps,),
            in_specs=specs,
            out_specs=out_specs,
            scratch_shapes=scratch,
        ),
        out_shape=out_shape,
        compiler_params=params(),
        cost_estimate=pl.CostEstimate(
            flops=2 * rows * steps * wide * cols, transcendentals=0, bytes_accessed=2 << 20
        ),
        name="project",
    )(where, *args)


def on_device(
    queries,
    key_rows,
    value_rows,
    residual,
    out_weight,
    norm_gain,
    norm_bias,
    global_list,
    random_device,
    random_offset,
    drop_seed,
    drop_offsets,
):
    row_count, width_here = queries.shape
    block_count = row_count // BLOCK
    n_y, n_x, n_zh = (lax.axis_size(a) for a in SEQ)
    plane = n_x * n_zh
    seq_count = n_y * plane
    n_zl = lax.axis_size("zl")
    tp_count = n_zl * lax.axis_size("core")
    tp_at = lax.axis_index(TP)
    cols_here = out_weight.shape[1]

    plane_at = lax.axis_index(PLANE)
    y_at = lax.axis_index("y")
    zh_at = lax.axis_index("zh")
    wide = width_here // PARTS

    paired = jnp.concatenate([key_rows, value_rows], axis=1)
    pool = lax.all_gather(paired, "y", axis=0, tiled=True)

    def moves(flip):
        return [
            ((y * plane + p) * tp_count + t, (t * plane + (p ^ flip)) * tp_count + y)
            for y in range(n_y)
            for p in range(plane)
            for t in range(tp_count)
        ]

    same_zh = lax.ppermute(out_weight.T, SEQ + TP, moves(0))
    other_zh = lax.ppermute(out_weight.T, SEQ + TP, moves(1))
    shards = jnp.concatenate(
        [
            jnp.where(zh_at == 0, same_zh, other_zh),
            jnp.where(zh_at == 0, other_zh, same_zh),
        ],
        axis=0,
    )

    request_count = block_count * RAND
    target = random_device.reshape(request_count)
    wanted = random_offset.reshape(request_count)
    rank = jnp.arange(request_count, dtype=jnp.int32)
    same = target[:, None] == target[None, :]
    earlier = rank[None, :] < rank[:, None]
    slot = jnp.sum(jnp.logical_and(same, earlier), axis=1).astype(jnp.int32)
    slots = n_y * CAP
    place = (target // plane) * CAP + slot
    column = target % plane
    entry = column * (2 * slots) + place
    cells = jnp.arange(plane * 2 * slots, dtype=jnp.int32)
    is_offset = entry[:, None] == cells[None, :]
    is_asker = entry[:, None] + slots == cells[None, :]
    asker = rank // RAND + 1
    table = jnp.sum(
        jnp.where(is_offset, wanted[:, None], jnp.where(is_asker, asker[:, None], 0)), axis=0
    )
    table = jnp.pad(table.astype(BF)[None], ((0, 7), (0, width_here - cells.shape[0])))

    flip = [(0, 1), (1, 0)]

    def over_x(x):
        x = jnp.broadcast_to(x[None], (n_x,) + x.shape)
        return lax.all_to_all(x, "x", split_axis=0, concat_axis=0, tiled=True)

    asking = jnp.concatenate([queries, table], axis=0)
    asked = over_x(jnp.stack([asking, lax.ppermute(asking, "zh", flip)]))
    shards = over_x(shards)
    weight = lax.all_gather(
        shards.reshape(plane * cols_here, width_here), "y", axis=0, tiled=True
    )
    weight = weight.reshape(tp_count, plane * cols_here, width_here)

    lists = asked[:, :, row_count, : cells.shape[0]].reshape(plane, plane, 2 * slots)
    lists = lax.dynamic_index_in_dim(lists, plane_at, 1, keepdims=False).astype(jnp.int32)
    base = (jnp.arange(slots, dtype=jnp.int32) // CAP) * block_count
    order = jnp.arange(plane, dtype=jnp.int32)
    peer = jnp.bitwise_xor(order, zh_at)
    nothing = jnp.int32(block_count)
    owner = global_list // block_count
    glob_row = (owner // plane) * block_count + global_list % block_count
    glob_mark = jnp.where(owner % plane == plane_at, -1, nothing)
    here = y_at * plane + peer
    low = (here + seq_count - 1) % seq_count
    high = (here + 1) % seq_count
    low_row = (low // plane) * block_count + block_count - 1
    high_row = (high // plane) * block_count
    low_mark = jnp.where(low % plane == plane_at, 0, nothing)
    high_mark = jnp.where(high % plane == plane_at, block_count - 1, nothing)
    marks = lists[:, slots:] - 1
    row = jnp.concatenate(
        [
            lists[:, :slots] + base[None],
            jnp.broadcast_to(glob_row[None], (plane, GLOB)),
            low_row[:, None],
            high_row[:, None],
        ],
        axis=1,
    ).reshape(-1)
    mark = jnp.concatenate(
        [
            jnp.where(marks < 0, nothing, marks),
            jnp.broadcast_to(glob_mark[None], (plane, GLOB)),
            low_mark[:, None],
            high_mark[:, None],
        ],
        axis=1,
    ).reshape(-1)
    zh = zh_at[None].astype(jnp.int32)

    near, stat = local(queries, key_rows, value_rows)
    where = jnp.stack([tp_at % 2, drop_seed[0], tp_at]).astype(jnp.int32)
    kept = keep(where, drop_offsets, residual.shape)
    folded = []
    for part in range(PARTS):
        partials = serve(part, row, mark, zh, asked, pool, row_count)
        partials = partials.reshape((n_x, 2) + partials.shape[1:])
        got = lax.all_to_all(partials, "x", split_axis=0, concat_axis=0, tiled=True)
        folded.append((got, lax.ppermute(fold(zh, got), "zh", flip)))
    mine, other = [], []
    for part in range(PARTS):
        context = merge(part, zh, *folded[part], near, stat)
        context = jnp.broadcast_to(context[None], (n_zl,) + context.shape)
        mine.append(lax.all_to_all(context, "zl", split_axis=0, concat_axis=0, tiled=True))
        other.append(lax.ppermute(mine[part], "core", flip))
    (acc,) = project(0, (0, 1), where, (mine[0], other[0]), weight)
    (acc,) = project(1, (0,), where, (mine[1],), weight, before=acc)
    summed, stats = project(
        1, (1,), where, (other[1],), weight, before=acc, finish=(kept, residual)
    )

    stats = jnp.broadcast_to(stats[:, :2].T[None], (tp_count, 2, row_count))
    stats = lax.all_to_all(stats, TP, split_axis=0, concat_axis=0, tiled=True)
    means, spreads = stats[:, 0], stats[:, 1]
    mean = jnp.sum(means, axis=0) / tp_count
    away = means - mean[None]
    cols = summed.shape[1]
    spread = jnp.sum(spreads, axis=0) + cols * jnp.sum(away * away, axis=0)
    factor = lax.rsqrt(spread / D + 1e-05)
    encoded = (summed - mean[:, None]) * factor[:, None] * norm_gain[None] + norm_bias[None]
    return encoded.astype(BF)


def solution(mesh):
    fine = Mesh(mesh.devices.reshape(8, 4, 2, 4, 2), SEQ + TP)
    placed = (
        P(SEQ, TP),
        P(SEQ, TP),
        P(SEQ, TP),
        P(SEQ, TP),
        P(TP, SEQ),
        P(TP),
        P(TP),
        P(),
        P(SEQ, None),
        P(SEQ, None),
        P(),
        P(SEQ),
    )
    return jax.shard_map(
        on_device, mesh=fine, in_specs=placed, out_specs=P(SEQ, TP), check_vma=False
    )
```

```python
import functools

import jax
import jax.numpy as jnp
from jax import lax
from jax.experimental import pallas as pl
from jax.experimental.pallas import tpu as pltpu
from jax.sharding import Mesh
from jax.sharding import PartitionSpec as P

D = 4096
DH = 128
BLOCK = 16
GLOB = 2
RAND = 3
CAP = 2
BF = jnp.bfloat16
F32 = jnp.float32
SEQ = ("y", "x", "zh")
TP = ("zl", "core")
PLANE = ("x", "zh")
PARTS = 2
STAT_ROWS = 16
NEG = -1e30
VMEM_LIMIT = 48 * 1024 * 1024


def whole(shape):
    return pl.BlockSpec(shape, lambda *a: (0,) * len(shape))


def params():
    return pltpu.CompilerParams(vmem_limit_bytes=VMEM_LIMIT)


def partial(scores, listed, values):
    scores = jnp.where(listed, scores, NEG)
    top = jnp.max(scores, axis=0, keepdims=True)
    expo = jnp.where(listed, jnp.exp(scores - top), 0.0)
    total = jnp.sum(expo, axis=0, keepdims=True)
    got = lax.dot_general(
        expo.astype(BF), values, (((0,), (0,)), ((), ())), preferred_element_type=F32
    )
    return top, total, got


def dot_t(a, b):
    return lax.dot_general(a, b, (((1,), (1,)), ((), ())), preferred_element_type=F32)


def split(x, parts):
    out = []
    for _ in range(parts):
        out.append(x.astype(BF))
        x = x - out[-1].astype(F32)
    return out


def serve_kernel(row_ref, mark_ref, zh_ref, q_ref, key_ref, value_ref, out_ref):
    peer = pl.program_id(0)
    rows = q_ref.shape[2]
    wide = q_ref.shape[3]
    listings = row_ref.shape[0] // pl.num_programs(0)
    scale = jnp.float32(1.0 / DH**0.5)
    block_of = lax.broadcasted_iota(jnp.int32, (BLOCK, rows), 1) // BLOCK
    places, listed = [], []
    for i in range(listings):
        at = peer * listings + i
        places.append(pl.ds(pl.multiple_of(row_ref[at] * BLOCK, BLOCK), BLOCK))
        mark = mark_ref[at]
        listed.append(jnp.logical_or(block_of == mark, jnp.full(block_of.shape, mark) < 0))
    listed = jnp.concatenate(listed, axis=0)
    stats = []
    for h in range(wide // DH):
        lanes = slice(h * DH, (h + 1) * DH)
        keys = jnp.concatenate([key_ref[p, lanes] for p in places], axis=0)
        values = jnp.concatenate([value_ref[p, lanes] for p in places], axis=0)
        top, total, got = partial(
            dot_t(keys, q_ref[0, 0, :, lanes]) * scale, listed, values
        )
        out_ref[0, :rows, lanes] = got.astype(BF)
        stats += split(top, 3) + split(total, 2)
    stats.append(jnp.zeros((STAT_ROWS - len(stats), rows), BF))
    out_ref[0, rows:, :] = jnp.concatenate([x.astype(F32) for x in stats], axis=0).astype(BF)


def serve(part, row, mark, zh, q, pool, out_rows):
    n_x = q.shape[0]
    wide = q.shape[3] // PARTS
    rows = out_rows
    peers = 2 * n_x
    out = (peers, rows + STAT_ROWS, wide)
    return pl.pallas_call(
        serve_kernel,
        grid_spec=pltpu.PrefetchScalarGridSpec(
            num_scalar_prefetch=3,
            grid=(peers,),
            in_specs=[
                pl.BlockSpec((1, 1, rows, wide), lambda i, a, b, c: (i // 2, i % 2, 0, part)),
                pl.BlockSpec((pool.shape[0], wide), lambda i, a, b, c: (0, part)),
                pl.BlockSpec((pool.shape[0], wide), lambda i, a, b, c: (0, PARTS + part)),
            ],
            out_specs=pl.BlockSpec(
                (1,) + out[1:], lambda i, a, b, zh_ref: (2 * (i // 2) + (i % 2 + zh_ref[0]) % 2, 0, 0)
            ),
        ),
        out_shape=jax.ShapeDtypeStruct(out, BF),
        compiler_params=params(),
        cost_estimate=pl.CostEstimate(
            flops=4 * peers * rows * 320 * wide,
            transcendentals=peers * rows * 320 * wide // DH,
            bytes_accessed=4 << 20,
        ),
        name="serve",
    )(row, mark, zh, q, pool, pool)


def local_kernel(q_ref, k_ref, v_ref, out_ref, stat_ref):
    rows = q_ref.shape[0]
    heads = q_ref.shape[1] // DH
    scale = jnp.float32(1.0 / DH**0.5)
    key_block = lax.broadcasted_iota(jnp.int32, (rows, rows), 0) // BLOCK
    query_block = lax.broadcasted_iota(jnp.int32, (rows, rows), 1) // BLOCK
    listed = jnp.abs(key_block - query_block) <= 1
    tops, totals = [], []
    for h in range(heads):
        lanes = slice(h * DH, (h + 1) * DH)
        top, total, got = partial(
            dot_t(k_ref[:, lanes], q_ref[:, lanes]) * scale, listed, v_ref[:, lanes]
        )
        out_ref[:, lanes] = got
        tops.append(top)
        totals.append(total)
    stat_ref[...] = jnp.concatenate(tops + totals, axis=0)


def local(q, k, v):
    rows, width = q.shape
    stat = (2 * (width // DH), rows)
    return pl.pallas_call(
        local_kernel,
        grid=(1,),
        in_specs=[whole(q.shape)] * 3,
        out_specs=[whole(q.shape), whole(stat)],
        out_shape=[jax.ShapeDtypeStruct(q.shape, F32), jax.ShapeDtypeStruct(stat, F32)],
        compiler_params=params(),
        cost_estimate=pl.CostEstimate(
            flops=4 * rows * rows * width,
            transcendentals=rows * rows * width // DH,
            bytes_accessed=2 << 20,
        ),
        name="local",
    )(q, k, v)


def stats_of(block, rows, h):
    stats = block[rows:, :].astype(F32)
    at = 5 * h
    top = stats[at : at + 1] + stats[at + 1 : at + 2] + stats[at + 2 : at + 3]
    return top, stats[at + 3 : at + 4] + stats[at + 4 : at + 5]


def columns(lines):
    rows = lines[0].shape[1]
    lines = lines + [jnp.zeros((DH - len(lines), rows), F32)]
    return jnp.concatenate(lines, axis=0).T


def fold_kernel(zh_ref, got_ref, _, out_ref):
    peers, _, rows, wide = got_ref.shape
    rows = rows - STAT_ROWS
    heads = wide // DH
    factors, stats = [], []
    for h in range(heads):
        pairs = [stats_of(got_ref[s, 0], rows, h) for s in range(peers)]
        top = functools.reduce(jnp.maximum, [t for t, _ in pairs])
        factor = [jnp.exp(t - top) for t, _ in pairs]
        total = sum(f * l for f, (_, l) in zip(factor, pairs))
        factors += factor
        stats += split(top, 3) + split(total, 2)
    stats.append(jnp.zeros((STAT_ROWS - len(stats), rows), BF))
    out_ref[rows:, :] = jnp.concatenate([x.astype(F32) for x in stats], axis=0).astype(BF)
    factors = columns(factors)
    for h in range(heads):
        lanes = slice(h * DH, (h + 1) * DH)
        out_ref[:rows, lanes] = sum(
            factors[:, h * peers + s : h * peers + s + 1] * got_ref[s, 0, :rows, lanes].astype(F32)
            for s in range(peers)
        ).astype(BF)


def fold(zh, got, after):
    peers, _, rows, wide = got.shape
    return pl.pallas_call(
        fold_kernel,
        grid_spec=pltpu.PrefetchScalarGridSpec(
            num_scalar_prefetch=1,
            grid=(1,),
            in_specs=[
                pl.BlockSpec((peers, 1, rows, wide), lambda i, zh_ref: (0, 1 - zh_ref[0], 0, 0)),
                pl.BlockSpec(memory_space=pl.ANY),
            ],
            out_specs=whole((rows, wide)),
        ),
        out_shape=jax.ShapeDtypeStruct((rows, wide), BF),
        compiler_params=params(),
        cost_estimate=pl.CostEstimate(
            flops=2 * peers * rows * wide, transcendentals=0, bytes_accessed=1 << 20
        ),
        name="fold",
    )(zh, got, after)


def merge_kernel(first, zh_ref, got_ref, far_ref, near_ref, stat_ref, _, out_ref):
    peers, _, rows, wide = got_ref.shape
    rows = rows - STAT_ROWS
    heads = wide // DH
    all_heads = stat_ref.shape[0] // 2
    weights = []
    for h in range(heads):
        pairs = [stats_of(got_ref[s, 0], rows, h) for s in range(peers)]
        pairs.append(stats_of(far_ref[...], rows, h))
        at = first + h
        pairs.append((stat_ref[at : at + 1, :], stat_ref[all_heads + at : all_heads + at + 1, :]))
        top = functools.reduce(jnp.maximum, [t for t, _ in pairs])
        factors = [jnp.exp(t - top) for t, _ in pairs]
        total = sum(f * l for f, (_, l) in zip(factors, pairs))
        weights += [f / total for f in factors]
    weights = columns(weights)
    for h in range(heads):
        lanes = slice(h * DH, (h + 1) * DH)
        at = h * (peers + 2)
        total = weights[:, at + peers + 1 : at + peers + 2] * near_ref[:, lanes]
        total += weights[:, at + peers : at + peers + 1] * far_ref[:rows, lanes].astype(F32)
        for s in range(peers):
            total += weights[:, at + s : at + s + 1] * got_ref[s, 0, :rows, lanes].astype(F32)
        out_ref[:, lanes] = total.astype(BF)


def merge(part, zh, got, far, near, stat, after):
    peers, _, rows, wide = got.shape
    out = (rows - STAT_ROWS, wide)
    return pl.pallas_call(
        functools.partial(merge_kernel, part * (wide // DH)),
        grid_spec=pltpu.PrefetchScalarGridSpec(
            num_scalar_prefetch=1,
            grid=(1,),
            in_specs=[
                pl.BlockSpec((peers, 1, rows, wide), lambda i, zh_ref: (0, zh_ref[0], 0, 0)),
                whole(far.shape),
                pl.BlockSpec(out, lambda i, zh_ref: (0, part)),
                whole(stat.shape),
                pl.BlockSpec(memory_space=pl.ANY),
            ],
            out_specs=whole(out),
        ),
        out_shape=jax.ShapeDtypeStruct(out, BF),
        compiler_params=params(),
        cost_estimate=pl.CostEstimate(
            flops=2 * peers * rows * wide, transcendentals=0, bytes_accessed=1 << 20
        ),
        name="merge",
    )(zh, got, far, near, stat, after)


def keep_kernel(where_ref, drop_ref, out_ref):
    rows, cols = out_ref.shape
    seed = where_ref[1] * 1000003 + where_ref[2] * cols
    inner = lax.broadcasted_iota(jnp.int32, (BLOCK, cols), 0) * D
    inner = inner + lax.broadcasted_iota(jnp.int32, (BLOCK, cols), 1) + seed
    for b in range(rows // BLOCK):
        hashed = inner + drop_ref[b]
        for _ in range(2):
            hashed = hashed ^ lax.shift_right_logical(hashed, jnp.int32(16))
            hashed = hashed * 73244475
        hashed = hashed ^ lax.shift_right_logical(hashed, jnp.int32(16))
        kept = (hashed & 1023) >= 102
        out_ref[b * BLOCK : (b + 1) * BLOCK, :] = jnp.where(
            kept, jnp.float32(1024.0 / 922.0), jnp.float32(0.0)
        )


def keep(where, drops, shape):
    return pl.pallas_call(
        keep_kernel,
        grid_spec=pltpu.PrefetchScalarGridSpec(
            num_scalar_prefetch=2, grid=(1,), in_specs=[], out_specs=whole(shape)
        ),
        out_shape=jax.ShapeDtypeStruct(shape, F32),
        compiler_params=params(),
        cost_estimate=pl.CostEstimate(
            flops=20 * shape[0] * shape[1], transcendentals=0, bytes_accessed=1 << 19
        ),
        name="keep",
    )(where, drops)


def project_kernel(count, last, where_ref, *refs):
    contexts, weights = refs[:count], refs[count : 2 * count]
    rest = refs[2 * count :]
    acc = sum(
        dot_t(c_ref[z], w_ref[z, 0])
        for c_ref, w_ref in zip(contexts, weights)
        for z in range(c_ref.shape[0])
    )
    if len(rest) > 1:
        acc = acc + rest[0][...]
    if not last:
        rest[-1][...] = acc
        return
    _, keep_ref, res_ref, sum_ref, stat_ref = rest
    cols = acc.shape[1]
    total = res_ref[...].astype(F32) + keep_ref[...] * acc
    sum_ref[...] = total
    mean = jnp.sum(total, axis=1, keepdims=True) * jnp.float32(1.0 / cols)
    dev = total - mean
    spread = jnp.sum(dev * dev, axis=1, keepdims=True)
    lane = lax.broadcasted_iota(jnp.int32, stat_ref.shape, 1)
    stat_ref[...] = jnp.where(lane == 0, mean, spread)


def project(part, shifts, where, contexts, weight, before=None, finish=None):
    half, rows, wide = contexts[0].shape
    cols = weight.shape[2]
    out = (rows, cols)
    args = list(contexts) + [weight] * len(contexts)
    specs = [whole(c.shape) for c in contexts] + [
        pl.BlockSpec(
            (half, 1, cols, wide),
            lambda i, where_ref, shift=shift: (0, (where_ref[0] + shift) % 2, 0, part),
        )
        for shift in shifts
    ]
    out_specs, out_shape = [whole(out)], [jax.ShapeDtypeStruct(out, F32)]
    if before is not None:
        args.append(before)
        specs.append(whole(out))
    if finish is not None:
        args += list(finish)
        specs += [whole(x.shape) for x in finish]
        out_specs.append(whole((rows, DH)))
        out_shape.append(jax.ShapeDtypeStruct((rows, DH), F32))
    return pl.pallas_call(
        functools.partial(project_kernel, len(contexts), finish is not None),
        grid_spec=pltpu.PrefetchScalarGridSpec(
            num_scalar_prefetch=1, grid=(1,), in_specs=specs, out_specs=out_specs
        ),
        out_shape=out_shape,
        compiler_params=params(),
        cost_estimate=pl.CostEstimate(
            flops=2 * rows * half * len(contexts) * wide * cols,
            transcendentals=0,
            bytes_accessed=2 << 20,
        ),
        name="project",
    )(where, *args)


def on_device(
    queries,
    key_rows,
    value_rows,
    residual,
    out_weight,
    norm_gain,
    norm_bias,
    global_list,
    random_device,
    random_offset,
    drop_seed,
    drop_offsets,
):
    row_count, width_here = queries.shape
    block_count = row_count // BLOCK
    n_y, n_x, n_zh = (lax.axis_size(a) for a in SEQ)
    plane = n_x * n_zh
    seq_count = n_y * plane
    n_zl = lax.axis_size("zl")
    tp_count = n_zl * lax.axis_size("core")
    tp_at = lax.axis_index(TP)
    cols_here = out_weight.shape[1]

    plane_at = lax.axis_index(PLANE)
    y_at = lax.axis_index("y")
    zh_at = lax.axis_index("zh")
    wide = width_here // PARTS

    paired = jnp.concatenate([key_rows, value_rows], axis=1)
    pool = lax.all_gather(paired, "y", axis=0, tiled=True)

    def moves(flip):
        return [
            ((y * plane + p) * tp_count + t, (t * plane + (p ^ flip)) * tp_count + y)
            for y in range(n_y)
            for p in range(plane)
            for t in range(tp_count)
        ]

    same_zh = lax.ppermute(out_weight.T, SEQ + TP, moves(0))
    other_zh = lax.ppermute(out_weight.T, SEQ + TP, moves(1))
    shards = jnp.concatenate(
        [
            jnp.where(zh_at == 0, same_zh, other_zh),
            jnp.where(zh_at == 0, other_zh, same_zh),
        ],
        axis=0,
    )

    request_count = block_count * RAND
    target = random_device.reshape(request_count)
    wanted = random_offset.reshape(request_count)
    rank = jnp.arange(request_count, dtype=jnp.int32)
    same = target[:, None] == target[None, :]
    earlier = rank[None, :] < rank[:, None]
    slot = jnp.sum(jnp.logical_and(same, earlier), axis=1).astype(jnp.int32)
    slots = n_y * CAP
    place = (target // plane) * CAP + slot
    column = target % plane
    entry = column * (2 * slots) + place
    cells = jnp.arange(plane * 2 * slots, dtype=jnp.int32)
    is_offset = entry[:, None] == cells[None, :]
    is_asker = entry[:, None] + slots == cells[None, :]
    asker = rank // RAND + 1
    table = jnp.sum(
        jnp.where(is_offset, wanted[:, None], jnp.where(is_asker, asker[:, None], 0)), axis=0
    )
    table = jnp.pad(table.astype(BF)[None], ((0, 7), (0, width_here - cells.shape[0])))

    flip = [(0, 1), (1, 0)]

    def over_x(x):
        x = jnp.broadcast_to(x[None], (n_x,) + x.shape)
        return lax.all_to_all(x, "x", split_axis=0, concat_axis=0, tiled=True)

    near_q = jnp.concatenate([queries, table], axis=0)
    far_q = jnp.concatenate(
        [lax.ppermute(queries, "zh", flip), lax.ppermute(table, "zh", flip)], axis=0
    )
    asked = over_x(jnp.stack([near_q, far_q]))
    after = asked[0, 0, row_count, 0] * 0
    shards = over_x(shards + after)
    weight = lax.all_gather(
        shards.reshape(plane * cols_here, width_here), "y", axis=0, tiled=True
    )
    weight = weight.reshape(n_zl, 2, plane * cols_here, width_here)

    lists = asked[:, :, row_count, : cells.shape[0]].reshape(plane, plane, 2 * slots)
    lists = lax.dynamic_index_in_dim(lists, plane_at, 1, keepdims=False).astype(jnp.int32)
    base = (jnp.arange(slots, dtype=jnp.int32) // CAP) * block_count
    order = jnp.arange(plane, dtype=jnp.int32)
    peer = jnp.bitwise_xor(order, zh_at)
    nothing = jnp.int32(block_count)
    owner = global_list // block_count
    glob_row = (owner // plane) * block_count + global_list % block_count
    glob_mark = jnp.where(owner % plane == plane_at, -1, nothing)
    here = y_at * plane + peer
    low = (here + seq_count - 1) % seq_count
    high = (here + 1) % seq_count
    low_row = (low // plane) * block_count + block_count - 1
    high_row = (high // plane) * block_count
    low_mark = jnp.where(low % plane == plane_at, 0, nothing)
    high_mark = jnp.where(high % plane == plane_at, block_count - 1, nothing)
    marks = lists[:, slots:] - 1
    row = jnp.concatenate(
        [
            lists[:, :slots] + base[None],
            jnp.broadcast_to(glob_row[None], (plane, GLOB)),
            low_row[:, None],
            high_row[:, None],
        ],
        axis=1,
    ).reshape(-1)
    mark = jnp.concatenate(
        [
            jnp.where(marks < 0, nothing, marks),
            jnp.broadcast_to(glob_mark[None], (plane, GLOB)),
            low_mark[:, None],
            high_mark[:, None],
        ],
        axis=1,
    ).reshape(-1)
    zh = zh_at[None].astype(jnp.int32)

    near, stat = local(queries, key_rows, value_rows)
    where = jnp.stack([tp_at % 2, drop_seed[0], tp_at]).astype(jnp.int32)
    kept = keep(where, drop_offsets, residual.shape)
    folded = []
    for part in range(PARTS):
        partials = serve(part, row, mark, zh, asked, pool, row_count)
        partials = partials.reshape((n_x, 2) + partials.shape[1:])
        got = lax.all_to_all(partials, "x", split_axis=0, concat_axis=0, tiled=True)
        gone = fold(zh, got, kept)
        folded.append((got, lax.ppermute(gone, "zh", flip)))
    mine, other = [], []
    for part in range(PARTS):
        context = merge(part, zh, *folded[part], near, stat, gone)
        context = jnp.broadcast_to(context[None], (n_zl,) + context.shape)
        mine.append(lax.all_to_all(context, "zl", split_axis=0, concat_axis=0, tiled=True))
        other.append(lax.ppermute(mine[part], "core", flip))
    (acc,) = project(0, (0, 1), where, (mine[0], other[0]), weight)
    (acc,) = project(1, (0,), where, (mine[1],), weight, before=acc)
    summed, stats = project(
        1, (1,), where, (other[1],), weight, before=acc, finish=(kept, residual)
    )

    stats = jnp.broadcast_to(stats[:, :2].T[None], (tp_count, 2, row_count))
    stats = lax.all_to_all(stats, TP, split_axis=0, concat_axis=0, tiled=True)
    means, spreads = stats[:, 0], stats[:, 1]
    mean = jnp.sum(means, axis=0) / tp_count
    away = means - mean[None]
    cols = summed.shape[1]
    spread = jnp.sum(spreads, axis=0) + cols * jnp.sum(away * away, axis=0)
    factor = lax.rsqrt(spread / D + 1e-05)
    encoded = (summed - mean[:, None]) * factor[:, None] * norm_gain[None] + norm_bias[None]
    return encoded.astype(BF)


def solution(mesh):
    fine = Mesh(mesh.devices.reshape(8, 4, 2, 4, 2), SEQ + TP)
    placed = (
        P(SEQ, TP),
        P(SEQ, TP),
        P(SEQ, TP),
        P(SEQ, TP),
        P(TP, SEQ),
        P(TP),
        P(TP),
        P(),
        P(SEQ, None),
        P(SEQ, None),
        P(),
        P(SEQ),
    )
    return jax.shard_map(
        on_device, mesh=fine, in_specs=placed, out_specs=P(SEQ, TP), check_vma=False
    )
```

```python
import functools
import math

import jax
import jax.numpy as jnp
from jax import lax
from jax.experimental import pallas as pl
from jax.experimental.pallas import tpu as pltpu
from jax.sharding import Mesh
from jax.sharding import PartitionSpec as P

D = 4096
DH = 128
BLOCK = 16
GLOB = 2
RAND = 3
CAP = 2
BF = jnp.bfloat16
F32 = jnp.float32
SEQ = ("y", "x", "zh")
TP = ("zl", "core")
PLANE = ("x", "zh")
PARTS = 2
STAT_ROWS = 16
NEG = -1e30
EMPTY = -1e20
VMEM_LIMIT = 48 * 1024 * 1024


def whole(shape):
    return pl.BlockSpec(shape, lambda *a: (0,) * len(shape))


def params(limit=VMEM_LIMIT):
    return pltpu.CompilerParams(vmem_limit_bytes=limit)


def partial(scores, listed, values):
    scores = jnp.where(listed, scores, NEG)
    top = jnp.maximum(jnp.max(scores, axis=0, keepdims=True), EMPTY)
    expo = weight_of(scores, top)
    total = jnp.sum(expo, axis=0, keepdims=True)
    got = lax.dot_general(
        values, expo.astype(BF), (((0,), (0,)), ((), ())), preferred_element_type=F32
    )
    return top, total, got


def weight_of(score, top):
    return jnp.exp2((score - top) * jnp.float32(math.log2(math.e) / DH**0.5))


def dot_t(a, b):
    return lax.dot_general(a, b, (((1,), (1,)), ((), ())), preferred_element_type=F32)


def split(x, parts):
    out = []
    for _ in range(parts):
        out.append(x.astype(BF))
        x = x - out[-1].astype(F32)
    return out


def serve_kernel(row_ref, mark_ref, zh_ref, q_ref, key_ref, value_ref, out_ref):
    peer = pl.program_id(0)
    rows = q_ref.shape[2]
    wide = q_ref.shape[3]
    listings = row_ref.shape[0] // pl.num_programs(0)
    block_of = lax.broadcasted_iota(jnp.int32, (BLOCK, rows), 1) // BLOCK
    places, listed = [], []
    for i in range(listings):
        at = peer * listings + i
        places.append(pl.ds(pl.multiple_of(row_ref[at] * BLOCK, BLOCK), BLOCK))
        mark = mark_ref[at]
        listed.append(jnp.logical_or(block_of == mark, jnp.full(block_of.shape, mark) < 0))
    listed = jnp.concatenate(listed, axis=0)
    stats = []
    for h in range(wide // DH):
        lanes = slice(h * DH, (h + 1) * DH)
        keys = jnp.concatenate([key_ref[p, lanes] for p in places], axis=0)
        values = jnp.concatenate([value_ref[p, lanes] for p in places], axis=0)
        top, total, got = partial(dot_t(keys, q_ref[0, 0, :, lanes]), listed, values)
        out_ref[0, lanes, :] = got.astype(BF)
        stats += split(top, 3) + split(total, 2)
    stats.append(jnp.zeros((STAT_ROWS - len(stats), rows), BF))
    out_ref[0, wide:, :] = jnp.concatenate([x.astype(F32) for x in stats], axis=0).astype(BF)


def serve(part, row, mark, zh, q, pool, out_rows):
    n_x = q.shape[0]
    wide = q.shape[3] // PARTS
    rows = out_rows
    peers = 2 * n_x
    out = (peers, wide + STAT_ROWS, rows)
    return pl.pallas_call(
        serve_kernel,
        grid_spec=pltpu.PrefetchScalarGridSpec(
            num_scalar_prefetch=3,
            grid=(peers,),
            in_specs=[
                pl.BlockSpec((1, 1, rows, wide), lambda i, a, b, c: (i // 2, i % 2, 0, part)),
                pl.BlockSpec((pool.shape[0], wide), lambda i, a, b, c: (0, part)),
                pl.BlockSpec((pool.shape[0], wide), lambda i, a, b, c: (0, PARTS + part)),
            ],
            out_specs=pl.BlockSpec(
                (1,) + out[1:], lambda i, a, b, zh_ref: (2 * (i // 2) + (i % 2 + zh_ref[0]) % 2, 0, 0)
            ),
        ),
        out_shape=jax.ShapeDtypeStruct(out, BF),
        compiler_params=params(),
        cost_estimate=pl.CostEstimate(
            flops=4 * peers * rows * 320 * wide,
            transcendentals=peers * rows * 320 * wide // DH,
            bytes_accessed=4 << 20,
        ),
        name="serve",
    )(row, mark, zh, q, pool, pool)


def local_kernel(q_ref, k_ref, v_ref, out_ref, stat_ref):
    rows = q_ref.shape[0]
    heads = q_ref.shape[1] // DH
    key_block = lax.broadcasted_iota(jnp.int32, (rows, rows), 0) // BLOCK
    query_block = lax.broadcasted_iota(jnp.int32, (rows, rows), 1) // BLOCK
    listed = jnp.abs(key_block - query_block) <= 1
    tops, totals = [], []
    for h in range(heads):
        lanes = slice(h * DH, (h + 1) * DH)
        top, total, got = partial(
            dot_t(k_ref[:, lanes], q_ref[:, lanes]), listed, v_ref[:, lanes]
        )
        out_ref[lanes, :] = got
        tops.append(top)
        totals.append(total)
    stat_ref[...] = jnp.concatenate(tops + totals, axis=0)


def local(part, q, k, v):
    rows = q.shape[0]
    wide = q.shape[1] // PARTS
    stat = (2 * (wide // DH), rows)
    return pl.pallas_call(
        local_kernel,
        grid=(1,),
        in_specs=[pl.BlockSpec((rows, wide), lambda i: (0, part))] * 3,
        out_specs=[whole((wide, rows)), whole(stat)],
        out_shape=[jax.ShapeDtypeStruct((wide, rows), F32), jax.ShapeDtypeStruct(stat, F32)],
        compiler_params=params(),
        cost_estimate=pl.CostEstimate(
            flops=4 * rows * rows * wide,
            transcendentals=rows * rows * wide // DH,
            bytes_accessed=1 << 20,
        ),
        name="local",
    )(q, k, v)


def stats_of(block, wide, h):
    stats = block[wide:, :].astype(F32)
    at = 5 * h
    top = stats[at : at + 1] + stats[at + 1 : at + 2] + stats[at + 2 : at + 3]
    return top, stats[at + 3 : at + 4] + stats[at + 4 : at + 5]


def fold_kernel(zh_ref, got_ref, _, out_ref):
    peers, _, wide, rows = got_ref.shape
    wide = wide - STAT_ROWS
    stats = []
    for h in range(wide // DH):
        lines = slice(h * DH, (h + 1) * DH)
        pairs = [stats_of(got_ref[s, 0], wide, h) for s in range(peers)]
        top = functools.reduce(jnp.maximum, [t for t, _ in pairs])
        factors = [weight_of(t, top) for t, _ in pairs]
        total = sum(f * l for f, (_, l) in zip(factors, pairs))
        stats += split(top, 3) + split(total, 2)
        out_ref[lines, :] = sum(
            f * got_ref[s, 0, lines, :].astype(F32) for s, f in enumerate(factors)
        ).astype(BF)
    stats.append(jnp.zeros((STAT_ROWS - len(stats), rows), BF))
    out_ref[wide:, :] = jnp.concatenate([x.astype(F32) for x in stats], axis=0).astype(BF)


def fold(zh, got, after):
    peers, _, lines, rows = got.shape
    return pl.pallas_call(
        fold_kernel,
        grid_spec=pltpu.PrefetchScalarGridSpec(
            num_scalar_prefetch=1,
            grid=(1,),
            in_specs=[
                pl.BlockSpec((peers, 1, lines, rows), lambda i, zh_ref: (0, 1 - zh_ref[0], 0, 0)),
                pl.BlockSpec((BLOCK, DH), lambda i, zh_ref: (0, 0)),
            ],
            out_specs=whole((lines, rows)),
        ),
        out_shape=jax.ShapeDtypeStruct((lines, rows), BF),
        compiler_params=params(),
        cost_estimate=pl.CostEstimate(
            flops=2 * peers * rows * lines, transcendentals=0, bytes_accessed=1 << 20
        ),
        name="fold",
    )(zh, got, after)


def merge_kernel(zh_ref, got_ref, far_ref, near_ref, stat_ref, _, out_ref):
    peers, _, wide, rows = got_ref.shape
    wide = wide - STAT_ROWS
    heads = wide // DH
    for h in range(heads):
        lines = slice(h * DH, (h + 1) * DH)
        pairs = [stats_of(got_ref[s, 0], wide, h) for s in range(peers)]
        pairs.append(stats_of(far_ref[...], wide, h))
        pairs.append((stat_ref[h : h + 1, :], stat_ref[heads + h : heads + h + 1, :]))
        top = functools.reduce(jnp.maximum, [t for t, _ in pairs])
        factors = [weight_of(t, top) for t, _ in pairs]
        total = sum(f * l for f, (_, l) in zip(factors, pairs))
        factors = [f / total for f in factors]
        context = factors[-1] * near_ref[lines, :]
        context += factors[-2] * far_ref[lines, :].astype(F32)
        for s in range(peers):
            context += factors[s] * got_ref[s, 0, lines, :].astype(F32)
        context = context.T.astype(BF)
        for copy in range(out_ref.shape[0]):
            out_ref[copy, :, lines] = context


def merge(zh, got, far, near, stat, after, copies):
    peers, _, lines, rows = got.shape
    wide = lines - STAT_ROWS
    out = (copies, rows, wide)
    return pl.pallas_call(
        merge_kernel,
        grid_spec=pltpu.PrefetchScalarGridSpec(
            num_scalar_prefetch=1,
            grid=(1,),
            in_specs=[
                pl.BlockSpec((peers, 1, lines, rows), lambda i, zh_ref: (0, zh_ref[0], 0, 0)),
                whole(far.shape),
                whole(near.shape),
                whole(stat.shape),
                pl.BlockSpec((BLOCK, DH), lambda i, zh_ref: (0, 0)),
            ],
            out_specs=whole(out),
        ),
        out_shape=jax.ShapeDtypeStruct(out, BF),
        compiler_params=params(),
        cost_estimate=pl.CostEstimate(
            flops=2 * peers * rows * wide, transcendentals=0, bytes_accessed=1 << 20
        ),
        name="merge",
    )(zh, got, far, near, stat, after.reshape(-1, after.shape[-1]))


def keep_kernel(where_ref, drop_ref, out_ref):
    rows, cols = out_ref.shape
    seed = where_ref[1] * 1000003 + where_ref[2] * cols
    inner = lax.broadcasted_iota(jnp.int32, (BLOCK, cols), 0) * D
    inner = inner + lax.broadcasted_iota(jnp.int32, (BLOCK, cols), 1) + seed
    for b in range(rows // BLOCK):
        hashed = inner + drop_ref[b]
        for _ in range(2):
            hashed = hashed ^ lax.shift_right_logical(hashed, jnp.int32(16))
            hashed = hashed * 73244475
        hashed = hashed ^ lax.shift_right_logical(hashed, jnp.int32(16))
        kept = (hashed & 1023) >= 102
        out_ref[b * BLOCK : (b + 1) * BLOCK, :] = jnp.where(
            kept, jnp.float32(1024.0 / 922.0), jnp.float32(0.0)
        )


def keep(where, drops, shape):
    return pl.pallas_call(
        keep_kernel,
        grid_spec=pltpu.PrefetchScalarGridSpec(
            num_scalar_prefetch=2, grid=(1,), in_specs=[], out_specs=whole(shape)
        ),
        out_shape=jax.ShapeDtypeStruct(shape, F32),
        compiler_params=params(),
        cost_estimate=pl.CostEstimate(
            flops=20 * shape[0] * shape[1], transcendentals=0, bytes_accessed=1 << 19
        ),
        name="keep",
    )(where, drops)


def project_kernel(part, shifts, last, where_ref, *refs):
    count = len(shifts)
    contexts, w_ref = refs[:count], refs[count]
    rest, held_ref, sems = refs[count + 1 : -2], refs[-2], refs[-1]
    half, _, wide = contexts[0].shape
    copies = []
    for i, shift in enumerate(shifts):
        parity = lax.rem(where_ref[0] + shift, 2)
        for z in range(half):
            at = i * half + z
            copies.append(
                pltpu.make_async_copy(
                    w_ref.at[z, parity, :, part * wide : (part + 1) * wide],
                    held_ref.at[at],
                    sems.at[at],
                )
            )
            copies[-1].start()
    acc = rest[0][...] if len(rest) > 1 else None
    for at, copy in enumerate(copies):
        copy.wait()
        term = dot_t(contexts[at // half][at % half], held_ref[at])
        acc = term if acc is None else acc + term
    if not last:
        rest[-1][...] = acc
        return
    _, keep_ref, res_ref, sum_ref, stat_ref = rest
    cols = acc.shape[1]
    total = res_ref[...].astype(F32) + keep_ref[...] * acc
    sum_ref[...] = total
    mean = jnp.sum(total, axis=1, keepdims=True) * jnp.float32(1.0 / cols)
    dev = total - mean
    spread = jnp.sum(dev * dev, axis=1, keepdims=True)
    lane = lax.broadcasted_iota(jnp.int32, stat_ref.shape, 1)
    stat_ref[...] = jnp.where(lane == 0, mean, spread)


def project(part, shifts, where, contexts, weight, before=None, finish=None):
    half, rows, wide = contexts[0].shape
    cols = weight.shape[2]
    out = (rows, cols)
    pieces = half * len(contexts)
    args = list(contexts) + [weight]
    specs = [whole(c.shape) for c in contexts] + [pl.BlockSpec(memory_space=pltpu.HBM)]
    out_specs, out_shape = [whole(out)], [jax.ShapeDtypeStruct(out, F32)]
    if before is not None:
        args.append(before)
        specs.append(whole(out))
    if finish is not None:
        args += list(finish)
        specs += [whole(x.shape) for x in finish]
        out_specs.append(whole((rows, DH)))
        out_shape.append(jax.ShapeDtypeStruct((rows, DH), F32))
    return pl.pallas_call(
        functools.partial(project_kernel, part, shifts, finish is not None),
        grid_spec=pltpu.PrefetchScalarGridSpec(
            num_scalar_prefetch=1,
            grid=(1,),
            in_specs=specs,
            out_specs=out_specs,
            scratch_shapes=[
                pltpu.VMEM((pieces, cols, wide), BF),
                pltpu.SemaphoreType.DMA((pieces,)),
            ],
        ),
        out_shape=out_shape,
        compiler_params=params(),
        cost_estimate=pl.CostEstimate(
            flops=2 * rows * pieces * wide * cols, transcendentals=0, bytes_accessed=2 << 20
        ),
        name="project",
    )(where, *args)


def on_device(
    queries,
    key_rows,
    value_rows,
    residual,
    out_weight,
    norm_gain,
    norm_bias,
    global_list,
    random_device,
    random_offset,
    drop_seed,
    drop_offsets,
):
    row_count, width_here = queries.shape
    block_count = row_count // BLOCK
    n_y, n_x, n_zh = (lax.axis_size(a) for a in SEQ)
    plane = n_x * n_zh
    seq_count = n_y * plane
    n_zl = lax.axis_size("zl")
    tp_count = n_zl * lax.axis_size("core")
    tp_at = lax.axis_index(TP)
    cols_here = out_weight.shape[1]

    plane_at = lax.axis_index(PLANE)
    y_at = lax.axis_index("y")
    zh_at = lax.axis_index("zh")
    wide = width_here // PARTS

    paired = jnp.concatenate([key_rows, value_rows], axis=1)
    pool = lax.all_gather(paired, "y", axis=0, tiled=True)

    def moves(flip):
        return [
            ((y * plane + p) * tp_count + t, (t * plane + (p ^ flip)) * tp_count + y)
            for y in range(n_y)
            for p in range(plane)
            for t in range(tp_count)
        ]

    same_zh = lax.ppermute(out_weight.T, SEQ + TP, moves(0))
    other_zh = lax.ppermute(out_weight.T, SEQ + TP, moves(1))
    shards = jnp.concatenate(
        [
            jnp.where(zh_at == 0, same_zh, other_zh),
            jnp.where(zh_at == 0, other_zh, same_zh),
        ],
        axis=0,
    )

    request_count = block_count * RAND
    target = random_device.reshape(request_count)
    wanted = random_offset.reshape(request_count)
    rank = jnp.arange(request_count, dtype=jnp.int32)
    same = target[:, None] == target[None, :]
    earlier = rank[None, :] < rank[:, None]
    slot = jnp.sum(jnp.logical_and(same, earlier), axis=1).astype(jnp.int32)
    slots = n_y * CAP
    place = (target // plane) * CAP + slot
    column = target % plane
    entry = column * (2 * slots) + place
    cells = jnp.arange(plane * 2 * slots, dtype=jnp.int32)
    is_offset = entry[:, None] == cells[None, :]
    is_asker = entry[:, None] + slots == cells[None, :]
    asker = rank // RAND + 1
    table = jnp.sum(
        jnp.where(is_offset, wanted[:, None], jnp.where(is_asker, asker[:, None], 0)), axis=0
    )
    table = jnp.pad(table.astype(BF)[None], ((0, 7), (0, width_here - cells.shape[0])))

    flip = [(0, 1), (1, 0)]

    def over_x(x):
        x = jnp.broadcast_to(x[None], (n_x,) + x.shape)
        return lax.all_to_all(x, "x", split_axis=0, concat_axis=0, tiled=True)

    near_q = jnp.concatenate([queries, table], axis=0)
    far_q = jnp.concatenate(
        [lax.ppermute(queries, "zh", flip), lax.ppermute(table, "zh", flip)], axis=0
    )
    asked = over_x(jnp.stack([near_q, far_q]))
    after = asked[0, 0, row_count, 0] * 0
    shards = over_x(shards + after)
    weight = lax.all_gather(
        shards.reshape(plane * cols_here, width_here), "y", axis=0, tiled=True
    )
    weight = weight.reshape(n_zl, 2, plane * cols_here, width_here)

    lists = asked[:, :, row_count, : cells.shape[0]].reshape(plane, plane, 2 * slots)
    lists = lax.dynamic_index_in_dim(lists, plane_at, 1, keepdims=False).astype(jnp.int32)
    base = (jnp.arange(slots, dtype=jnp.int32) // CAP) * block_count
    order = jnp.arange(plane, dtype=jnp.int32)
    peer = jnp.bitwise_xor(order, zh_at)
    nothing = jnp.int32(block_count)
    owner = global_list // block_count
    glob_row = (owner // plane) * block_count + global_list % block_count
    glob_mark = jnp.where(owner % plane == plane_at, -1, nothing)
    here = y_at * plane + peer
    low = (here + seq_count - 1) % seq_count
    high = (here + 1) % seq_count
    low_row = (low // plane) * block_count + block_count - 1
    high_row = (high // plane) * block_count
    low_mark = jnp.where(low % plane == plane_at, 0, nothing)
    high_mark = jnp.where(high % plane == plane_at, block_count - 1, nothing)
    marks = lists[:, slots:] - 1
    row = jnp.concatenate(
        [
            lists[:, :slots] + base[None],
            jnp.broadcast_to(glob_row[None], (plane, GLOB)),
            low_row[:, None],
            high_row[:, None],
        ],
        axis=1,
    ).reshape(-1)
    mark = jnp.concatenate(
        [
            jnp.where(marks < 0, nothing, marks),
            jnp.broadcast_to(glob_mark[None], (plane, GLOB)),
            low_mark[:, None],
            high_mark[:, None],
        ],
        axis=1,
    ).reshape(-1)
    zh = zh_at[None].astype(jnp.int32)

    near = [local(part, queries, key_rows, value_rows) for part in range(PARTS)]
    where = jnp.stack([tp_at % 2, drop_seed[0], tp_at]).astype(jnp.int32)
    kept = keep(where, drop_offsets, residual.shape)
    folded = []
    for part in range(PARTS):
        partials = serve(part, row, mark, zh, asked, pool, row_count)
        partials = partials.reshape((n_x, 2) + partials.shape[1:])
        got = lax.all_to_all(partials, "x", split_axis=0, concat_axis=0, tiled=True)
        gone = fold(zh, got, kept)
        folded.append((got, lax.ppermute(gone, "zh", flip)))
    mine, other = [], []
    for part in range(PARTS):
        context = merge(zh, *folded[part], *near[part], (gone, weight)[part], n_zl)
        mine.append(lax.all_to_all(context, "zl", split_axis=0, concat_axis=0, tiled=True))
        other.append(lax.ppermute(mine[part], "core", flip))
    (acc,) = project(0, (0, 1), where, (mine[0], other[0]), weight)
    (acc,) = project(1, (0,), where, (mine[1],), weight, before=acc)
    summed, stats = project(
        1, (1,), where, (other[1],), weight, before=acc, finish=(kept, residual)
    )

    stats = jnp.broadcast_to(stats[:, :2].T[None], (tp_count, 2, row_count))
    stats = lax.all_to_all(stats, TP, split_axis=0, concat_axis=0, tiled=True)
    means, spreads = stats[:, 0], stats[:, 1]
    mean = jnp.sum(means, axis=0) / tp_count
    away = means - mean[None]
    cols = summed.shape[1]
    spread = jnp.sum(spreads, axis=0) + cols * jnp.sum(away * away, axis=0)
    factor = lax.rsqrt(spread / D + 1e-05)
    encoded = (summed - mean[:, None]) * factor[:, None] * norm_gain[None] + norm_bias[None]
    return encoded.astype(BF)


def solution(mesh):
    fine = Mesh(mesh.devices.reshape(8, 4, 2, 4, 2), SEQ + TP)
    placed = (
        P(SEQ, TP),
        P(SEQ, TP),
        P(SEQ, TP),
        P(SEQ, TP),
        P(TP, SEQ),
        P(TP),
        P(TP),
        P(),
        P(SEQ, None),
        P(SEQ, None),
        P(),
        P(SEQ),
    )
    return jax.shard_map(
        on_device, mesh=fine, in_specs=placed, out_specs=P(SEQ, TP), check_vma=False
    )
```

```python
import functools
import math

import jax
import jax.numpy as jnp
from jax import lax
from jax.experimental import pallas as pl
from jax.experimental.pallas import tpu as pltpu
from jax.sharding import Mesh
from jax.sharding import PartitionSpec as P

D = 4096
DH = 128
BLOCK = 16
GLOB = 2
RAND = 3
CAP = 2
BF = jnp.bfloat16
F32 = jnp.float32
SEQ = ("y", "x", "zh")
TP = ("zl", "core")
PLANE = ("x", "zh")
PARTS = 2
STAT_ROWS = 16
NEG = -1e30
EMPTY = -1e20
MERGE_HINT = 30_000_000_000
VMEM_LIMIT = 48 * 1024 * 1024


def whole(shape):
    return pl.BlockSpec(shape, lambda *a: (0,) * len(shape))


def params(limit=VMEM_LIMIT):
    return pltpu.CompilerParams(vmem_limit_bytes=limit)


def partial(scores, listed, values):
    scores = jnp.where(listed, scores, NEG)
    top = jnp.maximum(jnp.max(scores, axis=0, keepdims=True), EMPTY)
    expo = weight_of(scores, top)
    total = jnp.sum(expo, axis=0, keepdims=True)
    got = lax.dot_general(
        values, expo.astype(BF), (((0,), (0,)), ((), ())), preferred_element_type=F32
    )
    return top, total, got


def weight_of(score, top):
    return jnp.exp2((score - top) * jnp.float32(math.log2(math.e) / DH**0.5))


def dot_t(a, b):
    return lax.dot_general(a, b, (((1,), (1,)), ((), ())), preferred_element_type=F32)


def split(x, parts):
    out = []
    for _ in range(parts):
        out.append(x.astype(BF))
        x = x - out[-1].astype(F32)
    return out


def serve_kernel(row_ref, mark_ref, zh_ref, q_ref, key_ref, value_ref, out_ref):
    n_x, n_zh, rows, wide = q_ref.shape
    listings = row_ref.shape[0] // (pl.num_programs(0) * n_x * n_zh)
    block_of = lax.broadcasted_iota(jnp.int32, (BLOCK, rows), 1) // BLOCK
    jobs = []
    for x in range(n_x):
        for j in range(n_zh):
            peer = (pl.program_id(0) * n_x + x) * n_zh + j
            places, listed = [], []
            for i in range(listings):
                at = peer * listings + i
                places.append(pl.ds(pl.multiple_of(row_ref[at] * BLOCK, BLOCK), BLOCK))
                mark = mark_ref[at]
                listed.append(
                    jnp.logical_or(block_of == mark, jnp.full(block_of.shape, mark) < 0)
                )
            listed = jnp.concatenate(listed, axis=0)
            jobs += [(x, j, h, places, listed) for h in range(wide // DH)]

    def scores(x, j, h, places, listed):
        lanes = slice(h * DH, (h + 1) * DH)
        keys = jnp.concatenate([key_ref[p, lanes] for p in places], axis=0)
        return dot_t(keys, q_ref[x, j, :, lanes])

    stats = []
    coming = scores(*jobs[0])
    for k, (x, j, h, places, listed) in enumerate(jobs):
        now = coming
        if k + 1 < len(jobs):
            coming = scores(*jobs[k + 1])
        lanes = slice(h * DH, (h + 1) * DH)
        values = jnp.concatenate([value_ref[p, lanes] for p in places], axis=0)
        top, total, got = partial(now, listed, values)
        peer = x * n_zh + lax.rem(j + zh_ref[0], n_zh)
        out_ref[peer, lanes, :] = got.astype(BF)
        stats += split(top, 3) + split(total, 2)
        if (h + 1) * DH == wide:
            stats.append(jnp.zeros((STAT_ROWS - len(stats), rows), BF))
            stats = jnp.concatenate([line.astype(F32) for line in stats], axis=0)
            out_ref[peer, wide:, :] = stats.astype(BF)
            stats = []


def serve(part, row, mark, zh, q, pool, out_rows):
    n_x = q.shape[0]
    wide = q.shape[3] // PARTS
    rows = out_rows
    peers = 2 * n_x
    out = (peers, wide + STAT_ROWS, rows)
    steps = n_x // 2
    return pl.pallas_call(
        serve_kernel,
        grid_spec=pltpu.PrefetchScalarGridSpec(
            num_scalar_prefetch=3,
            grid=(steps,),
            in_specs=[
                pl.BlockSpec((n_x // steps, 2, rows, wide), lambda i, a, b, c: (i, 0, 0, part)),
                pl.BlockSpec((pool.shape[0], wide), lambda i, a, b, c: (0, part)),
                pl.BlockSpec((pool.shape[0], wide), lambda i, a, b, c: (0, PARTS + part)),
            ],
            out_specs=pl.BlockSpec((peers // steps,) + out[1:], lambda i, a, b, c: (i, 0, 0)),
        ),
        out_shape=jax.ShapeDtypeStruct(out, BF),
        compiler_params=params(),
        cost_estimate=pl.CostEstimate(
            flops=4 * peers * rows * 320 * wide,
            transcendentals=peers * rows * 320 * wide // DH,
            bytes_accessed=4 << 20,
        ),
        name="serve",
    )(row, mark, zh, q, pool, pool)


def local_kernel(q_ref, k_ref, v_ref, out_ref, stat_ref):
    rows = q_ref.shape[0]
    heads = q_ref.shape[1] // DH
    key_block = lax.broadcasted_iota(jnp.int32, (rows, rows), 0) // BLOCK
    query_block = lax.broadcasted_iota(jnp.int32, (rows, rows), 1) // BLOCK
    listed = jnp.abs(key_block - query_block) <= 1
    tops, totals = [], []
    for h in range(heads):
        lanes = slice(h * DH, (h + 1) * DH)
        top, total, got = partial(
            dot_t(k_ref[:, lanes], q_ref[:, lanes]), listed, v_ref[:, lanes]
        )
        out_ref[lanes, :] = got
        tops.append(top)
        totals.append(total)
    stat_ref[...] = jnp.concatenate(tops + totals, axis=0)


def local(part, q, k, v):
    rows = q.shape[0]
    wide = q.shape[1] // PARTS
    stat = (2 * (wide // DH), rows)
    return pl.pallas_call(
        local_kernel,
        grid=(1,),
        in_specs=[pl.BlockSpec((rows, wide), lambda i: (0, part))] * 3,
        out_specs=[whole((wide, rows)), whole(stat)],
        out_shape=[jax.ShapeDtypeStruct((wide, rows), F32), jax.ShapeDtypeStruct(stat, F32)],
        compiler_params=params(),
        cost_estimate=pl.CostEstimate(
            flops=4 * rows * rows * wide,
            transcendentals=rows * rows * wide // DH,
            bytes_accessed=1 << 20,
        ),
        name="local",
    )(q, k, v)


def stats_of(block, wide, h):
    stats = block[wide:, :].astype(F32)
    at = 5 * h
    top = stats[at : at + 1] + stats[at + 1 : at + 2] + stats[at + 2 : at + 3]
    return top, stats[at + 3 : at + 4] + stats[at + 4 : at + 5]


def fold_kernel(zh_ref, got_ref, _, out_ref):
    peers, _, wide, rows = got_ref.shape
    wide = wide - STAT_ROWS
    stats = []
    for h in range(wide // DH):
        lines = slice(h * DH, (h + 1) * DH)
        pairs = [stats_of(got_ref[s, 0], wide, h) for s in range(peers)]
        top = functools.reduce(jnp.maximum, [t for t, _ in pairs])
        factors = [weight_of(t, top) for t, _ in pairs]
        total = sum(f * l for f, (_, l) in zip(factors, pairs))
        stats += split(top, 3) + split(total, 2)
        out_ref[lines, :] = sum(
            f * got_ref[s, 0, lines, :].astype(F32) for s, f in enumerate(factors)
        ).astype(BF)
    stats.append(jnp.zeros((STAT_ROWS - len(stats), rows), BF))
    out_ref[wide:, :] = jnp.concatenate([x.astype(F32) for x in stats], axis=0).astype(BF)


def fold(zh, got, after):
    peers, _, lines, rows = got.shape
    return pl.pallas_call(
        fold_kernel,
        grid_spec=pltpu.PrefetchScalarGridSpec(
            num_scalar_prefetch=1,
            grid=(1,),
            in_specs=[
                pl.BlockSpec((peers, 1, lines, rows), lambda i, zh_ref: (0, 1 - zh_ref[0], 0, 0)),
                pl.BlockSpec((BLOCK, DH), lambda i, zh_ref: (0, 0)),
            ],
            out_specs=whole((lines, rows)),
        ),
        out_shape=jax.ShapeDtypeStruct((lines, rows), BF),
        compiler_params=params(),
        cost_estimate=pl.CostEstimate(
            flops=2 * peers * rows * lines, transcendentals=0, bytes_accessed=1 << 20
        ),
        name="fold",
    )(zh, got, after)


def merge_kernel(zh_ref, got_ref, far_ref, near_ref, stat_ref, _, out_ref):
    peers, _, wide, rows = got_ref.shape
    wide = wide - STAT_ROWS
    heads = wide // DH
    for h in range(heads):
        lines = slice(h * DH, (h + 1) * DH)
        pairs = [stats_of(got_ref[s, 0], wide, h) for s in range(peers)]
        pairs.append(stats_of(far_ref[...], wide, h))
        pairs.append((stat_ref[h : h + 1, :], stat_ref[heads + h : heads + h + 1, :]))
        top = functools.reduce(jnp.maximum, [t for t, _ in pairs])
        factors = [weight_of(t, top) for t, _ in pairs]
        total = sum(f * l for f, (_, l) in zip(factors, pairs))
        factors = [f / total for f in factors]
        context = factors[-1] * near_ref[lines, :]
        context += factors[-2] * far_ref[lines, :].astype(F32)
        for s in range(peers):
            context += factors[s] * got_ref[s, 0, lines, :].astype(F32)
        context = context.T.astype(BF)
        for copy in range(out_ref.shape[0]):
            out_ref[copy, :, lines] = context


def merge(zh, got, far, near, stat, after, copies):
    peers, _, lines, rows = got.shape
    wide = lines - STAT_ROWS
    out = (copies, rows, wide)
    return pl.pallas_call(
        merge_kernel,
        grid_spec=pltpu.PrefetchScalarGridSpec(
            num_scalar_prefetch=1,
            grid=(1,),
            in_specs=[
                pl.BlockSpec((peers, 1, lines, rows), lambda i, zh_ref: (0, zh_ref[0], 0, 0)),
                whole(far.shape),
                whole(near.shape),
                whole(stat.shape),
                pl.BlockSpec((BLOCK, DH), lambda i, zh_ref: (0, 0)),
            ],
            out_specs=whole(out),
        ),
        out_shape=jax.ShapeDtypeStruct(out, BF),
        compiler_params=params(),
        cost_estimate=pl.CostEstimate(
            flops=MERGE_HINT, transcendentals=0, bytes_accessed=1 << 20
        ),
        name="merge",
    )(zh, got, far, near, stat, after.reshape(-1, after.shape[-1]))


def keep_kernel(where_ref, drop_ref, out_ref):
    rows, cols = out_ref.shape
    seed = where_ref[1] * 1000003 + where_ref[2] * cols
    inner = lax.broadcasted_iota(jnp.int32, (BLOCK, cols), 0) * D
    inner = inner + lax.broadcasted_iota(jnp.int32, (BLOCK, cols), 1) + seed
    for b in range(rows // BLOCK):
        hashed = inner + drop_ref[b]
        for _ in range(2):
            hashed = hashed ^ lax.shift_right_logical(hashed, jnp.int32(16))
            hashed = hashed * 73244475
        hashed = hashed ^ lax.shift_right_logical(hashed, jnp.int32(16))
        kept = (hashed & 1023) >= 102
        out_ref[b * BLOCK : (b + 1) * BLOCK, :] = jnp.where(
            kept, jnp.float32(1024.0 / 922.0), jnp.float32(0.0)
        )


def keep(where, drops, shape):
    return pl.pallas_call(
        keep_kernel,
        grid_spec=pltpu.PrefetchScalarGridSpec(
            num_scalar_prefetch=2, grid=(1,), in_specs=[], out_specs=whole(shape)
        ),
        out_shape=jax.ShapeDtypeStruct(shape, F32),
        compiler_params=params(),
        cost_estimate=pl.CostEstimate(
            flops=20 * shape[0] * shape[1], transcendentals=0, bytes_accessed=1 << 19
        ),
        name="keep",
    )(where, drops)


def project_kernel(part, shifts, last, where_ref, *refs):
    count = len(shifts)
    contexts, w_ref = refs[:count], refs[count]
    rest, held_ref, sems = refs[count + 1 : -2], refs[-2], refs[-1]
    half, _, wide = contexts[0].shape
    copies = []
    for i, shift in enumerate(shifts):
        parity = lax.rem(where_ref[0] + shift, 2)
        for z in range(half):
            at = i * half + z
            copies.append(
                pltpu.make_async_copy(
                    w_ref.at[z, parity, :, part * wide : (part + 1) * wide],
                    held_ref.at[at],
                    sems.at[at],
                )
            )
            copies[-1].start()
    acc = rest[0][...] if len(rest) > 1 else None
    for at, copy in enumerate(copies):
        copy.wait()
        term = dot_t(contexts[at // half][at % half], held_ref[at])
        acc = term if acc is None else acc + term
    if not last:
        rest[-1][...] = acc
        return
    _, keep_ref, res_ref, sum_ref, stat_ref = rest
    cols = acc.shape[1]
    total = res_ref[...].astype(F32) + keep_ref[...] * acc
    sum_ref[...] = total
    mean = jnp.sum(total, axis=1, keepdims=True) * jnp.float32(1.0 / cols)
    dev = total - mean
    spread = jnp.sum(dev * dev, axis=1, keepdims=True)
    lane = lax.broadcasted_iota(jnp.int32, stat_ref.shape, 1)
    stat_ref[...] = jnp.where(lane == 0, mean, spread)


def project(part, shifts, where, contexts, weight, before=None, finish=None):
    half, rows, wide = contexts[0].shape
    cols = weight.shape[2]
    out = (rows, cols)
    pieces = half * len(contexts)
    args = list(contexts) + [weight]
    specs = [whole(c.shape) for c in contexts] + [pl.BlockSpec(memory_space=pltpu.HBM)]
    out_specs, out_shape = [whole(out)], [jax.ShapeDtypeStruct(out, F32)]
    if before is not None:
        args.append(before)
        specs.append(whole(out))
    if finish is not None:
        args += list(finish)
        specs += [whole(x.shape) for x in finish]
        out_specs.append(whole((rows, DH)))
        out_shape.append(jax.ShapeDtypeStruct((rows, DH), F32))
    return pl.pallas_call(
        functools.partial(project_kernel, part, shifts, finish is not None),
        grid_spec=pltpu.PrefetchScalarGridSpec(
            num_scalar_prefetch=1,
            grid=(1,),
            in_specs=specs,
            out_specs=out_specs,
            scratch_shapes=[
                pltpu.VMEM((pieces, cols, wide), BF),
                pltpu.SemaphoreType.DMA((pieces,)),
            ],
        ),
        out_shape=out_shape,
        compiler_params=params(59 << 20),
        cost_estimate=pl.CostEstimate(
            flops=2 * rows * pieces * wide * cols, transcendentals=0, bytes_accessed=2 << 20
        ),
        name="project",
    )(where, *args)


def on_device(
    queries,
    key_rows,
    value_rows,
    residual,
    out_weight,
    norm_gain,
    norm_bias,
    global_list,
    random_device,
    random_offset,
    drop_seed,
    drop_offsets,
):
    row_count, width_here = queries.shape
    block_count = row_count // BLOCK
    n_y, n_x, n_zh = (lax.axis_size(a) for a in SEQ)
    plane = n_x * n_zh
    seq_count = n_y * plane
    n_zl = lax.axis_size("zl")
    tp_count = n_zl * lax.axis_size("core")
    tp_at = lax.axis_index(TP)
    cols_here = out_weight.shape[1]

    plane_at = lax.axis_index(PLANE)
    y_at = lax.axis_index("y")
    zh_at = lax.axis_index("zh")
    wide = width_here // PARTS

    paired = jnp.concatenate([key_rows, value_rows], axis=1)
    pool = lax.all_gather(paired, "y", axis=0, tiled=True)

    def moves(flip):
        return [
            ((y * plane + p) * tp_count + t, (t * plane + (p ^ flip)) * tp_count + y)
            for y in range(n_y)
            for p in range(plane)
            for t in range(tp_count)
        ]

    same_zh = lax.ppermute(out_weight.T, SEQ + TP, moves(0))
    other_zh = lax.ppermute(out_weight.T, SEQ + TP, moves(1))
    shards = jnp.concatenate(
        [
            jnp.where(zh_at == 0, same_zh, other_zh),
            jnp.where(zh_at == 0, other_zh, same_zh),
        ],
        axis=0,
    )

    request_count = block_count * RAND
    target = random_device.reshape(request_count)
    wanted = random_offset.reshape(request_count)
    rank = jnp.arange(request_count, dtype=jnp.int32)
    same = target[:, None] == target[None, :]
    earlier = rank[None, :] < rank[:, None]
    slot = jnp.sum(jnp.logical_and(same, earlier), axis=1).astype(jnp.int32)
    slots = n_y * CAP
    place = (target // plane) * CAP + slot
    column = target % plane
    entry = column * (2 * slots) + place
    cells = jnp.arange(plane * 2 * slots, dtype=jnp.int32)
    is_offset = entry[:, None] == cells[None, :]
    is_asker = entry[:, None] + slots == cells[None, :]
    asker = rank // RAND + 1
    table = jnp.sum(
        jnp.where(is_offset, wanted[:, None], jnp.where(is_asker, asker[:, None], 0)), axis=0
    )
    table = jnp.pad(table.astype(BF)[None], ((0, 7), (0, width_here - cells.shape[0])))

    flip = [(0, 1), (1, 0)]

    def over_x(x):
        x = jnp.broadcast_to(x[None], (n_x,) + x.shape)
        return lax.all_to_all(x, "x", split_axis=0, concat_axis=0, tiled=True)

    near_q = jnp.concatenate([queries, table], axis=0)
    far_q = jnp.concatenate(
        [lax.ppermute(queries, "zh", flip), lax.ppermute(table, "zh", flip)], axis=0
    )
    asked = over_x(jnp.stack([near_q, far_q]))
    after = asked[0, 0, row_count, 0] * 0
    shards = over_x(shards + after)
    weight = lax.all_gather(
        shards.reshape(plane * cols_here, width_here), "y", axis=0, tiled=True
    )
    weight = weight.reshape(n_zl, 2, plane * cols_here, width_here)

    lists = asked[:, :, row_count, : cells.shape[0]].reshape(plane, plane, 2 * slots)
    lists = lax.dynamic_index_in_dim(lists, plane_at, 1, keepdims=False).astype(jnp.int32)
    base = (jnp.arange(slots, dtype=jnp.int32) // CAP) * block_count
    order = jnp.arange(plane, dtype=jnp.int32)
    peer = jnp.bitwise_xor(order, zh_at)
    nothing = jnp.int32(block_count)
    owner = global_list // block_count
    glob_row = (owner // plane) * block_count + global_list % block_count
    glob_mark = jnp.where(owner % plane == plane_at, -1, nothing)
    here = y_at * plane + peer
    low = (here + seq_count - 1) % seq_count
    high = (here + 1) % seq_count
    low_row = (low // plane) * block_count + block_count - 1
    high_row = (high // plane) * block_count
    low_mark = jnp.where(low % plane == plane_at, 0, nothing)
    high_mark = jnp.where(high % plane == plane_at, block_count - 1, nothing)
    marks = lists[:, slots:] - 1
    row = jnp.concatenate(
        [
            lists[:, :slots] + base[None],
            jnp.broadcast_to(glob_row[None], (plane, GLOB)),
            low_row[:, None],
            high_row[:, None],
        ],
        axis=1,
    ).reshape(-1)
    mark = jnp.concatenate(
        [
            jnp.where(marks < 0, nothing, marks),
            jnp.broadcast_to(glob_mark[None], (plane, GLOB)),
            low_mark[:, None],
            high_mark[:, None],
        ],
        axis=1,
    ).reshape(-1)
    zh = zh_at[None].astype(jnp.int32)

    near = [local(part, queries, key_rows, value_rows) for part in range(PARTS)]
    where = jnp.stack([tp_at % 2, drop_seed[0], tp_at]).astype(jnp.int32)
    kept = keep(where, drop_offsets, residual.shape)
    folded = []
    for part in range(PARTS):
        partials = serve(part, row, mark, zh, asked, pool, row_count)
        partials = partials.reshape((n_x, 2) + partials.shape[1:])
        got = lax.all_to_all(partials, "x", split_axis=0, concat_axis=0, tiled=True)
        gone = fold(zh, got, kept)
        folded.append((got, lax.ppermute(gone, "zh", flip)))
    mine, other = [], []
    for part in range(PARTS):
        context = merge(zh, *folded[part], *near[part], (gone, weight)[part], n_zl)
        mine.append(lax.all_to_all(context, "zl", split_axis=0, concat_axis=0, tiled=True))
        other.append(lax.ppermute(mine[part], "core", flip))
    (acc,) = project(0, (0, 1), where, (mine[0], other[0]), weight)
    (acc,) = project(1, (0,), where, (mine[1],), weight, before=acc)
    summed, stats = project(
        1, (1,), where, (other[1],), weight, before=acc, finish=(kept, residual)
    )

    stats = jnp.broadcast_to(stats[:, :2].T[None], (tp_count, 2, row_count))
    stats = lax.all_to_all(stats, TP, split_axis=0, concat_axis=0, tiled=True)
    means, spreads = stats[:, 0], stats[:, 1]
    mean = jnp.sum(means, axis=0) / tp_count
    away = means - mean[None]
    cols = summed.shape[1]
    spread = jnp.sum(spreads, axis=0) + cols * jnp.sum(away * away, axis=0)
    factor = lax.rsqrt(spread / D + 1e-05)
    encoded = (summed - mean[:, None]) * factor[:, None] * norm_gain[None] + norm_bias[None]
    return encoded.astype(BF)


def solution(mesh):
    fine = Mesh(mesh.devices.reshape(8, 4, 2, 4, 2), SEQ + TP)
    placed = (
        P(SEQ, TP),
        P(SEQ, TP),
        P(SEQ, TP),
        P(SEQ, TP),
        P(TP, SEQ),
        P(TP),
        P(TP),
        P(),
        P(SEQ, None),
        P(SEQ, None),
        P(),
        P(SEQ),
    )
    return jax.shard_map(
        on_device, mesh=fine, in_specs=placed, out_specs=P(SEQ, TP), check_vma=False
    )
```

```python
import functools
import math

import jax
import jax.numpy as jnp
from jax import lax
from jax.experimental import pallas as pl
from jax.experimental.pallas import tpu as pltpu
from jax.sharding import Mesh
from jax.sharding import PartitionSpec as P

D = 4096
DH = 128
BLOCK = 16
GLOB = 2
RAND = 3
CAP = 2
BF = jnp.bfloat16
F32 = jnp.float32
SEQ = ("y", "x", "zh")
TP = ("zl", "core")
PLANE = ("x", "zh")
PARTS = 2
PROJECT_LIMIT = 48
STAT_ROWS = 16
NEG = -1e30
EMPTY = -1e20
MERGE_HINT = 30_000_000_000
VMEM_LIMIT = 48 * 1024 * 1024


def whole(shape):
    return pl.BlockSpec(shape, lambda *a: (0,) * len(shape))


def params(limit=VMEM_LIMIT):
    return pltpu.CompilerParams(vmem_limit_bytes=limit)


def partial(scores, listed, values):
    scores = jnp.where(listed, scores, NEG)
    top = jnp.maximum(jnp.max(scores, axis=0, keepdims=True), EMPTY)
    expo = weight_of(scores, top)
    total = jnp.sum(expo, axis=0, keepdims=True)
    got = lax.dot_general(
        values, expo.astype(BF), (((0,), (0,)), ((), ())), preferred_element_type=F32
    )
    return top, total, got


def weight_of(score, top):
    return jnp.exp2((score - top) * jnp.float32(math.log2(math.e) / DH**0.5))


def dot_t(a, b):
    return lax.dot_general(a, b, (((1,), (1,)), ((), ())), preferred_element_type=F32)


def split(x, parts):
    out = []
    for _ in range(parts):
        out.append(x.astype(BF))
        x = x - out[-1].astype(F32)
    return out


def serve_kernel(row_ref, mark_ref, zh_ref, q_ref, key_ref, value_ref, out_ref):
    n_x, n_zh, rows, wide = q_ref.shape
    listings = row_ref.shape[0] // (pl.num_programs(0) * n_x * n_zh)
    block_of = lax.broadcasted_iota(jnp.int32, (BLOCK, rows), 1) // BLOCK
    jobs = []
    for x in range(n_x):
        for j in range(n_zh):
            peer = (pl.program_id(0) * n_x + x) * n_zh + j
            places, listed = [], []
            for i in range(listings):
                at = peer * listings + i
                places.append(pl.ds(pl.multiple_of(row_ref[at] * BLOCK, BLOCK), BLOCK))
                mark = mark_ref[at]
                listed.append(
                    jnp.logical_or(block_of == mark, jnp.full(block_of.shape, mark) < 0)
                )
            listed = jnp.concatenate(listed, axis=0)
            jobs += [(x, j, h, places, listed) for h in range(wide // DH)]

    def scores(x, j, h, places, listed):
        lanes = slice(h * DH, (h + 1) * DH)
        keys = jnp.concatenate([key_ref[p, lanes] for p in places], axis=0)
        return dot_t(keys, q_ref[x, j, :, lanes])

    stats = []
    coming = scores(*jobs[0])
    for k, (x, j, h, places, listed) in enumerate(jobs):
        now = coming
        if k + 1 < len(jobs):
            coming = scores(*jobs[k + 1])
        lanes = slice(h * DH, (h + 1) * DH)
        values = jnp.concatenate([value_ref[p, lanes] for p in places], axis=0)
        top, total, got = partial(now, listed, values)
        peer = x * n_zh + lax.rem(j + zh_ref[0], n_zh)
        out_ref[peer, lanes, :] = got.astype(BF)
        stats += split(top, 3) + split(total, 2)
        if (h + 1) * DH == wide:
            stats.append(jnp.zeros((STAT_ROWS - len(stats), rows), BF))
            stats = jnp.concatenate([line.astype(F32) for line in stats], axis=0)
            out_ref[peer, wide:, :] = stats.astype(BF)
            stats = []


def serve(part, row, mark, zh, q, pool, out_rows):
    n_x = q.shape[0]
    wide = q.shape[3] // PARTS
    rows = out_rows
    peers = 2 * n_x
    out = (peers, wide + STAT_ROWS, rows)
    steps = n_x // 2
    return pl.pallas_call(
        serve_kernel,
        grid_spec=pltpu.PrefetchScalarGridSpec(
            num_scalar_prefetch=3,
            grid=(steps,),
            in_specs=[
                pl.BlockSpec((n_x // steps, 2, rows, wide), lambda i, a, b, c: (i, 0, 0, part)),
                pl.BlockSpec((pool.shape[0], wide), lambda i, a, b, c: (0, part)),
                pl.BlockSpec((pool.shape[0], wide), lambda i, a, b, c: (0, PARTS + part)),
            ],
            out_specs=pl.BlockSpec((peers // steps,) + out[1:], lambda i, a, b, c: (i, 0, 0)),
        ),
        out_shape=jax.ShapeDtypeStruct(out, BF),
        compiler_params=params(),
        cost_estimate=pl.CostEstimate(
            flops=4 * peers * rows * 320 * wide,
            transcendentals=peers * rows * 320 * wide // DH,
            bytes_accessed=4 << 20,
        ),
        name="serve",
    )(row, mark, zh, q, pool, pool)


def local_kernel(q_ref, k_ref, v_ref, out_ref, stat_ref):
    rows = q_ref.shape[0]
    heads = q_ref.shape[1] // DH
    key_block = lax.broadcasted_iota(jnp.int32, (rows, rows), 0) // BLOCK
    query_block = lax.broadcasted_iota(jnp.int32, (rows, rows), 1) // BLOCK
    listed = jnp.abs(key_block - query_block) <= 1
    tops, totals = [], []
    for h in range(heads):
        lanes = slice(h * DH, (h + 1) * DH)
        top, total, got = partial(
            dot_t(k_ref[:, lanes], q_ref[:, lanes]), listed, v_ref[:, lanes]
        )
        out_ref[lanes, :] = got
        tops.append(top)
        totals.append(total)
    stat_ref[...] = jnp.concatenate(tops + totals, axis=0)


def local(part, q, k, v):
    rows = q.shape[0]
    wide = q.shape[1] // PARTS
    stat = (2 * (wide // DH), rows)
    return pl.pallas_call(
        local_kernel,
        grid=(1,),
        in_specs=[pl.BlockSpec((rows, wide), lambda i: (0, part))] * 3,
        out_specs=[whole((wide, rows)), whole(stat)],
        out_shape=[jax.ShapeDtypeStruct((wide, rows), F32), jax.ShapeDtypeStruct(stat, F32)],
        compiler_params=params(),
        cost_estimate=pl.CostEstimate(
            flops=4 * rows * rows * wide,
            transcendentals=rows * rows * wide // DH,
            bytes_accessed=1 << 20,
        ),
        name="local",
    )(q, k, v)


def stats_of(block, wide, h):
    stats = block[wide:, :].astype(F32)
    at = 5 * h
    top = stats[at : at + 1] + stats[at + 1 : at + 2] + stats[at + 2 : at + 3]
    return top, stats[at + 3 : at + 4] + stats[at + 4 : at + 5]


def fold_kernel(zh_ref, got_ref, _, out_ref):
    peers, _, wide, rows = got_ref.shape
    wide = wide - STAT_ROWS
    stats = []
    for h in range(wide // DH):
        lines = slice(h * DH, (h + 1) * DH)
        pairs = [stats_of(got_ref[s, 0], wide, h) for s in range(peers)]
        top = functools.reduce(jnp.maximum, [t for t, _ in pairs])
        factors = [weight_of(t, top) for t, _ in pairs]
        total = sum(f * l for f, (_, l) in zip(factors, pairs))
        stats += split(top, 3) + split(total, 2)
        out_ref[lines, :] = sum(
            f * got_ref[s, 0, lines, :].astype(F32) for s, f in enumerate(factors)
        ).astype(BF)
    stats.append(jnp.zeros((STAT_ROWS - len(stats), rows), BF))
    out_ref[wide:, :] = jnp.concatenate([x.astype(F32) for x in stats], axis=0).astype(BF)


def fold(zh, got, after):
    peers, _, lines, rows = got.shape
    return pl.pallas_call(
        fold_kernel,
        grid_spec=pltpu.PrefetchScalarGridSpec(
            num_scalar_prefetch=1,
            grid=(1,),
            in_specs=[
                pl.BlockSpec((peers, 1, lines, rows), lambda i, zh_ref: (0, 1 - zh_ref[0], 0, 0)),
                pl.BlockSpec((BLOCK, DH), lambda i, zh_ref: (0, 0)),
            ],
            out_specs=whole((lines, rows)),
        ),
        out_shape=jax.ShapeDtypeStruct((lines, rows), BF),
        compiler_params=params(),
        cost_estimate=pl.CostEstimate(
            flops=2 * peers * rows * lines, transcendentals=0, bytes_accessed=1 << 20
        ),
        name="fold",
    )(zh, got, after)


def merge_kernel(zh_ref, got_ref, far_ref, near_ref, stat_ref, _, out_ref):
    peers, _, wide, rows = got_ref.shape
    wide = wide - STAT_ROWS
    heads = wide // DH
    for h in range(heads):
        lines = slice(h * DH, (h + 1) * DH)
        pairs = [stats_of(got_ref[s, 0], wide, h) for s in range(peers)]
        pairs.append(stats_of(far_ref[...], wide, h))
        pairs.append((stat_ref[h : h + 1, :], stat_ref[heads + h : heads + h + 1, :]))
        top = functools.reduce(jnp.maximum, [t for t, _ in pairs])
        factors = [weight_of(t, top) for t, _ in pairs]
        total = sum(f * l for f, (_, l) in zip(factors, pairs))
        factors = [f / total for f in factors]
        context = factors[-1] * near_ref[lines, :]
        context += factors[-2] * far_ref[lines, :].astype(F32)
        for s in range(peers):
            context += factors[s] * got_ref[s, 0, lines, :].astype(F32)
        context = context.T.astype(BF)
        for copy in range(out_ref.shape[0]):
            out_ref[copy, :, lines] = context


def merge(zh, got, far, near, stat, after, copies):
    peers, _, lines, rows = got.shape
    wide = lines - STAT_ROWS
    out = (copies, rows, wide)
    return pl.pallas_call(
        merge_kernel,
        grid_spec=pltpu.PrefetchScalarGridSpec(
            num_scalar_prefetch=1,
            grid=(1,),
            in_specs=[
                pl.BlockSpec((peers, 1, lines, rows), lambda i, zh_ref: (0, zh_ref[0], 0, 0)),
                whole(far.shape),
                whole(near.shape),
                whole(stat.shape),
                pl.BlockSpec((BLOCK, DH), lambda i, zh_ref: (0, 0)),
            ],
            out_specs=whole(out),
        ),
        out_shape=jax.ShapeDtypeStruct(out, BF),
        compiler_params=params(),
        cost_estimate=pl.CostEstimate(
            flops=MERGE_HINT, transcendentals=0, bytes_accessed=1 << 20
        ),
        name="merge",
    )(zh, got, far, near, stat, after.reshape(-1, after.shape[-1]))


def keep_kernel(where_ref, drop_ref, out_ref):
    rows, cols = out_ref.shape
    seed = where_ref[1] * 1000003 + where_ref[2] * cols
    inner = lax.broadcasted_iota(jnp.int32, (BLOCK, cols), 0) * D
    inner = inner + lax.broadcasted_iota(jnp.int32, (BLOCK, cols), 1) + seed
    for b in range(rows // BLOCK):
        hashed = inner + drop_ref[b]
        for _ in range(2):
            hashed = hashed ^ lax.shift_right_logical(hashed, jnp.int32(16))
            hashed = hashed * 73244475
        hashed = hashed ^ lax.shift_right_logical(hashed, jnp.int32(16))
        kept = (hashed & 1023) >= 102
        out_ref[b * BLOCK : (b + 1) * BLOCK, :] = jnp.where(
            kept, jnp.float32(1024.0 / 922.0), jnp.float32(0.0)
        )


def keep(where, drops, shape):
    return pl.pallas_call(
        keep_kernel,
        grid_spec=pltpu.PrefetchScalarGridSpec(
            num_scalar_prefetch=2, grid=(1,), in_specs=[], out_specs=whole(shape)
        ),
        out_shape=jax.ShapeDtypeStruct(shape, F32),
        compiler_params=params(),
        cost_estimate=pl.CostEstimate(
            flops=20 * shape[0] * shape[1], transcendentals=0, bytes_accessed=1 << 19
        ),
        name="keep",
    )(where, drops)


def project_kernel(where_ref, *refs):
    contexts, rest = refs[: 2 * PARTS], refs[2 * PARTS :]
    w_ref, keep_ref, res_ref, sum_ref, stat_ref, held_ref, sems = rest
    half, _, wide = contexts[0].shape
    copies = []
    for z in range(half):
        for shift in range(2):
            at = 2 * z + shift
            copies.append(
                pltpu.make_async_copy(
                    w_ref.at[2 * z + lax.rem(where_ref[0] + shift, 2)],
                    held_ref.at[at],
                    sems.at[at],
                )
            )
            copies[-1].start()
    acc = None
    for at, copy in enumerate(copies):
        copy.wait()
        for part in range(PARTS):
            term = dot_t(
                contexts[2 * part + at % 2][at // 2],
                held_ref[at, :, part * wide : (part + 1) * wide],
            )
            acc = term if acc is None else acc + term
    rows, cols = acc.shape
    total = res_ref[...].astype(F32) + keep_ref[...] * acc
    sum_ref[...] = total
    mean = jnp.sum(total, axis=1, keepdims=True) * jnp.float32(1.0 / cols)
    dev = total - mean
    spread = jnp.sum(dev * dev, axis=1, keepdims=True)
    lane = lax.broadcasted_iota(jnp.int32, (rows, DH), 1)
    lines = jnp.where(lane == 0, mean, spread).T[:2, :]
    for copy in range(stat_ref.shape[0]):
        stat_ref[copy] = lines


def project(where, contexts, weight, kept, residual):
    rows, cols = residual.shape
    groups = weight.shape[0]
    args = list(contexts) + [weight, kept, residual]
    specs = [whole(x.shape) for x in args]
    specs[len(contexts)] = pl.BlockSpec(memory_space=pltpu.HBM)
    stat = (groups, 2, rows)
    return pl.pallas_call(
        project_kernel,
        grid_spec=pltpu.PrefetchScalarGridSpec(
            num_scalar_prefetch=1,
            grid=(1,),
            in_specs=specs,
            out_specs=[whole((rows, cols)), whole(stat)],
            scratch_shapes=[
                pltpu.VMEM(weight.shape, BF),
                pltpu.SemaphoreType.DMA((groups,)),
            ],
        ),
        out_shape=[
            jax.ShapeDtypeStruct((rows, cols), F32),
            jax.ShapeDtypeStruct(stat, F32),
        ],
        compiler_params=params(PROJECT_LIMIT << 20),
        cost_estimate=pl.CostEstimate(
            flops=2 * rows * D * cols, transcendentals=0, bytes_accessed=6 << 20
        ),
        name="project",
    )(where, *args)


def on_device(
    queries,
    key_rows,
    value_rows,
    residual,
    out_weight,
    norm_gain,
    norm_bias,
    global_list,
    random_device,
    random_offset,
    drop_seed,
    drop_offsets,
):
    row_count, width_here = queries.shape
    block_count = row_count // BLOCK
    n_y, n_x, n_zh = (lax.axis_size(a) for a in SEQ)
    plane = n_x * n_zh
    seq_count = n_y * plane
    n_zl = lax.axis_size("zl")
    tp_count = n_zl * lax.axis_size("core")
    tp_at = lax.axis_index(TP)
    cols_here = out_weight.shape[1]

    plane_at = lax.axis_index(PLANE)
    y_at = lax.axis_index("y")
    zh_at = lax.axis_index("zh")
    wide = width_here // PARTS

    paired = jnp.concatenate([key_rows, value_rows], axis=1)
    pool = lax.all_gather(paired, "y", axis=0, tiled=True)

    def moves(flip):
        return [
            ((y * plane + p) * tp_count + t, (t * plane + (p ^ flip)) * tp_count + y)
            for y in range(n_y)
            for p in range(plane)
            for t in range(tp_count)
        ]

    same_zh = lax.ppermute(out_weight.T, SEQ + TP, moves(0))
    other_zh = lax.ppermute(out_weight.T, SEQ + TP, moves(1))
    shards = jnp.concatenate(
        [
            jnp.where(zh_at == 0, same_zh, other_zh),
            jnp.where(zh_at == 0, other_zh, same_zh),
        ],
        axis=0,
    )

    request_count = block_count * RAND
    target = random_device.reshape(request_count)
    wanted = random_offset.reshape(request_count)
    rank = jnp.arange(request_count, dtype=jnp.int32)
    same = target[:, None] == target[None, :]
    earlier = rank[None, :] < rank[:, None]
    slot = jnp.sum(jnp.logical_and(same, earlier), axis=1).astype(jnp.int32)
    slots = n_y * CAP
    place = (target // plane) * CAP + slot
    column = target % plane
    entry = column * (2 * slots) + place
    cells = jnp.arange(plane * 2 * slots, dtype=jnp.int32)
    is_offset = entry[:, None] == cells[None, :]
    is_asker = entry[:, None] + slots == cells[None, :]
    asker = rank // RAND + 1
    table = jnp.sum(
        jnp.where(is_offset, wanted[:, None], jnp.where(is_asker, asker[:, None], 0)), axis=0
    )
    table = jnp.pad(table.astype(BF)[None], ((0, 7), (0, width_here - cells.shape[0])))

    flip = [(0, 1), (1, 0)]

    def over_x(x):
        x = jnp.broadcast_to(x[None], (n_x,) + x.shape)
        return lax.all_to_all(x, "x", split_axis=0, concat_axis=0, tiled=True)

    near_q = jnp.concatenate([queries, table], axis=0)
    far_q = jnp.concatenate(
        [lax.ppermute(queries, "zh", flip), lax.ppermute(table, "zh", flip)], axis=0
    )
    asked = over_x(jnp.stack([near_q, far_q]))
    after = asked[0, 0, row_count, 0] * 0
    shards = over_x(shards + after)
    weight = lax.all_gather(
        shards.reshape(plane * cols_here, width_here), "y", axis=0, tiled=True
    )
    weight = weight.reshape(tp_count, plane * cols_here, width_here)

    lists = asked[:, :, row_count, : cells.shape[0]].reshape(plane, plane, 2 * slots)
    lists = lax.dynamic_index_in_dim(lists, plane_at, 1, keepdims=False).astype(jnp.int32)
    base = (jnp.arange(slots, dtype=jnp.int32) // CAP) * block_count
    order = jnp.arange(plane, dtype=jnp.int32)
    peer = jnp.bitwise_xor(order, zh_at)
    nothing = jnp.int32(block_count)
    owner = global_list // block_count
    glob_row = (owner // plane) * block_count + global_list % block_count
    glob_mark = jnp.where(owner % plane == plane_at, -1, nothing)
    here = y_at * plane + peer
    low = (here + seq_count - 1) % seq_count
    high = (here + 1) % seq_count
    low_row = (low // plane) * block_count + block_count - 1
    high_row = (high // plane) * block_count
    low_mark = jnp.where(low % plane == plane_at, 0, nothing)
    high_mark = jnp.where(high % plane == plane_at, block_count - 1, nothing)
    marks = lists[:, slots:] - 1
    row = jnp.concatenate(
        [
            lists[:, :slots] + base[None],
            jnp.broadcast_to(glob_row[None], (plane, GLOB)),
            low_row[:, None],
            high_row[:, None],
        ],
        axis=1,
    ).reshape(-1)
    mark = jnp.concatenate(
        [
            jnp.where(marks < 0, nothing, marks),
            jnp.broadcast_to(glob_mark[None], (plane, GLOB)),
            low_mark[:, None],
            high_mark[:, None],
        ],
        axis=1,
    ).reshape(-1)
    zh = zh_at[None].astype(jnp.int32)

    near = [local(part, queries, key_rows, value_rows) for part in range(PARTS)]
    where = jnp.stack([tp_at % 2, drop_seed[0], tp_at]).astype(jnp.int32)
    kept = keep(where, drop_offsets, residual.shape)
    folded = []
    for part in range(PARTS):
        partials = serve(part, row, mark, zh, asked, pool, row_count)
        partials = partials.reshape((n_x, 2) + partials.shape[1:])
        got = lax.all_to_all(partials, "x", split_axis=0, concat_axis=0, tiled=True)
        gone = fold(zh, got, kept)
        folded.append((got, lax.ppermute(gone, "zh", flip)))
    contexts = []
    for part in range(PARTS):
        context = merge(zh, *folded[part], *near[part], (gone, weight)[part], n_zl)
        mine = lax.all_to_all(context, "zl", split_axis=0, concat_axis=0, tiled=True)
        contexts += [mine, lax.ppermute(mine, "core", flip)]
    summed, stats = project(where, contexts, weight, kept, residual)
    stats = lax.all_to_all(stats, TP, split_axis=0, concat_axis=0, tiled=True)
    means, spreads = stats[:, 0], stats[:, 1]
    mean = jnp.sum(means, axis=0) / tp_count
    away = means - mean[None]
    cols = summed.shape[1]
    spread = jnp.sum(spreads, axis=0) + cols * jnp.sum(away * away, axis=0)
    factor = lax.rsqrt(spread / D + 1e-05)
    encoded = (summed - mean[:, None]) * factor[:, None] * norm_gain[None] + norm_bias[None]
    return encoded.astype(BF)


def solution(mesh):
    fine = Mesh(mesh.devices.reshape(8, 4, 2, 4, 2), SEQ + TP)
    placed = (
        P(SEQ, TP),
        P(SEQ, TP),
        P(SEQ, TP),
        P(SEQ, TP),
        P(TP, SEQ),
        P(TP),
        P(TP),
        P(),
        P(SEQ, None),
        P(SEQ, None),
        P(),
        P(SEQ),
    )
    return jax.shard_map(
        on_device, mesh=fine, in_specs=placed, out_specs=P(SEQ, TP), check_vma=False
    )
```

```python
import functools
import math

import jax
import jax.numpy as jnp
from jax import lax
from jax.experimental import pallas as pl
from jax.experimental.pallas import tpu as pltpu
from jax.sharding import Mesh
from jax.sharding import PartitionSpec as P

D = 4096
DH = 128
BLOCK = 16
GLOB = 2
RAND = 3
CAP = 2
BF = jnp.bfloat16
F32 = jnp.float32
SEQ = ("y", "x", "zh")
TP = ("zl", "core")
PLANE = ("x", "zh")
PARTS = 2
PROJECT_LIMIT = 48
STAT_ROWS = 16
NEG = -1e30
EMPTY = -1e20
MERGE_HINT = 30_000_000_000
VMEM_LIMIT = 48 * 1024 * 1024


def whole(shape):
    return pl.BlockSpec(shape, lambda *a: (0,) * len(shape))


def params(limit=VMEM_LIMIT):
    return pltpu.CompilerParams(vmem_limit_bytes=limit)


def partial(scores, listed, values):
    scores = jnp.where(listed, scores, NEG)
    top = jnp.maximum(jnp.max(scores, axis=0, keepdims=True), EMPTY)
    expo = weight_of(scores, top)
    total = jnp.sum(expo, axis=0, keepdims=True)
    got = lax.dot_general(
        values, expo.astype(BF), (((0,), (0,)), ((), ())), preferred_element_type=F32
    )
    return top, total, got


def weight_of(score, top):
    return jnp.exp2((score - top) * jnp.float32(math.log2(math.e) / DH**0.5))


def dot_t(a, b):
    return lax.dot_general(a, b, (((1,), (1,)), ((), ())), preferred_element_type=F32)


def split(x, parts):
    out = []
    for _ in range(parts):
        out.append(x.astype(BF))
        x = x - out[-1].astype(F32)
    return out


def serve_kernel(row_ref, mark_ref, zh_ref, q_ref, key_ref, value_ref, out_ref):
    n_x, n_zh, rows, wide = q_ref.shape
    listings = row_ref.shape[0] // (pl.num_programs(0) * n_x * n_zh)
    block_of = lax.broadcasted_iota(jnp.int32, (BLOCK, rows), 1) // BLOCK
    jobs = []
    for x in range(n_x):
        for j in range(n_zh):
            peer = (pl.program_id(0) * n_x + x) * n_zh + j
            places, listed = [], []
            for i in range(listings):
                at = peer * listings + i
                places.append(pl.ds(pl.multiple_of(row_ref[at] * BLOCK, BLOCK), BLOCK))
                mark = mark_ref[at]
                listed.append(
                    jnp.logical_or(block_of == mark, jnp.full(block_of.shape, mark) < 0)
                )
            listed = jnp.concatenate(listed, axis=0)
            jobs += [(x, j, h, places, listed) for h in range(wide // DH)]

    def scores(x, j, h, places, listed):
        lanes = slice(h * DH, (h + 1) * DH)
        keys = jnp.concatenate([key_ref[p, lanes] for p in places], axis=0)
        return dot_t(keys, q_ref[x, j, :, lanes])

    stats = []
    coming = scores(*jobs[0])
    for k, (x, j, h, places, listed) in enumerate(jobs):
        now = coming
        if k + 1 < len(jobs):
            coming = scores(*jobs[k + 1])
        lanes = slice(h * DH, (h + 1) * DH)
        values = jnp.concatenate([value_ref[p, lanes] for p in places], axis=0)
        top, total, got = partial(now, listed, values)
        peer = x * n_zh + lax.rem(j + zh_ref[0], n_zh)
        out_ref[peer, lanes, :] = got.astype(BF)
        stats += split(top, 3) + split(total, 2)
        if (h + 1) * DH == wide:
            stats.append(jnp.zeros((STAT_ROWS - len(stats), rows), BF))
            stats = jnp.concatenate([line.astype(F32) for line in stats], axis=0)
            out_ref[peer, wide:, :] = stats.astype(BF)
            stats = []


def serve(part, row, mark, zh, q, pool, out_rows):
    n_x = q.shape[0]
    wide = q.shape[3] // PARTS
    rows = out_rows
    peers = 2 * n_x
    out = (peers, wide + STAT_ROWS, rows)
    steps = n_x // 2
    return pl.pallas_call(
        serve_kernel,
        grid_spec=pltpu.PrefetchScalarGridSpec(
            num_scalar_prefetch=3,
            grid=(steps,),
            in_specs=[
                pl.BlockSpec((n_x // steps, 2, rows, wide), lambda i, a, b, c: (i, 0, 0, part)),
                pl.BlockSpec((pool.shape[0], wide), lambda i, a, b, c: (0, part)),
                pl.BlockSpec((pool.shape[0], wide), lambda i, a, b, c: (0, PARTS + part)),
            ],
            out_specs=pl.BlockSpec((peers // steps,) + out[1:], lambda i, a, b, c: (i, 0, 0)),
        ),
        out_shape=jax.ShapeDtypeStruct(out, BF),
        compiler_params=params(),
        cost_estimate=pl.CostEstimate(
            flops=4 * peers * rows * 320 * wide,
            transcendentals=peers * rows * 320 * wide // DH,
            bytes_accessed=4 << 20,
        ),
        name="serve",
    )(row, mark, zh, q, pool, pool)


def local_kernel(q_ref, k_ref, v_ref, out_ref, stat_ref):
    rows = q_ref.shape[0]
    heads = q_ref.shape[1] // DH
    key_block = lax.broadcasted_iota(jnp.int32, (rows, rows), 0) // BLOCK
    query_block = lax.broadcasted_iota(jnp.int32, (rows, rows), 1) // BLOCK
    listed = jnp.abs(key_block - query_block) <= 1
    tops, totals = [], []
    for h in range(heads):
        lanes = slice(h * DH, (h + 1) * DH)
        top, total, got = partial(
            dot_t(k_ref[:, lanes], q_ref[:, lanes]), listed, v_ref[:, lanes]
        )
        out_ref[lanes, :] = got
        tops.append(top)
        totals.append(total)
    stat_ref[...] = jnp.concatenate(tops + totals, axis=0)


def local(part, q, k, v):
    rows = q.shape[0]
    wide = q.shape[1] // PARTS
    stat = (2 * (wide // DH), rows)
    return pl.pallas_call(
        local_kernel,
        grid=(1,),
        in_specs=[pl.BlockSpec((rows, wide), lambda i: (0, part))] * 3,
        out_specs=[whole((wide, rows)), whole(stat)],
        out_shape=[jax.ShapeDtypeStruct((wide, rows), F32), jax.ShapeDtypeStruct(stat, F32)],
        compiler_params=params(),
        cost_estimate=pl.CostEstimate(
            flops=4 * rows * rows * wide,
            transcendentals=rows * rows * wide // DH,
            bytes_accessed=1 << 20,
        ),
        name="local",
    )(q, k, v)


def stats_of(block, wide, h):
    stats = block[wide:, :].astype(F32)
    at = 5 * h
    top = stats[at : at + 1] + stats[at + 1 : at + 2] + stats[at + 2 : at + 3]
    return top, stats[at + 3 : at + 4] + stats[at + 4 : at + 5]


def fold_kernel(zh_ref, got_ref, _, out_ref):
    peers, _, wide, rows = got_ref.shape
    wide = wide - STAT_ROWS
    stats = []
    for h in range(wide // DH):
        lines = slice(h * DH, (h + 1) * DH)
        pairs = [stats_of(got_ref[s, 0], wide, h) for s in range(peers)]
        top = functools.reduce(jnp.maximum, [t for t, _ in pairs])
        factors = [weight_of(t, top) for t, _ in pairs]
        total = sum(f * l for f, (_, l) in zip(factors, pairs))
        stats += split(top, 3) + split(total, 2)
        out_ref[lines, :] = sum(
            f * got_ref[s, 0, lines, :].astype(F32) for s, f in enumerate(factors)
        ).astype(BF)
    stats.append(jnp.zeros((STAT_ROWS - len(stats), rows), BF))
    out_ref[wide:, :] = jnp.concatenate([x.astype(F32) for x in stats], axis=0).astype(BF)


def fold(zh, got, after):
    peers, _, lines, rows = got.shape
    return pl.pallas_call(
        fold_kernel,
        grid_spec=pltpu.PrefetchScalarGridSpec(
            num_scalar_prefetch=1,
            grid=(1,),
            in_specs=[
                pl.BlockSpec((peers, 1, lines, rows), lambda i, zh_ref: (0, 1 - zh_ref[0], 0, 0)),
                pl.BlockSpec((BLOCK, DH), lambda i, zh_ref: (0, 0)),
            ],
            out_specs=whole((lines, rows)),
        ),
        out_shape=jax.ShapeDtypeStruct((lines, rows), BF),
        compiler_params=params(),
        cost_estimate=pl.CostEstimate(
            flops=2 * peers * rows * lines, transcendentals=0, bytes_accessed=1 << 20
        ),
        name="fold",
    )(zh, got, after)


def merge_kernel(zh_ref, got_ref, far_ref, near_ref, stat_ref, _, out_ref):
    peers, _, wide, rows = got_ref.shape
    wide = wide - STAT_ROWS
    heads = wide // DH
    for h in range(heads):
        lines = slice(h * DH, (h + 1) * DH)
        pairs = [stats_of(got_ref[s, 0], wide, h) for s in range(peers)]
        pairs.append(stats_of(far_ref[...], wide, h))
        pairs.append((stat_ref[h : h + 1, :], stat_ref[heads + h : heads + h + 1, :]))
        top = functools.reduce(jnp.maximum, [t for t, _ in pairs])
        factors = [weight_of(t, top) for t, _ in pairs]
        total = sum(f * l for f, (_, l) in zip(factors, pairs))
        factors = [f / total for f in factors]
        context = factors[-1] * near_ref[lines, :]
        context += factors[-2] * far_ref[lines, :].astype(F32)
        for s in range(peers):
            context += factors[s] * got_ref[s, 0, lines, :].astype(F32)
        context = context.T.astype(BF)
        for copy in range(out_ref.shape[0]):
            out_ref[copy, :, lines] = context


def merge(zh, got, far, near, stat, after, copies):
    peers, _, lines, rows = got.shape
    wide = lines - STAT_ROWS
    out = (copies, rows, wide)
    return pl.pallas_call(
        merge_kernel,
        grid_spec=pltpu.PrefetchScalarGridSpec(
            num_scalar_prefetch=1,
            grid=(1,),
            in_specs=[
                pl.BlockSpec((peers, 1, lines, rows), lambda i, zh_ref: (0, zh_ref[0], 0, 0)),
                whole(far.shape),
                whole(near.shape),
                whole(stat.shape),
                pl.BlockSpec((BLOCK, DH), lambda i, zh_ref: (0, 0)),
            ],
            out_specs=whole(out),
        ),
        out_shape=jax.ShapeDtypeStruct(out, BF),
        compiler_params=params(),
        cost_estimate=pl.CostEstimate(
            flops=MERGE_HINT, transcendentals=0, bytes_accessed=1 << 20
        ),
        name="merge",
    )(zh, got, far, near, stat, after)


def keep_kernel(where_ref, drop_ref, out_ref):
    rows, cols = out_ref.shape
    seed = where_ref[1] * 1000003 + where_ref[2] * cols
    inner = lax.broadcasted_iota(jnp.int32, (BLOCK, cols), 0) * D
    inner = inner + lax.broadcasted_iota(jnp.int32, (BLOCK, cols), 1) + seed
    for b in range(rows // BLOCK):
        hashed = inner + drop_ref[b]
        for _ in range(2):
            hashed = hashed ^ lax.shift_right_logical(hashed, jnp.int32(16))
            hashed = hashed * 73244475
        hashed = hashed ^ lax.shift_right_logical(hashed, jnp.int32(16))
        kept = (hashed & 1023) >= 102
        out_ref[b * BLOCK : (b + 1) * BLOCK, :] = jnp.where(
            kept, jnp.float32(1024.0 / 922.0), jnp.float32(0.0)
        )


def keep(where, drops, shape):
    return pl.pallas_call(
        keep_kernel,
        grid_spec=pltpu.PrefetchScalarGridSpec(
            num_scalar_prefetch=2, grid=(1,), in_specs=[], out_specs=whole(shape)
        ),
        out_shape=jax.ShapeDtypeStruct(shape, F32),
        compiler_params=params(),
        cost_estimate=pl.CostEstimate(
            flops=20 * shape[0] * shape[1], transcendentals=0, bytes_accessed=1 << 19
        ),
        name="keep",
    )(where, drops)


def project_kernel(where_ref, *refs):
    contexts, rest = refs[: 2 * PARTS], refs[2 * PARTS :]
    w_ref, keep_ref, res_ref, sum_ref, stat_ref, held_ref, sems = rest
    half, _, wide = contexts[0].shape
    copies = []
    for z in range(half):
        for shift in range(2):
            at = 2 * z + shift
            copies.append(
                pltpu.make_async_copy(
                    w_ref.at[2 * z + lax.rem(where_ref[0] + shift, 2)],
                    held_ref.at[at],
                    sems.at[at],
                )
            )
            copies[-1].start()
    acc = None
    for at, copy in enumerate(copies):
        copy.wait()
        for part in range(PARTS):
            z = at // 2
            slot = lax.rem(where_ref[2] // 2 + half - z, half) if part == 0 else z
            term = dot_t(
                contexts[2 * part + at % 2][slot],
                held_ref[at, :, part * wide : (part + 1) * wide],
            )
            acc = term if acc is None else acc + term
    rows, cols = acc.shape
    total = res_ref[...].astype(F32) + keep_ref[...] * acc
    sum_ref[...] = total
    mean = jnp.sum(total, axis=1, keepdims=True) * jnp.float32(1.0 / cols)
    dev = total - mean
    spread = jnp.sum(dev * dev, axis=1, keepdims=True)
    lane = lax.broadcasted_iota(jnp.int32, (rows, DH), 1)
    lines = jnp.where(lane == 0, mean, spread).T[:2, :]
    for copy in range(stat_ref.shape[0]):
        stat_ref[copy] = lines


def project(where, contexts, weight, kept, residual):
    rows, cols = residual.shape
    groups = weight.shape[0]
    args = list(contexts) + [weight, kept, residual]
    specs = [whole(x.shape) for x in args]
    specs[len(contexts)] = pl.BlockSpec(memory_space=pltpu.HBM)
    stat = (groups, 2, rows)
    return pl.pallas_call(
        project_kernel,
        grid_spec=pltpu.PrefetchScalarGridSpec(
            num_scalar_prefetch=1,
            grid=(1,),
            in_specs=specs,
            out_specs=[whole((rows, cols)), whole(stat)],
            scratch_shapes=[
                pltpu.VMEM(weight.shape, BF),
                pltpu.SemaphoreType.DMA((groups,)),
            ],
        ),
        out_shape=[
            jax.ShapeDtypeStruct((rows, cols), F32),
            jax.ShapeDtypeStruct(stat, F32),
        ],
        compiler_params=params(PROJECT_LIMIT << 20),
        cost_estimate=pl.CostEstimate(
            flops=2 * rows * D * cols, transcendentals=0, bytes_accessed=6 << 20
        ),
        name="project",
    )(where, *args)


def on_device(
    queries,
    key_rows,
    value_rows,
    residual,
    out_weight,
    norm_gain,
    norm_bias,
    global_list,
    random_device,
    random_offset,
    drop_seed,
    drop_offsets,
):
    row_count, width_here = queries.shape
    block_count = row_count // BLOCK
    n_y, n_x, n_zh = (lax.axis_size(a) for a in SEQ)
    plane = n_x * n_zh
    seq_count = n_y * plane
    n_zl = lax.axis_size("zl")
    tp_count = n_zl * lax.axis_size("core")
    tp_at = lax.axis_index(TP)
    cols_here = out_weight.shape[1]

    plane_at = lax.axis_index(PLANE)
    y_at = lax.axis_index("y")
    zh_at = lax.axis_index("zh")
    wide = width_here // PARTS

    paired = jnp.concatenate([key_rows, value_rows], axis=1)
    pool = lax.all_gather(paired, "y", axis=0, tiled=True)

    def moves(flip):
        return [
            ((y * plane + p) * tp_count + t, (t * plane + (p ^ flip)) * tp_count + y)
            for y in range(n_y)
            for p in range(plane)
            for t in range(tp_count)
        ]

    same_zh = lax.ppermute(out_weight.T, SEQ + TP, moves(0))
    other_zh = lax.ppermute(out_weight.T, SEQ + TP, moves(1))
    shards = jnp.concatenate(
        [
            jnp.where(zh_at == 0, same_zh, other_zh),
            jnp.where(zh_at == 0, other_zh, same_zh),
        ],
        axis=0,
    )

    request_count = block_count * RAND
    target = random_device.reshape(request_count)
    wanted = random_offset.reshape(request_count)
    rank = jnp.arange(request_count, dtype=jnp.int32)
    same = target[:, None] == target[None, :]
    earlier = rank[None, :] < rank[:, None]
    slot = jnp.sum(jnp.logical_and(same, earlier), axis=1).astype(jnp.int32)
    slots = n_y * CAP
    place = (target // plane) * CAP + slot
    column = target % plane
    entry = column * (2 * slots) + place
    cells = jnp.arange(plane * 2 * slots, dtype=jnp.int32)
    is_offset = entry[:, None] == cells[None, :]
    is_asker = entry[:, None] + slots == cells[None, :]
    asker = rank // RAND + 1
    table = jnp.sum(
        jnp.where(is_offset, wanted[:, None], jnp.where(is_asker, asker[:, None], 0)), axis=0
    )
    table = jnp.pad(table.astype(BF)[None], ((0, 7), (0, width_here - cells.shape[0])))

    flip = [(0, 1), (1, 0)]

    def over_x(x):
        x = jnp.broadcast_to(x[None], (n_x,) + x.shape)
        return lax.all_to_all(x, "x", split_axis=0, concat_axis=0, tiled=True)

    near_q = jnp.concatenate([queries, table], axis=0)
    far_q = jnp.concatenate(
        [lax.ppermute(queries, "zh", flip), lax.ppermute(table, "zh", flip)], axis=0
    )
    asked = over_x(jnp.stack([near_q, far_q]))
    after = asked[0, 0, row_count, 0] * 0
    shards = over_x(shards + after)
    weight = lax.all_gather(
        shards.reshape(plane * cols_here, width_here), "y", axis=0, tiled=True
    )
    weight = weight.reshape(tp_count, plane * cols_here, width_here)

    lists = asked[:, :, row_count, : cells.shape[0]].reshape(plane, plane, 2 * slots)
    lists = lax.dynamic_index_in_dim(lists, plane_at, 1, keepdims=False).astype(jnp.int32)
    base = (jnp.arange(slots, dtype=jnp.int32) // CAP) * block_count
    order = jnp.arange(plane, dtype=jnp.int32)
    peer = jnp.bitwise_xor(order, zh_at)
    nothing = jnp.int32(block_count)
    owner = global_list // block_count
    glob_row = (owner // plane) * block_count + global_list % block_count
    glob_mark = jnp.where(owner % plane == plane_at, -1, nothing)
    here = y_at * plane + peer
    low = (here + seq_count - 1) % seq_count
    high = (here + 1) % seq_count
    low_row = (low // plane) * block_count + block_count - 1
    high_row = (high // plane) * block_count
    low_mark = jnp.where(low % plane == plane_at, 0, nothing)
    high_mark = jnp.where(high % plane == plane_at, block_count - 1, nothing)
    marks = lists[:, slots:] - 1
    row = jnp.concatenate(
        [
            lists[:, :slots] + base[None],
            jnp.broadcast_to(glob_row[None], (plane, GLOB)),
            low_row[:, None],
            high_row[:, None],
        ],
        axis=1,
    ).reshape(-1)
    mark = jnp.concatenate(
        [
            jnp.where(marks < 0, nothing, marks),
            jnp.broadcast_to(glob_mark[None], (plane, GLOB)),
            low_mark[:, None],
            high_mark[:, None],
        ],
        axis=1,
    ).reshape(-1)
    zh = zh_at[None].astype(jnp.int32)

    near = [local(part, queries, key_rows, value_rows) for part in range(PARTS)]
    where = jnp.stack([tp_at % 2, drop_seed[0], tp_at]).astype(jnp.int32)
    kept = keep(where, drop_offsets, residual.shape)
    folded, gone = [], []
    for part in range(PARTS):
        partials = serve(part, row, mark, zh, asked, pool, row_count)
        partials = partials.reshape((n_x, 2) + partials.shape[1:])
        got = lax.all_to_all(partials, "x", split_axis=0, concat_axis=0, tiled=True)
        gone.append(fold(zh, got, kept))
        folded.append((got, lax.ppermute(gone[part], "zh", flip)))
    contexts = []
    for part in range(PARTS):
        copies = n_zl if part else 1
        context = merge(zh, *folded[part], *near[part], gone[1 - part], copies)
        if part:
            mine = lax.all_to_all(context, "zl", split_axis=0, concat_axis=0, tiled=True)
        else:
            shifted = [
                lax.ppermute(context, "zl", [(z, (z + by) % n_zl) for z in range(n_zl)])
                for by in range(1, n_zl)
            ]
            mine = jnp.concatenate([context] + shifted, axis=0)
        contexts += [mine, lax.ppermute(mine, "core", flip)]
    summed, stats = project(where, contexts, weight, kept, residual)
    stats = lax.all_to_all(stats, TP, split_axis=0, concat_axis=0, tiled=True)
    means, spreads = stats[:, 0], stats[:, 1]
    mean = jnp.sum(means, axis=0) / tp_count
    away = means - mean[None]
    cols = summed.shape[1]
    spread = jnp.sum(spreads, axis=0) + cols * jnp.sum(away * away, axis=0)
    factor = lax.rsqrt(spread / D + 1e-05)
    encoded = (summed - mean[:, None]) * factor[:, None] * norm_gain[None] + norm_bias[None]
    return encoded.astype(BF)


def solution(mesh):
    fine = Mesh(mesh.devices.reshape(8, 4, 2, 4, 2), SEQ + TP)
    placed = (
        P(SEQ, TP),
        P(SEQ, TP),
        P(SEQ, TP),
        P(SEQ, TP),
        P(TP, SEQ),
        P(TP),
        P(TP),
        P(),
        P(SEQ, None),
        P(SEQ, None),
        P(),
        P(SEQ),
    )
    return jax.shard_map(
        on_device, mesh=fine, in_specs=placed, out_specs=P(SEQ, TP), check_vma=False
    )
```

```python
import functools
import math

import jax
import jax.numpy as jnp
from jax import lax
from jax.experimental import pallas as pl
from jax.experimental.pallas import tpu as pltpu
from jax.sharding import Mesh
from jax.sharding import PartitionSpec as P

D = 4096
DH = 128
BLOCK = 16
GLOB = 2
RAND = 3
CAP = 2
BF = jnp.bfloat16
F32 = jnp.float32
SEQ = ("y", "x", "zh")
TP = ("zl", "core")
PLANE = ("x", "zh")
PARTS = 2
PROJECT_LIMIT = 48
STAT_ROWS = 16
NEG = -1e30
EMPTY = -1e20
MERGE_HINT = 30_000_000_000
VMEM_LIMIT = 48 * 1024 * 1024


def whole(shape):
    return pl.BlockSpec(shape, lambda *a: (0,) * len(shape))


def params(limit=VMEM_LIMIT):
    return pltpu.CompilerParams(vmem_limit_bytes=limit)


def partial(scores, listed, values):
    scores = jnp.where(listed, scores, NEG)
    top = jnp.maximum(jnp.max(scores, axis=0, keepdims=True), EMPTY)
    expo = weight_of(scores, top)
    total = jnp.sum(expo, axis=0, keepdims=True)
    got = lax.dot_general(
        values, expo.astype(BF), (((0,), (0,)), ((), ())), preferred_element_type=F32
    )
    return top, total, got


def weight_of(score, top):
    return jnp.exp2((score - top) * jnp.float32(math.log2(math.e) / DH**0.5))


def dot_t(a, b):
    return lax.dot_general(a, b, (((1,), (1,)), ((), ())), preferred_element_type=F32)


def split(x, parts):
    out = []
    for _ in range(parts):
        out.append(x.astype(BF))
        x = x - out[-1].astype(F32)
    return out


def serve_kernel(value_at, row_ref, mark_ref, zh_ref, q_ref, pool_ref, out_ref):
    n_x, n_zh, rows, wide = q_ref.shape
    listings = row_ref.shape[0] // (pl.num_programs(0) * n_x * n_zh)
    block_of = lax.broadcasted_iota(jnp.int32, (BLOCK, rows), 1) // BLOCK
    jobs = []
    for x in range(n_x):
        for j in range(n_zh):
            peer = (pl.program_id(0) * n_x + x) * n_zh + j
            places, listed = [], []
            for i in range(listings):
                at = peer * listings + i
                places.append(row_ref[at] * BLOCK)
                mark = mark_ref[at]
                listed.append(
                    jnp.logical_or(block_of == mark, jnp.full(block_of.shape, mark) < 0)
                )
            listed = jnp.concatenate(listed, axis=0)
            jobs += [(x, j, h, places, listed) for h in range(wide // DH)]

    def taken(places, shift, lanes):
        blocks = [pl.ds(pl.multiple_of(p + shift, BLOCK), BLOCK) for p in places]
        return jnp.concatenate([pool_ref[b, lanes] for b in blocks], axis=0)

    def scores(x, j, h, places, listed):
        lanes = slice(h * DH, (h + 1) * DH)
        return dot_t(taken(places, 0, lanes), q_ref[x, j, :, lanes])

    stats = []
    coming = scores(*jobs[0])
    for k, (x, j, h, places, listed) in enumerate(jobs):
        now = coming
        if k + 1 < len(jobs):
            coming = scores(*jobs[k + 1])
        lanes = slice(h * DH, (h + 1) * DH)
        top, total, got = partial(now, listed, taken(places, value_at, lanes))
        peer = x * n_zh + lax.rem(j + zh_ref[0], n_zh)
        out_ref[peer, lanes, :] = got.astype(BF)
        stats += split(top, 3) + split(total, 2)
        if (h + 1) * DH == wide:
            stats.append(jnp.zeros((STAT_ROWS - len(stats), rows), BF))
            stats = jnp.concatenate([line.astype(F32) for line in stats], axis=0)
            out_ref[peer, wide:, :] = stats.astype(BF)
            stats = []


def serve(part, row, mark, zh, q, pool, out_rows):
    n_x = q.shape[0]
    wide = q.shape[3] // PARTS
    rows = out_rows
    peers = 2 * n_x
    out = (peers, wide + STAT_ROWS, rows)
    steps = n_x // 2
    return pl.pallas_call(
        functools.partial(serve_kernel, rows),
        grid_spec=pltpu.PrefetchScalarGridSpec(
            num_scalar_prefetch=3,
            grid=(steps,),
            in_specs=[
                pl.BlockSpec((n_x // steps, 2, rows, wide), lambda i, a, b, c: (i, 0, 0, part)),
                pl.BlockSpec((pool.shape[0], wide), lambda i, a, b, c: (0, part)),
            ],
            out_specs=pl.BlockSpec((peers // steps,) + out[1:], lambda i, a, b, c: (i, 0, 0)),
        ),
        out_shape=jax.ShapeDtypeStruct(out, BF),
        compiler_params=params(56 << 20),
        cost_estimate=pl.CostEstimate(
            flops=4 * peers * rows * 320 * wide,
            transcendentals=peers * rows * 320 * wide // DH,
            bytes_accessed=4 << 20,
        ),
        name="serve",
    )(row, mark, zh, q, pool)


def local_kernel(q_ref, k_ref, v_ref, out_ref, stat_ref):
    rows = q_ref.shape[0]
    heads = q_ref.shape[1] // DH
    key_block = lax.broadcasted_iota(jnp.int32, (rows, rows), 0) // BLOCK
    query_block = lax.broadcasted_iota(jnp.int32, (rows, rows), 1) // BLOCK
    listed = jnp.abs(key_block - query_block) <= 1
    tops, totals = [], []
    for h in range(heads):
        lanes = slice(h * DH, (h + 1) * DH)
        top, total, got = partial(
            dot_t(k_ref[:, lanes], q_ref[:, lanes]), listed, v_ref[:, lanes]
        )
        out_ref[lanes, :] = got
        tops.append(top)
        totals.append(total)
    stat_ref[...] = jnp.concatenate(tops + totals, axis=0)


def local(part, q, k, v):
    rows = q.shape[0]
    wide = q.shape[1] // PARTS
    stat = (2 * (wide // DH), rows)
    return pl.pallas_call(
        local_kernel,
        grid=(1,),
        in_specs=[pl.BlockSpec((rows, wide), lambda i: (0, part))] * 3,
        out_specs=[whole((wide, rows)), whole(stat)],
        out_shape=[jax.ShapeDtypeStruct((wide, rows), F32), jax.ShapeDtypeStruct(stat, F32)],
        compiler_params=params(),
        cost_estimate=pl.CostEstimate(
            flops=4 * rows * rows * wide,
            transcendentals=rows * rows * wide // DH,
            bytes_accessed=1 << 20,
        ),
        name="local",
    )(q, k, v)


def stats_of(block, wide, h):
    stats = block[wide:, :].astype(F32)
    at = 5 * h
    top = stats[at : at + 1] + stats[at + 1 : at + 2] + stats[at + 2 : at + 3]
    return top, stats[at + 3 : at + 4] + stats[at + 4 : at + 5]


def fold_kernel(zh_ref, got_ref, _, out_ref):
    peers, _, wide, rows = got_ref.shape
    wide = wide - STAT_ROWS
    stats = []
    for h in range(wide // DH):
        lines = slice(h * DH, (h + 1) * DH)
        pairs = [stats_of(got_ref[s, 0], wide, h) for s in range(peers)]
        top = functools.reduce(jnp.maximum, [t for t, _ in pairs])
        factors = [weight_of(t, top) for t, _ in pairs]
        total = sum(f * l for f, (_, l) in zip(factors, pairs))
        stats += split(top, 3) + split(total, 2)
        out_ref[lines, :] = sum(
            f * got_ref[s, 0, lines, :].astype(F32) for s, f in enumerate(factors)
        ).astype(BF)
    stats.append(jnp.zeros((STAT_ROWS - len(stats), rows), BF))
    out_ref[wide:, :] = jnp.concatenate([x.astype(F32) for x in stats], axis=0).astype(BF)


def fold(zh, got, after):
    peers, _, lines, rows = got.shape
    return pl.pallas_call(
        fold_kernel,
        grid_spec=pltpu.PrefetchScalarGridSpec(
            num_scalar_prefetch=1,
            grid=(1,),
            in_specs=[
                pl.BlockSpec((peers, 1, lines, rows), lambda i, zh_ref: (0, 1 - zh_ref[0], 0, 0)),
                pl.BlockSpec((BLOCK, DH), lambda i, zh_ref: (0, 0)),
            ],
            out_specs=whole((lines, rows)),
        ),
        out_shape=jax.ShapeDtypeStruct((lines, rows), BF),
        compiler_params=params(),
        cost_estimate=pl.CostEstimate(
            flops=2 * peers * rows * lines, transcendentals=0, bytes_accessed=1 << 20
        ),
        name="fold",
    )(zh, got, after)


def merge_kernel(zh_ref, got_ref, far_ref, near_ref, stat_ref, _, out_ref):
    peers, _, wide, rows = got_ref.shape
    wide = wide - STAT_ROWS
    heads = wide // DH
    for h in range(heads):
        lines = slice(h * DH, (h + 1) * DH)
        pairs = [stats_of(got_ref[s, 0], wide, h) for s in range(peers)]
        pairs.append(stats_of(far_ref[...], wide, h))
        pairs.append((stat_ref[h : h + 1, :], stat_ref[heads + h : heads + h + 1, :]))
        top = functools.reduce(jnp.maximum, [t for t, _ in pairs])
        factors = [weight_of(t, top) for t, _ in pairs]
        total = sum(f * l for f, (_, l) in zip(factors, pairs))
        factors = [f / total for f in factors]
        context = factors[-1] * near_ref[lines, :]
        context += factors[-2] * far_ref[lines, :].astype(F32)
        for s in range(peers):
            context += factors[s] * got_ref[s, 0, lines, :].astype(F32)
        context = context.T.astype(BF)
        for copy in range(out_ref.shape[0]):
            out_ref[copy, :, lines] = context


def merge(zh, got, far, near, stat, after, copies):
    peers, _, lines, rows = got.shape
    wide = lines - STAT_ROWS
    out = (copies, rows, wide)
    return pl.pallas_call(
        merge_kernel,
        grid_spec=pltpu.PrefetchScalarGridSpec(
            num_scalar_prefetch=1,
            grid=(1,),
            in_specs=[
                pl.BlockSpec((peers, 1, lines, rows), lambda i, zh_ref: (0, zh_ref[0], 0, 0)),
                whole(far.shape),
                whole(near.shape),
                whole(stat.shape),
                pl.BlockSpec((BLOCK, DH), lambda i, zh_ref: (0, 0)),
            ],
            out_specs=whole(out),
        ),
        out_shape=jax.ShapeDtypeStruct(out, BF),
        compiler_params=params(),
        cost_estimate=pl.CostEstimate(
            flops=MERGE_HINT, transcendentals=0, bytes_accessed=1 << 20
        ),
        name="merge",
    )(zh, got, far, near, stat, after)


def keep_kernel(where_ref, drop_ref, out_ref):
    rows, cols = out_ref.shape
    seed = where_ref[1] * 1000003 + where_ref[2] * cols
    inner = lax.broadcasted_iota(jnp.int32, (BLOCK, cols), 0) * D
    inner = inner + lax.broadcasted_iota(jnp.int32, (BLOCK, cols), 1) + seed
    for b in range(rows // BLOCK):
        hashed = inner + drop_ref[b]
        for _ in range(2):
            hashed = hashed ^ lax.shift_right_logical(hashed, jnp.int32(16))
            hashed = hashed * 73244475
        hashed = hashed ^ lax.shift_right_logical(hashed, jnp.int32(16))
        kept = (hashed & 1023) >= 102
        out_ref[b * BLOCK : (b + 1) * BLOCK, :] = jnp.where(
            kept, jnp.float32(1024.0 / 922.0), jnp.float32(0.0)
        )


def keep(where, drops, shape):
    return pl.pallas_call(
        keep_kernel,
        grid_spec=pltpu.PrefetchScalarGridSpec(
            num_scalar_prefetch=2, grid=(1,), in_specs=[], out_specs=whole(shape)
        ),
        out_shape=jax.ShapeDtypeStruct(shape, F32),
        compiler_params=params(),
        cost_estimate=pl.CostEstimate(
            flops=20 * shape[0] * shape[1], transcendentals=0, bytes_accessed=1 << 19
        ),
        name="keep",
    )(where, drops)


def project_kernel(where_ref, *refs):
    contexts, rest = refs[: 2 * PARTS], refs[2 * PARTS :]
    w_ref, keep_ref, res_ref, sum_ref, stat_ref, held_ref, sems = rest
    half, _, wide = contexts[0].shape
    copies = []
    for z in range(half):
        for shift in range(2):
            at = 2 * z + shift
            copies.append(
                pltpu.make_async_copy(
                    w_ref.at[2 * z + lax.rem(where_ref[0] + shift, 2)],
                    held_ref.at[at],
                    sems.at[at],
                )
            )
            copies[-1].start()
    acc = None
    for at, copy in enumerate(copies):
        copy.wait()
        for part in range(PARTS):
            z = at // 2
            slot = lax.rem(where_ref[2] // 2 + half - z, half) if part == 0 else z
            term = dot_t(
                contexts[2 * part + at % 2][slot],
                held_ref[at, :, part * wide : (part + 1) * wide],
            )
            acc = term if acc is None else acc + term
    rows, cols = acc.shape
    total = res_ref[...].astype(F32) + keep_ref[...] * acc
    sum_ref[...] = total
    mean = jnp.sum(total, axis=1, keepdims=True) * jnp.float32(1.0 / cols)
    dev = total - mean
    spread = jnp.sum(dev * dev, axis=1, keepdims=True)
    lane = lax.broadcasted_iota(jnp.int32, (rows, DH), 1)
    lines = jnp.where(lane == 0, mean, spread).T[:2, :]
    for copy in range(stat_ref.shape[0]):
        stat_ref[copy] = lines


def project(where, contexts, weight, kept, residual):
    rows, cols = residual.shape
    groups = weight.shape[0]
    args = list(contexts) + [weight, kept, residual]
    specs = [whole(x.shape) for x in args]
    specs[len(contexts)] = pl.BlockSpec(memory_space=pltpu.HBM)
    stat = (groups, 2, rows)
    return pl.pallas_call(
        project_kernel,
        grid_spec=pltpu.PrefetchScalarGridSpec(
            num_scalar_prefetch=1,
            grid=(1,),
            in_specs=specs,
            out_specs=[whole((rows, cols)), whole(stat)],
            scratch_shapes=[
                pltpu.VMEM(weight.shape, BF),
                pltpu.SemaphoreType.DMA((groups,)),
            ],
        ),
        out_shape=[
            jax.ShapeDtypeStruct((rows, cols), F32),
            jax.ShapeDtypeStruct(stat, F32),
        ],
        compiler_params=params(PROJECT_LIMIT << 20),
        cost_estimate=pl.CostEstimate(
            flops=2 * rows * D * cols, transcendentals=0, bytes_accessed=6 << 20
        ),
        name="project",
    )(where, *args)


def on_device(
    queries,
    key_rows,
    value_rows,
    residual,
    out_weight,
    norm_gain,
    norm_bias,
    global_list,
    random_device,
    random_offset,
    drop_seed,
    drop_offsets,
):
    row_count, width_here = queries.shape
    block_count = row_count // BLOCK
    n_y, n_x, n_zh = (lax.axis_size(a) for a in SEQ)
    plane = n_x * n_zh
    seq_count = n_y * plane
    n_zl = lax.axis_size("zl")
    tp_count = n_zl * lax.axis_size("core")
    tp_at = lax.axis_index(TP)
    cols_here = out_weight.shape[1]

    plane_at = lax.axis_index(PLANE)
    y_at = lax.axis_index("y")
    zh_at = lax.axis_index("zh")
    wide = width_here // PARTS

    pool = lax.all_gather(jnp.stack([key_rows, value_rows]), "y", axis=0, tiled=True)
    pool = pool.reshape(n_y * 2 * row_count, width_here)

    def moves(flip):
        return [
            ((y * plane + p) * tp_count + t, (t * plane + (p ^ flip)) * tp_count + y)
            for y in range(n_y)
            for p in range(plane)
            for t in range(tp_count)
        ]

    same_zh = lax.ppermute(out_weight.T, SEQ + TP, moves(0))
    other_zh = lax.ppermute(out_weight.T, SEQ + TP, moves(1))
    shards = jnp.concatenate(
        [
            jnp.where(zh_at == 0, same_zh, other_zh),
            jnp.where(zh_at == 0, other_zh, same_zh),
        ],
        axis=0,
    )

    request_count = block_count * RAND
    target = random_device.reshape(request_count)
    wanted = random_offset.reshape(request_count)
    rank = jnp.arange(request_count, dtype=jnp.int32)
    same = target[:, None] == target[None, :]
    earlier = rank[None, :] < rank[:, None]
    slot = jnp.sum(jnp.logical_and(same, earlier), axis=1).astype(jnp.int32)
    slots = n_y * CAP
    place = (target // plane) * CAP + slot
    column = target % plane
    entry = column * (2 * slots) + place
    cells = jnp.arange(plane * 2 * slots, dtype=jnp.int32)
    is_offset = entry[:, None] == cells[None, :]
    is_asker = entry[:, None] + slots == cells[None, :]
    asker = rank // RAND + 1
    table = jnp.sum(
        jnp.where(is_offset, wanted[:, None], jnp.where(is_asker, asker[:, None], 0)), axis=0
    )
    table = jnp.pad(table.astype(BF)[None], ((0, 7), (0, width_here - cells.shape[0])))

    flip = [(0, 1), (1, 0)]

    def over_x(x):
        x = jnp.broadcast_to(x[None], (n_x,) + x.shape)
        return lax.all_to_all(x, "x", split_axis=0, concat_axis=0, tiled=True)

    near_q = jnp.concatenate([queries, table], axis=0)
    far_q = jnp.concatenate(
        [lax.ppermute(queries, "zh", flip), lax.ppermute(table, "zh", flip)], axis=0
    )
    asked = over_x(jnp.stack([near_q, far_q]))
    after = asked[0, 0, row_count, 0] * 0
    shards = over_x(shards + after)
    shards = shards.reshape(plane * cols_here, width_here)
    weight = lax.all_gather(shards, "y", axis=0, tiled=True)

    lists = asked[:, :, row_count, : cells.shape[0]].reshape(plane, plane, 2 * slots)
    lists = lax.dynamic_index_in_dim(lists, plane_at, 1, keepdims=False).astype(jnp.int32)
    base = (jnp.arange(slots, dtype=jnp.int32) // CAP) * (2 * block_count)
    order = jnp.arange(plane, dtype=jnp.int32)
    peer = jnp.bitwise_xor(order, zh_at)
    nothing = jnp.int32(block_count)
    owner = global_list // block_count
    glob_row = (owner // plane) * (2 * block_count) + global_list % block_count
    glob_mark = jnp.where(owner % plane == plane_at, -1, nothing)
    here = y_at * plane + peer
    low = (here + seq_count - 1) % seq_count
    high = (here + 1) % seq_count
    low_row = (low // plane) * (2 * block_count) + block_count - 1
    high_row = (high // plane) * (2 * block_count)
    low_mark = jnp.where(low % plane == plane_at, 0, nothing)
    high_mark = jnp.where(high % plane == plane_at, block_count - 1, nothing)
    marks = lists[:, slots:] - 1
    row = jnp.concatenate(
        [
            lists[:, :slots] + base[None],
            jnp.broadcast_to(glob_row[None], (plane, GLOB)),
            low_row[:, None],
            high_row[:, None],
        ],
        axis=1,
    ).reshape(-1)
    mark = jnp.concatenate(
        [
            jnp.where(marks < 0, nothing, marks),
            jnp.broadcast_to(glob_mark[None], (plane, GLOB)),
            low_mark[:, None],
            high_mark[:, None],
        ],
        axis=1,
    ).reshape(-1)
    zh = zh_at[None].astype(jnp.int32)

    near = [local(part, queries, key_rows, value_rows) for part in range(PARTS)]
    where = jnp.stack([tp_at % 2, drop_seed[0], tp_at]).astype(jnp.int32)
    kept = keep(where, drop_offsets, residual.shape)
    folded, gone = [], []
    for part in range(PARTS):
        partials = serve(part, row, mark, zh, asked, pool, row_count)
        partials = partials.reshape((n_x, 2) + partials.shape[1:])
        got = lax.all_to_all(partials, "x", split_axis=0, concat_axis=0, tiled=True)
        gone.append(fold(zh, got, kept))
        folded.append((got, lax.ppermute(gone[part], "zh", flip)))
    contexts = []
    for part in range(PARTS):
        copies = n_zl if part else 1
        context = merge(zh, *folded[part], *near[part], (weight, gone[0])[part], copies)
        if part:
            mine = lax.all_to_all(context, "zl", split_axis=0, concat_axis=0, tiled=True)
        else:
            shifted = [
                lax.ppermute(context, "zl", [(z, (z + by) % n_zl) for z in range(n_zl)])
                for by in range(1, n_zl)
            ]
            mine = jnp.concatenate([context] + shifted, axis=0)
        contexts += [mine, lax.ppermute(mine, "core", flip)]
    summed, stats = project(where, contexts, weight.reshape(tp_count, -1, width_here), kept, residual)
    stats = lax.all_to_all(stats, TP, split_axis=0, concat_axis=0, tiled=True)
    means, spreads = stats[:, 0], stats[:, 1]
    mean = jnp.sum(means, axis=0) / tp_count
    away = means - mean[None]
    cols = summed.shape[1]
    spread = jnp.sum(spreads, axis=0) + cols * jnp.sum(away * away, axis=0)
    factor = lax.rsqrt(spread / D + 1e-05)
    encoded = (summed - mean[:, None]) * factor[:, None] * norm_gain[None] + norm_bias[None]
    return encoded.astype(BF)


def solution(mesh):
    fine = Mesh(mesh.devices.reshape(8, 4, 2, 4, 2), SEQ + TP)
    placed = (
        P(SEQ, TP),
        P(SEQ, TP),
        P(SEQ, TP),
        P(SEQ, TP),
        P(TP, SEQ),
        P(TP),
        P(TP),
        P(),
        P(SEQ, None),
        P(SEQ, None),
        P(),
        P(SEQ),
    )
    return jax.shard_map(
        on_device, mesh=fine, in_specs=placed, out_specs=P(SEQ, TP), check_vma=False
    )
```

```python
import functools
import math

import jax
import jax.numpy as jnp
from jax import lax
from jax.experimental import pallas as pl
from jax.experimental.pallas import tpu as pltpu
from jax.sharding import Mesh
from jax.sharding import PartitionSpec as P

D = 4096
DH = 128
BLOCK = 16
GLOB = 2
RAND = 3
CAP = 2
BF = jnp.bfloat16
F32 = jnp.float32
SEQ = ("y", "x", "zh")
TP = ("zl", "core")
PLANE = ("x", "zh")
PARTS = 2
PROJECT_LIMIT = 48
STAT_ROWS = 16
NEG = -1e30
EMPTY = -1e20
MERGE_HINT = 30_000_000_000
VMEM_LIMIT = 48 * 1024 * 1024


def whole(shape):
    return pl.BlockSpec(shape, lambda *a: (0,) * len(shape))


def params(limit=VMEM_LIMIT):
    return pltpu.CompilerParams(vmem_limit_bytes=limit)


def partial(scores, listed, values):
    scores = jnp.where(listed, scores, NEG)
    top = jnp.maximum(jnp.max(scores, axis=0, keepdims=True), EMPTY)
    expo = weight_of(scores, top)
    total = jnp.sum(expo, axis=0, keepdims=True)
    got = lax.dot_general(
        values, expo.astype(BF), (((0,), (0,)), ((), ())), preferred_element_type=F32
    )
    return top, total, got


def weight_of(score, top):
    return jnp.exp2((score - top) * jnp.float32(math.log2(math.e) / DH**0.5))


def dot_t(a, b):
    return lax.dot_general(a, b, (((1,), (1,)), ((), ())), preferred_element_type=F32)


def split(x, parts):
    out = []
    for _ in range(parts):
        out.append(x.astype(BF))
        x = x - out[-1].astype(F32)
    return out


def serve_kernel(value_at, row_ref, mark_ref, zh_ref, q_ref, pool_ref, out_ref):
    n_x, n_zh, rows, wide = q_ref.shape
    listings = row_ref.shape[0] // (pl.num_programs(0) * n_x * n_zh)
    block_of = lax.broadcasted_iota(jnp.int32, (BLOCK, rows), 1) // BLOCK
    jobs = []
    for x in range(n_x):
        for j in range(n_zh):
            peer = (pl.program_id(0) * n_x + x) * n_zh + j
            places, listed = [], []
            for i in range(listings):
                at = peer * listings + i
                places.append(row_ref[at] * BLOCK)
                mark = mark_ref[at]
                listed.append(
                    jnp.logical_or(block_of == mark, jnp.full(block_of.shape, mark) < 0)
                )
            listed = jnp.concatenate(listed, axis=0)
            jobs += [(x, j, h, places, listed) for h in range(wide // DH)]

    def taken(places, shift, lanes):
        blocks = [pl.ds(pl.multiple_of(p + shift, BLOCK), BLOCK) for p in places]
        return jnp.concatenate([pool_ref[b, lanes] for b in blocks], axis=0)

    def scores(x, j, h, places, listed):
        lanes = slice(h * DH, (h + 1) * DH)
        return dot_t(taken(places, 0, lanes), q_ref[x, j, :, lanes])

    stats = []
    coming = scores(*jobs[0])
    for k, (x, j, h, places, listed) in enumerate(jobs):
        now = coming
        if k + 1 < len(jobs):
            coming = scores(*jobs[k + 1])
        lanes = slice(h * DH, (h + 1) * DH)
        top, total, got = partial(now, listed, taken(places, value_at, lanes))
        peer = x * n_zh + lax.rem(j + zh_ref[0], n_zh)
        out_ref[peer, lanes, :] = got.astype(BF)
        stats += split(top, 3) + split(total, 2)
        if (h + 1) * DH == wide:
            stats.append(jnp.zeros((STAT_ROWS - len(stats), rows), BF))
            stats = jnp.concatenate([line.astype(F32) for line in stats], axis=0)
            out_ref[peer, wide:, :] = stats.astype(BF)
            stats = []


def serve(part, row, mark, zh, q, pool, out_rows):
    n_x = q.shape[0]
    wide = q.shape[3] // PARTS
    rows = out_rows
    peers = 2 * n_x
    out = (peers, wide + STAT_ROWS, rows)
    steps = n_x // 2
    return pl.pallas_call(
        functools.partial(serve_kernel, rows),
        grid_spec=pltpu.PrefetchScalarGridSpec(
            num_scalar_prefetch=3,
            grid=(steps,),
            in_specs=[
                pl.BlockSpec((n_x // steps, 2, rows, wide), lambda i, a, b, c: (i, 0, 0, part)),
                pl.BlockSpec((pool.shape[0], wide), lambda i, a, b, c: (0, part)),
            ],
            out_specs=pl.BlockSpec((peers // steps,) + out[1:], lambda i, a, b, c: (i, 0, 0)),
        ),
        out_shape=jax.ShapeDtypeStruct(out, BF),
        compiler_params=params(56 << 20),
        cost_estimate=pl.CostEstimate(
            flops=4 * peers * rows * 320 * wide,
            transcendentals=peers * rows * 320 * wide // DH,
            bytes_accessed=4 << 20,
        ),
        name="serve",
    )(row, mark, zh, q, pool)


def local_kernel(q_ref, k_ref, v_ref, out_ref, stat_ref):
    rows = q_ref.shape[0]
    heads = q_ref.shape[1] // DH
    key_block = lax.broadcasted_iota(jnp.int32, (rows, rows), 0) // BLOCK
    query_block = lax.broadcasted_iota(jnp.int32, (rows, rows), 1) // BLOCK
    listed = jnp.abs(key_block - query_block) <= 1
    tops, totals = [], []
    for h in range(heads):
        lanes = slice(h * DH, (h + 1) * DH)
        top, total, got = partial(
            dot_t(k_ref[:, lanes], q_ref[:, lanes]), listed, v_ref[:, lanes]
        )
        out_ref[lanes, :] = got
        tops.append(top)
        totals.append(total)
    stat_ref[...] = jnp.concatenate(tops + totals, axis=0)


def local(part, q, k, v):
    rows = q.shape[0]
    wide = q.shape[1] // PARTS
    stat = (2 * (wide // DH), rows)
    return pl.pallas_call(
        local_kernel,
        grid=(1,),
        in_specs=[pl.BlockSpec((rows, wide), lambda i: (0, part))] * 3,
        out_specs=[whole((wide, rows)), whole(stat)],
        out_shape=[jax.ShapeDtypeStruct((wide, rows), F32), jax.ShapeDtypeStruct(stat, F32)],
        compiler_params=params(),
        cost_estimate=pl.CostEstimate(
            flops=4 * rows * rows * wide,
            transcendentals=rows * rows * wide // DH,
            bytes_accessed=1 << 20,
        ),
        name="local",
    )(q, k, v)


def stats_of(block, wide, h):
    stats = block[wide:, :].astype(F32)
    at = 5 * h
    top = stats[at : at + 1] + stats[at + 1 : at + 2] + stats[at + 2 : at + 3]
    return top, stats[at + 3 : at + 4] + stats[at + 4 : at + 5]


def fold_kernel(zh_ref, got_ref, _, out_ref):
    peers, _, wide, rows = got_ref.shape
    wide = wide - STAT_ROWS
    stats = []
    for h in range(wide // DH):
        lines = slice(h * DH, (h + 1) * DH)
        pairs = [stats_of(got_ref[s, 0], wide, h) for s in range(peers)]
        top = functools.reduce(jnp.maximum, [t for t, _ in pairs])
        factors = [weight_of(t, top) for t, _ in pairs]
        total = sum(f * l for f, (_, l) in zip(factors, pairs))
        stats += split(top, 3) + split(total, 2)
        out_ref[lines, :] = sum(
            f * got_ref[s, 0, lines, :].astype(F32) for s, f in enumerate(factors)
        ).astype(BF)
    stats.append(jnp.zeros((STAT_ROWS - len(stats), rows), BF))
    out_ref[wide:, :] = jnp.concatenate([x.astype(F32) for x in stats], axis=0).astype(BF)


def fold(zh, got, after):
    peers, _, lines, rows = got.shape
    return pl.pallas_call(
        fold_kernel,
        grid_spec=pltpu.PrefetchScalarGridSpec(
            num_scalar_prefetch=1,
            grid=(1,),
            in_specs=[
                pl.BlockSpec((peers, 1, lines, rows), lambda i, zh_ref: (0, 1 - zh_ref[0], 0, 0)),
                pl.BlockSpec((BLOCK, DH), lambda i, zh_ref: (0, 0)),
            ],
            out_specs=whole((lines, rows)),
        ),
        out_shape=jax.ShapeDtypeStruct((lines, rows), BF),
        compiler_params=params(),
        cost_estimate=pl.CostEstimate(
            flops=2 * peers * rows * lines, transcendentals=0, bytes_accessed=1 << 20
        ),
        name="fold",
    )(zh, got, after)


def merge_kernel(zh_ref, got_ref, far_ref, near_ref, stat_ref, _, out_ref):
    peers, _, wide, rows = got_ref.shape
    wide = wide - STAT_ROWS
    heads = wide // DH
    for h in range(heads):
        lines = slice(h * DH, (h + 1) * DH)
        pairs = [stats_of(got_ref[s, 0], wide, h) for s in range(peers)]
        pairs.append(stats_of(far_ref[...], wide, h))
        pairs.append((stat_ref[h : h + 1, :], stat_ref[heads + h : heads + h + 1, :]))
        top = functools.reduce(jnp.maximum, [t for t, _ in pairs])
        factors = [weight_of(t, top) for t, _ in pairs]
        total = sum(f * l for f, (_, l) in zip(factors, pairs))
        factors = [f / total for f in factors]
        context = factors[-1] * near_ref[lines, :]
        context += factors[-2] * far_ref[lines, :].astype(F32)
        for s in range(peers):
            context += factors[s] * got_ref[s, 0, lines, :].astype(F32)
        context = context.T.astype(BF)
        for copy in range(out_ref.shape[0]):
            out_ref[copy, :, lines] = context


def merge(zh, got, far, near, stat, after, copies, flops):
    peers, _, lines, rows = got.shape
    wide = lines - STAT_ROWS
    out = (copies, rows, wide)
    return pl.pallas_call(
        merge_kernel,
        grid_spec=pltpu.PrefetchScalarGridSpec(
            num_scalar_prefetch=1,
            grid=(1,),
            in_specs=[
                pl.BlockSpec((peers, 1, lines, rows), lambda i, zh_ref: (0, zh_ref[0], 0, 0)),
                whole(far.shape),
                whole(near.shape),
                whole(stat.shape),
                pl.BlockSpec((BLOCK, DH), lambda i, zh_ref: (0, 0)),
            ],
            out_specs=whole(out),
        ),
        out_shape=jax.ShapeDtypeStruct(out, BF),
        compiler_params=params(),
        cost_estimate=pl.CostEstimate(
            flops=flops, transcendentals=0, bytes_accessed=1 << 20
        ),
        name="merge",
    )(zh, got, far, near, stat, after)


def spread_kernel(x_ref, _, out_ref):
    for copy in range(out_ref.shape[0]):
        out_ref[copy] = x_ref[0]


def spread_out(x, after, copies):
    out = (copies,) + x.shape[1:]
    return pl.pallas_call(
        spread_kernel,
        grid=(1,),
        in_specs=[whole(x.shape), pl.BlockSpec((BLOCK, DH), lambda i: (0, 0))],
        out_specs=whole(out),
        out_shape=jax.ShapeDtypeStruct(out, BF),
        compiler_params=params(),
        cost_estimate=pl.CostEstimate(
            flops=MERGE_HINT, transcendentals=0, bytes_accessed=1 << 20
        ),
        name="spread",
    )(x, after)


def keep_kernel(where_ref, drop_ref, out_ref):
    rows, cols = out_ref.shape
    seed = where_ref[1] * 1000003 + where_ref[2] * cols
    inner = lax.broadcasted_iota(jnp.int32, (BLOCK, cols), 0) * D
    inner = inner + lax.broadcasted_iota(jnp.int32, (BLOCK, cols), 1) + seed
    for b in range(rows // BLOCK):
        hashed = inner + drop_ref[b]
        for _ in range(2):
            hashed = hashed ^ lax.shift_right_logical(hashed, jnp.int32(16))
            hashed = hashed * 73244475
        hashed = hashed ^ lax.shift_right_logical(hashed, jnp.int32(16))
        kept = (hashed & 1023) >= 102
        out_ref[b * BLOCK : (b + 1) * BLOCK, :] = jnp.where(
            kept, jnp.float32(1024.0 / 922.0), jnp.float32(0.0)
        )


def keep(where, drops, shape):
    return pl.pallas_call(
        keep_kernel,
        grid_spec=pltpu.PrefetchScalarGridSpec(
            num_scalar_prefetch=2, grid=(1,), in_specs=[], out_specs=whole(shape)
        ),
        out_shape=jax.ShapeDtypeStruct(shape, F32),
        compiler_params=params(),
        cost_estimate=pl.CostEstimate(
            flops=20 * shape[0] * shape[1], transcendentals=0, bytes_accessed=1 << 19
        ),
        name="keep",
    )(where, drops)


def project_kernel(where_ref, *refs):
    contexts, rest = refs[: 2 * PARTS], refs[2 * PARTS :]
    w_ref, keep_ref, res_ref, sum_ref, stat_ref, held_ref, sems = rest
    half, _, wide = contexts[0].shape
    copies = []
    for z in range(half):
        for shift in range(2):
            at = 2 * z + shift
            copies.append(
                pltpu.make_async_copy(
                    w_ref.at[2 * z + lax.rem(where_ref[0] + shift, 2)],
                    held_ref.at[at],
                    sems.at[at],
                )
            )
            copies[-1].start()
    acc = None
    for at, copy in enumerate(copies):
        copy.wait()
        for part in range(PARTS):
            z = at // 2
            slot = lax.rem(where_ref[2] // 2 + half - z, half) if part == 0 else z
            term = dot_t(
                contexts[2 * part + at % 2][slot],
                held_ref[at, :, part * wide : (part + 1) * wide],
            )
            acc = term if acc is None else acc + term
    rows, cols = acc.shape
    total = res_ref[...].astype(F32) + keep_ref[...] * acc
    sum_ref[...] = total
    mean = jnp.sum(total, axis=1, keepdims=True) * jnp.float32(1.0 / cols)
    dev = total - mean
    spread = jnp.sum(dev * dev, axis=1, keepdims=True)
    lane = lax.broadcasted_iota(jnp.int32, (rows, DH), 1)
    lines = jnp.where(lane == 0, mean, spread).T[:2, :]
    for copy in range(stat_ref.shape[0]):
        stat_ref[copy] = lines


def project(where, contexts, weight, kept, residual):
    rows, cols = residual.shape
    groups = weight.shape[0]
    args = list(contexts) + [weight, kept, residual]
    specs = [whole(x.shape) for x in args]
    specs[len(contexts)] = pl.BlockSpec(memory_space=pltpu.HBM)
    stat = (groups, 2, rows)
    return pl.pallas_call(
        project_kernel,
        grid_spec=pltpu.PrefetchScalarGridSpec(
            num_scalar_prefetch=1,
            grid=(1,),
            in_specs=specs,
            out_specs=[whole((rows, cols)), whole(stat)],
            scratch_shapes=[
                pltpu.VMEM(weight.shape, BF),
                pltpu.SemaphoreType.DMA((groups,)),
            ],
        ),
        out_shape=[
            jax.ShapeDtypeStruct((rows, cols), F32),
            jax.ShapeDtypeStruct(stat, F32),
        ],
        compiler_params=params(PROJECT_LIMIT << 20),
        cost_estimate=pl.CostEstimate(
            flops=2 * rows * D * cols, transcendentals=0, bytes_accessed=6 << 20
        ),
        name="project",
    )(where, *args)


def on_device(
    queries,
    key_rows,
    value_rows,
    residual,
    out_weight,
    norm_gain,
    norm_bias,
    global_list,
    random_device,
    random_offset,
    drop_seed,
    drop_offsets,
):
    row_count, width_here = queries.shape
    block_count = row_count // BLOCK
    n_y, n_x, n_zh = (lax.axis_size(a) for a in SEQ)
    plane = n_x * n_zh
    seq_count = n_y * plane
    n_zl = lax.axis_size("zl")
    tp_count = n_zl * lax.axis_size("core")
    tp_at = lax.axis_index(TP)
    cols_here = out_weight.shape[1]

    plane_at = lax.axis_index(PLANE)
    y_at = lax.axis_index("y")
    zh_at = lax.axis_index("zh")
    wide = width_here // PARTS

    pool = lax.all_gather(jnp.stack([key_rows, value_rows]), "y", axis=0, tiled=True)
    pool = pool.reshape(n_y * 2 * row_count, width_here)

    def moves(flip):
        return [
            ((y * plane + p) * tp_count + t, (t * plane + (p ^ flip)) * tp_count + y)
            for y in range(n_y)
            for p in range(plane)
            for t in range(tp_count)
        ]

    same_zh = lax.ppermute(out_weight.T, SEQ + TP, moves(0))
    other_zh = lax.ppermute(out_weight.T, SEQ + TP, moves(1))
    shards = jnp.concatenate(
        [
            jnp.where(zh_at == 0, same_zh, other_zh),
            jnp.where(zh_at == 0, other_zh, same_zh),
        ],
        axis=0,
    )

    request_count = block_count * RAND
    target = random_device.reshape(request_count)
    wanted = random_offset.reshape(request_count)
    rank = jnp.arange(request_count, dtype=jnp.int32)
    same = target[:, None] == target[None, :]
    earlier = rank[None, :] < rank[:, None]
    slot = jnp.sum(jnp.logical_and(same, earlier), axis=1).astype(jnp.int32)
    slots = n_y * CAP
    place = (target // plane) * CAP + slot
    column = target % plane
    entry = column * (2 * slots) + place
    cells = jnp.arange(plane * 2 * slots, dtype=jnp.int32)
    is_offset = entry[:, None] == cells[None, :]
    is_asker = entry[:, None] + slots == cells[None, :]
    asker = rank // RAND + 1
    table = jnp.sum(
        jnp.where(is_offset, wanted[:, None], jnp.where(is_asker, asker[:, None], 0)), axis=0
    )
    table = jnp.pad(table.astype(BF)[None], ((0, 7), (0, width_here - cells.shape[0])))

    flip = [(0, 1), (1, 0)]

    def over_x(x):
        x = jnp.broadcast_to(x[None], (n_x,) + x.shape)
        return lax.all_to_all(x, "x", split_axis=0, concat_axis=0, tiled=True)

    near_q = jnp.concatenate([queries, table], axis=0)
    far_q = jnp.concatenate(
        [lax.ppermute(queries, "zh", flip), lax.ppermute(table, "zh", flip)], axis=0
    )
    asked = over_x(jnp.stack([near_q, far_q]))
    after = asked[0, 0, row_count, 0] * 0
    shards = over_x(shards + after)
    shards = shards.reshape(plane * cols_here, width_here)
    weight = lax.all_gather(shards, "y", axis=0, tiled=True)

    lists = asked[:, :, row_count, : cells.shape[0]].reshape(plane, plane, 2 * slots)
    lists = lax.dynamic_index_in_dim(lists, plane_at, 1, keepdims=False).astype(jnp.int32)
    base = (jnp.arange(slots, dtype=jnp.int32) // CAP) * (2 * block_count)
    order = jnp.arange(plane, dtype=jnp.int32)
    peer = jnp.bitwise_xor(order, zh_at)
    nothing = jnp.int32(block_count)
    owner = global_list // block_count
    glob_row = (owner // plane) * (2 * block_count) + global_list % block_count
    glob_mark = jnp.where(owner % plane == plane_at, -1, nothing)
    here = y_at * plane + peer
    low = (here + seq_count - 1) % seq_count
    high = (here + 1) % seq_count
    low_row = (low // plane) * (2 * block_count) + block_count - 1
    high_row = (high // plane) * (2 * block_count)
    low_mark = jnp.where(low % plane == plane_at, 0, nothing)
    high_mark = jnp.where(high % plane == plane_at, block_count - 1, nothing)
    marks = lists[:, slots:] - 1
    row = jnp.concatenate(
        [
            lists[:, :slots] + base[None],
            jnp.broadcast_to(glob_row[None], (plane, GLOB)),
            low_row[:, None],
            high_row[:, None],
        ],
        axis=1,
    ).reshape(-1)
    mark = jnp.concatenate(
        [
            jnp.where(marks < 0, nothing, marks),
            jnp.broadcast_to(glob_mark[None], (plane, GLOB)),
            low_mark[:, None],
            high_mark[:, None],
        ],
        axis=1,
    ).reshape(-1)
    zh = zh_at[None].astype(jnp.int32)

    near = [local(part, queries, key_rows, value_rows) for part in range(PARTS)]
    where = jnp.stack([tp_at % 2, drop_seed[0], tp_at]).astype(jnp.int32)
    kept = keep(where, drop_offsets, residual.shape)
    contexts, after = [], kept
    for part in (1, 0):
        partials = serve(part, row, mark, zh, asked, pool, row_count)
        partials = partials.reshape((n_x, 2) + partials.shape[1:])
        got = lax.all_to_all(partials, "x", split_axis=0, concat_axis=0, tiled=True)
        gone = fold(zh, got, after)
        far = lax.ppermute(gone, "zh", flip)
        cost = 2 * row_count * width_here if part else MERGE_HINT
        context = merge(zh, got, far, *near[part], kept if part else weight, 1, cost)
        contexts.append(context)
        after = context[0]
    first, second = contexts
    shifted = [
        lax.ppermute(second, "zl", [(z, (z + by) % n_zl) for z in range(n_zl)])
        for by in range(1, n_zl)
    ]
    late = jnp.concatenate([second] + shifted, axis=0)
    early = spread_out(first, gone, n_zl)
    early = lax.all_to_all(early, "zl", split_axis=0, concat_axis=0, tiled=True)
    contexts = [x for half in (late, early) for x in (half, lax.ppermute(half, "core", flip))]
    summed, stats = project(where, contexts, weight.reshape(tp_count, -1, width_here), kept, residual)
    stats = lax.all_to_all(stats, TP, split_axis=0, concat_axis=0, tiled=True)
    means, spreads = stats[:, 0], stats[:, 1]
    mean = jnp.sum(means, axis=0) / tp_count
    away = means - mean[None]
    cols = summed.shape[1]
    spread = jnp.sum(spreads, axis=0) + cols * jnp.sum(away * away, axis=0)
    factor = lax.rsqrt(spread / D + 1e-05)
    encoded = (summed - mean[:, None]) * factor[:, None] * norm_gain[None] + norm_bias[None]
    return encoded.astype(BF)


def solution(mesh):
    fine = Mesh(mesh.devices.reshape(8, 4, 2, 4, 2), SEQ + TP)
    placed = (
        P(SEQ, TP),
        P(SEQ, TP),
        P(SEQ, TP),
        P(SEQ, TP),
        P(TP, SEQ),
        P(TP),
        P(TP),
        P(),
        P(SEQ, None),
        P(SEQ, None),
        P(),
        P(SEQ),
    )
    return jax.shard_map(
        on_device, mesh=fine, in_specs=placed, out_specs=P(SEQ, TP), check_vma=False
    )
```
